32 devices in a mesh: dp: 4 (over y, x), seq: 2 (over core), tensor: 4 (over z).
Axes of the slice: x: 2, y: 2, z: 4, core: 2. Of those that a mesh axis runs over, the one named last changes fastest.
Arguments:
- block_input: bfloat16 [8, 256, 1024], P('dp', 'seq'), may hold values from -6 to 6
- cotangent: bfloat16 [8, 256, 1024], P('dp', 'seq'), may hold values from -6 to 6
- segments: int32 [8, 256], P('dp', 'seq'), may hold values from 0 to 3, as said below
- positions: int32 [8, 256], P('dp', 'seq'), may hold values from 0 to 255, as said below
- w_qkv: bfloat16 [3, 1024, 1024], P(None, ('dp', 'seq'), 'tensor')
- qkv_bias: float32 [3, 1024], P(None, 'tensor'), may hold values from -3 to 3
- w_out: bfloat16 [1024, 1024], P('tensor', ('dp', 'seq')), may hold values from -1.5 to 1.5
- w_fc1: bfloat16 [1024, 4096], P(('dp', 'seq'), 'tensor'), may hold values from -0.1875 to 0.1875
- fc1_bias: float32 [4096], P('tensor'), may hold values from -3 to 3
- w_fc2: bfloat16 [4096, 1024], P('tensor', ('dp', 'seq')), may hold values from -0.09375 to 0.09375
- ln_gains: float32 [2, 1024], replicated, may hold values from 0.5 to 1.5
- row_biases: float32 [4, 1024], replicated, may hold values from -3 to 3
Outputs:
- output: bfloat16 [8, 256, 1024], P('dp', 'seq')
- grad_input: float32 [8, 256, 1024], P('dp', 'seq')
- grad_w_qkv: float32 [3, 1024, 1024], P(None, ('dp', 'seq'), 'tensor')
- grad_w_out: float32 [1024, 1024], P('tensor', ('dp', 'seq'))
- grad_w_fc1: float32 [1024, 4096], P(('dp', 'seq'), 'tensor')
- grad_w_fc2: float32 [4096, 1024], P('tensor', ('dp', 'seq'))
- grad_qkv_bias: float32 [3, 1024], P(None, 'tensor')
- grad_fc1_bias: float32 [4096], P('tensor')
- grad_ln_gains: float32 [2, 1024], replicated
- grad_row_biases: float32 [4, 1024], replicated
The draws below stay inside these ranges and needn't reach their ends.
Inputs may be any that keep to these rules, and one draw needn't show every extreme that they name: `segments`: segment numbers start at 0 and never fall along a sequence; a rise marks the start of a document; the first sequence is one document and the second reaches document number 3. `positions`: each token's position counts the tokens before it in its own document.
All inputs are finite; a program needn't handle non-finite values.
Results may differ from the reference program's by a relative error of at most 0.02.
Values may be sent and summed in bfloat16 or wider, within the bound.
A program may use at most 128 MiB of HBM per device.

```python
import jax
import jax.numpy as jnp
from jax import lax

D = 1024
H = 16
HD = 64
ROT = 16
FF = 4096
SEQS = 8
LENGTH = 256


def layout_draw(key):
    base = jax.random.fold_in(key, 7301)
    cut_key, pick_key = jax.random.split(base)
    cuts = jax.random.randint(cut_key, (SEQS, 3), 1, LENGTH)
    active = jax.random.randint(pick_key, (SEQS, 3), 0, 2)
    row_ids = jnp.arange(SEQS)[:, None]
    active = jnp.where(row_ids == 0, 0, jnp.where(row_ids == 1, 1, active))
    token_ids = jnp.arange(LENGTH)
    passed = active[:, None, :] * (token_ids[None, :, None] >= cuts[:, None, :]).astype(jnp.int32)
    seg_ids = jnp.sum(passed, axis=-1)
    starts = jnp.max(passed * cuts[:, None, :], axis=-1)
    return (seg_ids.astype(jnp.int32), (token_ids[None, :] - starts).astype(jnp.int32))


def draw_segments(key, part):
    return layout_draw(key)[0]


def draw_positions(key, part):
    return layout_draw(key)[1]


def draw_w_qkv(key, part):
    normal_key = jax.random.fold_in(jax.random.fold_in(key, 4409), 0)
    base = jax.random.normal(normal_key, (3, D, D), jnp.float32) * D ** (-0.5)
    return base.astype(jnp.bfloat16)


def shard_levels(stream_key, shape, cuts, least, top_value):
    def one(dim, parts):
        steps = jax.random.uniform(jax.random.fold_in(jax.random.fold_in(stream_key, 6), dim), (parts,), jnp.float32, least / len(cuts), top_value / len(cuts))
        return jnp.repeat(jnp.exp(steps), shape[dim] // parts).reshape((-1,) + (1,) * (len(shape) - dim - 1))

    factor_of = one(*cuts[0])
    for cut in cuts[1:]:
        factor_of = factor_of * one(*cut)
    return factor_of


def gaussian(stream_key, dims, scale, limit, cuts=(), held_as=jnp.bfloat16):
    entries = jax.random.normal(stream_key, dims, jnp.float32) * scale
    if len(cuts) > 0:
        entries = shard_levels(stream_key, dims, cuts, -0.22, 0.18) * entries
    return jnp.clip(entries, min=-limit, max=limit).astype(held_as)


def setup_inputs(seed: int = 0) -> dict:
    keys = jax.random.split(jax.random.key(seed), 13)
    block_input = gaussian(keys[0], (SEQS, LENGTH, D), 1.0, 6.0, ((0, 4), (1, 2)))
    cotangent = gaussian(keys[1], (SEQS, LENGTH, D), 1.0, 6.0, ((0, 4), (1, 2)))
    segments = draw_segments(jax.random.fold_in(keys[12], 71), 0)
    positions = draw_positions(jax.random.fold_in(keys[12], 71), 0)
    w_qkv = draw_w_qkv(jax.random.fold_in(keys[12], 71), 0)
    qkv_bias = gaussian(keys[5], (3, D), 0.5, 3.0, ((1, 4),), jnp.float32)
    w_out = gaussian(keys[6], (D, D), (D // 64) ** -0.5, 1.5, ((0, 4), (1, 8)))
    w_fc1 = gaussian(keys[7], (D, FF), D ** -0.5, 0.1875, ((0, 8), (1, 4)))
    fc1_bias = gaussian(keys[8], (FF,), 0.5, 3.0, ((0, 4),), jnp.float32)
    w_fc2 = gaussian(keys[9], (FF, D), FF ** -0.5, 0.09375, ((0, 4), (1, 8)))
    ln_gains = jnp.clip(1.0 + 0.1 * jax.random.normal(keys[10], (2, D), jnp.float32), 0.5, 1.5)
    row_biases = gaussian(keys[11], (4, D), 0.5, 3.0, (), jnp.float32)
    return dict(block_input=block_input, cotangent=cotangent, segments=segments, positions=positions, w_qkv=w_qkv, qkv_bias=qkv_bias, w_out=w_out, w_fc1=w_fc1, fc1_bias=fc1_bias, w_fc2=w_fc2, ln_gains=ln_gains, row_biases=row_biases)


norm_eps = 1e-05
neg_big = -1e+30
inv_root_two = 0.7071067811865476
inv_root_tau = 0.3989422804014327

def rounded(values):
    return lax.optimization_barrier(values.astype(jnp.bfloat16))

def layer_norm(values, gain, shift):
    centred = values - lax.optimization_barrier(jnp.mean(values, axis=-1, keepdims=True))
    inv_std = lax.rsqrt(lax.optimization_barrier(jnp.mean(centred * centred, axis=-1, keepdims=True)) + norm_eps)
    normed = centred * inv_std
    return (normed * gain + shift, normed, inv_std)

def norm_back(grad_out, normed, inv_std, gain):
    scaled = grad_out * gain
    centre = lax.optimization_barrier(jnp.mean(scaled, axis=-1, keepdims=True))
    slope = lax.optimization_barrier(jnp.mean(scaled * normed, axis=-1, keepdims=True))
    return inv_std * (scaled - centre - normed * slope)

def gelu_pair(pre_act):
    cumul = 0.5 * (1.0 + lax.erf(pre_act * inv_root_two))
    return (pre_act * cumul, cumul + pre_act * inv_root_tau * jnp.exp(-0.5 * pre_act * pre_act))

def rotary_tables(positions):
    half_rot = ROT // 2
    freqs = 10000.0 ** (-2.0 * jnp.arange(half_rot).astype(jnp.float32) / ROT)
    angles = positions.astype(jnp.float32)[..., None] * freqs
    cosine = jnp.cos(angles)
    sine = jnp.sin(angles)
    return (jnp.concatenate([cosine, cosine], -1)[..., None, :], jnp.concatenate([sine, sine], -1)[..., None, :])

def rotate(tensor, cosine, sine):
    half_rot = ROT // 2
    head = tensor[..., :ROT]
    turned = jnp.concatenate([-head[..., half_rot:], head[..., :half_rot]], -1)
    return jnp.concatenate([head * cosine + turned * sine, tensor[..., ROT:]], -1)

def unrotate(grads, cosine, sine):
    half_rot = ROT // 2
    head = grads[..., :ROT]
    times_sine = head * sine
    back = jnp.concatenate([times_sine[..., half_rot:], -times_sine[..., :half_rot]], -1)
    return jnp.concatenate([head * cosine + back, grads[..., ROT:]], -1)

def reference(block_input, cotangent, segments, positions, w_qkv, qkv_bias, w_out, w_fc1, fc1_bias, w_fc2, ln_gains, row_biases):
    qkv_float = w_qkv.astype(jnp.float32)
    scale = HD ** (-0.5)
    token_ids = jnp.arange(LENGTH)
    causal = token_ids[None, :] <= token_ids[:, None]

    def one_sequence(totals, inputs):
        tokens, grad_y, seg_ids, seq_pos = inputs
        tokens_f = tokens.astype(jnp.float32)
        first_out, first_normed, first_inv = layer_norm(tokens_f, ln_gains[0], row_biases[0])
        second_out, second_normed, second_inv = layer_norm(tokens_f, ln_gains[1], row_biases[1])
        first_norm_input = rounded(first_out)
        second_norm_input = rounded(second_out)
        projected = jnp.einsum('ld,jdc->jlc', first_norm_input.astype(jnp.float32), qkv_float) + qkv_bias[:, None, :]
        cosine, sine = rotary_tables(seq_pos)
        queries = rounded(rotate(projected[0].reshape(LENGTH, H, HD), cosine, sine))
        keys_rot = rounded(rotate(projected[1].reshape(LENGTH, H, HD), cosine, sine))
        values_in = rounded(projected[2].reshape(LENGTH, H, HD))
        queries_f = queries.astype(jnp.float32)
        keys_f = keys_rot.astype(jnp.float32)
        values_f = values_in.astype(jnp.float32)
        scores = jnp.einsum('qhd,khd->hqk', queries_f, keys_f) * scale
        allowed = ((seg_ids[:, None] == seg_ids[None, :]) & causal)[None]
        row_max = lax.optimization_barrier(jnp.max(jnp.where(allowed, scores, neg_big), axis=-1, keepdims=True))
        expo = jnp.where(allowed, jnp.exp(scores - row_max), 0.0)
        row_sum = lax.optimization_barrier(jnp.sum(expo, axis=-1, keepdims=True))
        log_sum = row_max + jnp.log(row_sum)
        mixed = jnp.einsum('hqk,khd->hqd', rounded(expo).astype(jnp.float32), values_f) / row_sum
        attention_context = rounded(mixed.transpose(1, 0, 2).reshape(LENGTH, D))
        attn_out = jnp.dot(attention_context, w_out, preferred_element_type=jnp.float32)
        pre_act = jnp.dot(second_norm_input, w_fc1, preferred_element_type=jnp.float32) + fc1_bias
        activ, gelu_slope = gelu_pair(pre_act)
        hidden_activation = rounded(activ)
        mlp_out = jnp.dot(hidden_activation, w_fc2, preferred_element_type=jnp.float32)
        output = (tokens_f + attn_out + row_biases[2] + mlp_out + row_biases[3]).astype(jnp.bfloat16)
        grad_f = grad_y.astype(jnp.float32)
        gradient_output_weight = jnp.dot(attention_context.T, grad_y, preferred_element_type=jnp.float32)
        grad_context = rounded(jnp.dot(grad_y, w_out.T, preferred_element_type=jnp.float32))
        gradient_down_weight = jnp.dot(hidden_activation.T, grad_y, preferred_element_type=jnp.float32)
        grad_pre = jnp.dot(grad_y, w_fc2.T, preferred_element_type=jnp.float32) * gelu_slope
        gradient_hidden_input = rounded(grad_pre)
        grad_fc1_w = jnp.dot(second_norm_input.T, gradient_hidden_input, preferred_element_type=jnp.float32)
        grad_second = jnp.dot(gradient_hidden_input, w_fc1.T, preferred_element_type=jnp.float32)
        grad_ctx3 = grad_context.reshape(LENGTH, H, HD).astype(jnp.float32)
        delta = lax.optimization_barrier(jnp.sum(grad_ctx3 * attention_context.reshape(LENGTH, H, HD).astype(jnp.float32), axis=-1)).T
        probs = jnp.where(allowed, jnp.exp(scores - log_sum), 0.0)
        grad_values = jnp.einsum('hqk,qhd->khd', rounded(probs).astype(jnp.float32), grad_ctx3)
        grad_probs = jnp.einsum('qhd,khd->hqk', grad_ctx3, values_f)
        grad_scores = rounded(probs * (grad_probs - delta[:, :, None])).astype(jnp.float32)
        grad_queries = jnp.einsum('hqk,khd->qhd', grad_scores, keys_f) * scale
        grad_keys = jnp.einsum('hqk,qhd->khd', grad_scores, queries_f) * scale
        grad_proj = jnp.stack([unrotate(grad_queries, cosine, sine).reshape(LENGTH, D), unrotate(grad_keys, cosine, sine).reshape(LENGTH, D), grad_values.reshape(LENGTH, D)])
        gradient_projection_input = rounded(grad_proj).astype(jnp.float32)
        grad_qkv_w = jnp.einsum('ld,jlc->jdc', first_norm_input.astype(jnp.float32), gradient_projection_input)
        grad_first = jnp.einsum('jlc,jdc->ld', gradient_projection_input, qkv_float)
        grad_tokens = grad_f + norm_back(grad_first, first_normed, first_inv, ln_gains[0]) + norm_back(grad_second, second_normed, second_inv, ln_gains[1])
        grad_gain_pair = jnp.stack([lax.optimization_barrier(jnp.sum(grad_first * first_normed, axis=0)), lax.optimization_barrier(jnp.sum(grad_second * second_normed, axis=0))])
        grad_rows = jnp.stack([lax.optimization_barrier(jnp.sum(grad_first, axis=0)), lax.optimization_barrier(jnp.sum(grad_second, axis=0)), lax.optimization_barrier(jnp.sum(grad_f, axis=0)), lax.optimization_barrier(jnp.sum(grad_f, axis=0))])
        updated = (totals[0] + grad_qkv_w, totals[1] + gradient_output_weight, totals[2] + grad_fc1_w, totals[3] + gradient_down_weight, totals[4] + lax.optimization_barrier(jnp.sum(grad_proj, axis=1)), totals[5] + lax.optimization_barrier(jnp.sum(grad_pre, axis=0)), totals[6] + grad_gain_pair, totals[7] + grad_rows)
        return (updated, (output, grad_tokens))
    start_totals = (jnp.zeros((3, D, D), jnp.float32), jnp.zeros((D, D), jnp.float32), jnp.zeros((D, FF), jnp.float32), jnp.zeros((FF, D), jnp.float32), jnp.zeros((3, D), jnp.float32), jnp.zeros((FF,), jnp.float32), jnp.zeros((2, D), jnp.float32), jnp.zeros((4, D), jnp.float32))
    totals, results = lax.scan(one_sequence, start_totals, (block_input, cotangent, segments, positions))
    return (results[0], results[1], totals[0], totals[1], totals[2], totals[3], totals[4], totals[5], totals[6], totals[7])
```

```python
import functools
import math

import jax
import jax.numpy as jnp
from jax import lax
from jax.experimental import pallas as pl
from jax.experimental.pallas import tpu as pltpu
from jax.sharding import PartitionSpec as P

HD = 64
ROT = 16


norm_eps = 1e-05
neg_big = -1e30
inv_root_two = 0.7071067811865476
inv_root_tau = 0.3989422804014327


def layer_norm(values, gain, shift):
    centred = values - jnp.mean(values, axis=-1, keepdims=True)
    inv_std = lax.rsqrt(jnp.mean(centred * centred, axis=-1, keepdims=True) + norm_eps)
    normed = centred * inv_std
    return (normed * gain + shift, normed, inv_std)


def norm_back(grad_out, normed, inv_std, gain):
    scaled = grad_out * gain
    centre = jnp.mean(scaled, axis=-1, keepdims=True)
    slope = jnp.mean(scaled * normed, axis=-1, keepdims=True)
    return inv_std * (scaled - centre - normed * slope)


def gelu_pair(pre_act):
    cumul = 0.5 * (1.0 + lax.erf(pre_act * inv_root_two))
    return (pre_act * cumul, cumul + pre_act * inv_root_tau * jnp.exp(-0.5 * pre_act * pre_act))


def rotary_tables(positions):
    half_rot = ROT // 2
    freqs = 10000.0 ** (-2.0 * jnp.arange(half_rot).astype(jnp.float32) / ROT)
    angles = positions.astype(jnp.float32)[..., None] * freqs
    cosine = jnp.cos(angles)
    sine = jnp.sin(angles)
    return (
        jnp.concatenate([cosine, cosine], -1)[..., None, :],
        jnp.concatenate([sine, sine], -1)[..., None, :],
    )


def rotate(tensor, cosine, sine):
    half_rot = ROT // 2
    head = tensor[..., :ROT]
    turned = jnp.concatenate([-head[..., half_rot:], head[..., :half_rot]], -1)
    return jnp.concatenate([head * cosine + turned * sine, tensor[..., ROT:]], -1)


def unrotate(grads, cosine, sine):
    half_rot = ROT // 2
    head = grads[..., :ROT]
    times_sine = head * sine
    back = jnp.concatenate([times_sine[..., half_rot:], -times_sine[..., :half_rot]], -1)
    return jnp.concatenate([head * cosine + back, grads[..., ROT:]], -1)


def gather_keys(keys_flat, values_in, segments):
    return (
        lax.all_gather(keys_flat, "seq", axis=1, tiled=True),
        lax.all_gather(values_in, "seq", axis=1, tiled=True),
        lax.all_gather(segments, "seq", axis=1, tiled=True),
    )


def pair_terms(
    query_blk,
    query_pos,
    query_seg,
    key_blk,
    value_blk,
    key_pos,
    key_seg,
    grad_blk,
    log_blk,
    delta_blk,
    scale,
):
    scores = (
        jnp.einsum("sqhd,skhd->shqk", query_blk, key_blk, preferred_element_type=jnp.float32)
        * scale
    )
    same_doc = query_seg[:, None, :, None] == key_seg[:, None, None, :]
    earlier = key_pos[None, None, None, :] <= query_pos[None, None, :, None]
    probs = jnp.where(same_doc & earlier, jnp.exp(scores - log_blk[..., None]), 0.0)
    grad_p = jnp.einsum("sqhd,skhd->shqk", grad_blk, value_blk, preferred_element_type=jnp.float32)
    grad_s = (probs * (grad_p - delta_blk[..., None])).astype(jnp.bfloat16)
    return (probs, grad_s)


def shards(
    block_input,
    cotangent,
    segments,
    positions,
    w_qkv,
    qkv_bias,
    w_out,
    w_fc1,
    fc1_bias,
    w_fc2,
    ln_gains,
    row_biases,
):
    seqs_here, rows_here, width = block_input.shape
    heads_here = w_qkv.shape[2] // HD
    flat_width = heads_here * HD
    scale = HD ** (-0.5)
    shape_heads = (seqs_here, rows_here, heads_here, HD)
    forward_weights = (
        lax.all_gather(w_qkv, ("dp", "seq"), axis=1, tiled=True),
        lax.all_gather(w_out, ("dp", "seq"), axis=1, tiled=True),
        lax.all_gather(w_fc1, ("dp", "seq"), axis=0, tiled=True),
        lax.all_gather(w_fc2, ("dp", "seq"), axis=1, tiled=True),
    )
    query_key_value_gathered, output_weight_gathered, up_weight_gathered, down_weight_gathered = (
        forward_weights
    )
    inputs_f = block_input.astype(jnp.float32)
    first_out, first_normed, first_inv = layer_norm(inputs_f, ln_gains[0], row_biases[0])
    second_out, second_normed, second_inv = layer_norm(inputs_f, ln_gains[1], row_biases[1])
    first_norm_input = first_out.astype(jnp.bfloat16)
    second_norm_input = second_out.astype(jnp.bfloat16)
    projected = (
        jnp.einsum(
            "bxf,kfh->kbxh",
            first_norm_input,
            query_key_value_gathered,
            preferred_element_type=jnp.float32,
        )
        + qkv_bias[:, None, None, :]
    )
    cosine, sine = rotary_tables(positions)
    queries = rotate(projected[0].reshape(shape_heads), cosine, sine).astype(jnp.bfloat16)
    keys_flat = (
        rotate(projected[1].reshape(shape_heads), cosine, sine)
        .astype(jnp.bfloat16)
        .reshape(seqs_here, rows_here, flat_width)
    )
    values_in = projected[2].astype(jnp.bfloat16)
    query_pos = lax.axis_index("seq") * rows_here + jnp.arange(rows_here)

    def block_scores(key_block, seg_block, key_start):
        count = key_block.shape[1]
        keys_heads = key_block.reshape(seqs_here, count, heads_here, HD)
        scores = (
            jnp.einsum("sqhd,skhd->shqk", queries, keys_heads, preferred_element_type=jnp.float32)
            * scale
        )
        key_pos = key_start + jnp.arange(count)
        same_doc = segments[:, None, :, None] == seg_block[:, None, None, :]
        earlier = key_pos[None, None, None, :] <= query_pos[None, None, :, None]
        return (scores, same_doc & earlier)

    start_state = (
        jnp.full((seqs_here, heads_here, rows_here), neg_big, jnp.float32),
        jnp.zeros((seqs_here, heads_here, rows_here), jnp.float32),
        jnp.zeros((seqs_here, heads_here, rows_here, HD), jnp.float32),
    )
    key_part = lax.all_gather(keys_flat, "seq", axis=1, tiled=True)
    value_part = lax.all_gather(values_in, "seq", axis=1, tiled=True)
    seg_part = lax.all_gather(segments, "seq", axis=1, tiled=True)
    count = key_part.shape[1]
    attend_block = math.gcd(count, 512)

    def step_block(block_idx, state):
        run_max, run_sum, accum = state
        offset = block_idx * attend_block
        key_block = lax.dynamic_slice_in_dim(key_part, offset, attend_block, 1)
        value_block = lax.dynamic_slice_in_dim(value_part, offset, attend_block, 1).reshape(
            seqs_here, attend_block, heads_here, HD
        )
        seg_block = lax.dynamic_slice_in_dim(seg_part, offset, attend_block, 1)
        scores, allowed = block_scores(key_block, seg_block, offset)
        new_max = jnp.maximum(run_max, jnp.max(jnp.where(allowed, scores, neg_big), axis=-1))
        factor = jnp.exp(run_max - new_max)
        expo = jnp.where(allowed, jnp.exp(scores - new_max[..., None]), 0.0)
        new_sum = run_sum * factor + jnp.sum(expo, axis=-1)
        update = jnp.einsum(
            "shqk,skhd->shqd",
            expo.astype(jnp.bfloat16),
            value_block,
            preferred_element_type=jnp.float32,
        )
        return (new_max, new_sum, accum * factor[..., None] + update)

    run_max, run_sum, accum = lax.fori_loop(0, count // attend_block, step_block, start_state)
    log_sum = run_max + jnp.log(run_sum)
    attention_context = (
        (accum / run_sum[..., None])
        .transpose(0, 2, 1, 3)
        .reshape(seqs_here, rows_here, flat_width)
        .astype(jnp.bfloat16)
    )
    pre_act = (
        jnp.einsum(
            "vrk,kt->vrt", second_norm_input, up_weight_gathered, preferred_element_type=jnp.float32
        )
        + fc1_bias
    )
    activ, gelu_slope = gelu_pair(pre_act)
    hidden_activation = activ.astype(jnp.bfloat16)
    partial_output_sum = jnp.einsum(
        "qhw,wj->qhj", attention_context, output_weight_gathered, preferred_element_type=jnp.float32
    )
    partial_output_sum = partial_output_sum + jnp.einsum(
        "qzg,gc->qzc", hidden_activation, down_weight_gathered, preferred_element_type=jnp.float32
    )
    branches = lax.psum(partial_output_sum.astype(jnp.bfloat16), "tensor").astype(jnp.float32)
    output = (inputs_f + branches + row_biases[2] + row_biases[3]).astype(jnp.bfloat16)
    query_key_value_backward, output_weight_backward, up_weight_backward, down_weight_backward = (
        lax.all_gather(w_qkv, ("dp", "seq"), axis=1, tiled=True),
        lax.all_gather(w_out, ("dp", "seq"), axis=1, tiled=True),
        lax.all_gather(w_fc1, ("dp", "seq"), axis=0, tiled=True),
        lax.all_gather(w_fc2, ("dp", "seq"), axis=1, tiled=True),
    )
    grad_f = cotangent.astype(jnp.float32)
    gradient_output_weight = jnp.einsum(
        "bxz,bxe->ze", attention_context, cotangent, preferred_element_type=jnp.float32
    )
    grad_context = jnp.einsum(
        "zpi,xi->zpx", cotangent, output_weight_backward, preferred_element_type=jnp.float32
    ).astype(jnp.bfloat16)
    gradient_down_weight = jnp.einsum(
        "tzi,tzo->io", hidden_activation, cotangent, preferred_element_type=jnp.float32
    )
    grad_pre = (
        jnp.einsum(
            "hvg,rg->hvr", cotangent, down_weight_backward, preferred_element_type=jnp.float32
        )
        * gelu_slope
    )
    gradient_hidden_input = grad_pre.astype(jnp.bfloat16)
    grad_fc1_w = jnp.einsum(
        "mxa,mxr->ar", second_norm_input, gradient_hidden_input, preferred_element_type=jnp.float32
    )
    grad_second = jnp.einsum(
        "ikq,uq->iku", gradient_hidden_input, up_weight_backward, preferred_element_type=jnp.float32
    )
    grad_ctx_heads = grad_context.reshape(shape_heads)
    delta = jnp.sum(
        grad_ctx_heads.astype(jnp.float32)
        * attention_context.reshape(shape_heads).astype(jnp.float32),
        axis=-1,
    ).transpose(0, 2, 1)
    key_all, value_all, seg_all = gather_keys(keys_flat, values_in, segments)
    total_len = key_all.shape[1]
    block = math.gcd(total_len, 512)

    def key_slices(offset):
        key_block = lax.dynamic_slice_in_dim(key_all, offset, block, 1).reshape(
            seqs_here, block, heads_here, HD
        )
        value_block = lax.dynamic_slice_in_dim(value_all, offset, block, 1).reshape(
            seqs_here, block, heads_here, HD
        )
        seg_block = lax.dynamic_slice_in_dim(seg_all, offset, block, 1)
        return (key_block, value_block, seg_block)

    def back_block(block_idx, state):
        grad_q, grad_key_all, grad_value_all = state
        offset = block_idx * block
        key_block, value_block, seg_block = key_slices(offset)
        probs, grad_s = pair_terms(
            queries,
            query_pos,
            segments,
            key_block,
            value_block,
            offset + jnp.arange(block),
            seg_block,
            grad_ctx_heads,
            log_sum,
            delta,
            scale,
        )
        grad_v = jnp.einsum(
            "shqk,sqhd->skhd",
            probs.astype(jnp.bfloat16),
            grad_ctx_heads,
            preferred_element_type=jnp.float32,
        )
        grad_q = (
            grad_q
            + jnp.einsum("shqk,skhd->sqhd", grad_s, key_block, preferred_element_type=jnp.float32)
            * scale
        )
        grad_k = (
            jnp.einsum("shqk,sqhd->skhd", grad_s, queries, preferred_element_type=jnp.float32)
            * scale
        )
        grad_key_all = lax.dynamic_update_slice_in_dim(
            grad_key_all, grad_k.reshape(seqs_here, block, flat_width), offset, 1
        )
        grad_value_all = lax.dynamic_update_slice_in_dim(
            grad_value_all, grad_v.reshape(seqs_here, block, flat_width), offset, 1
        )
        return (grad_q, grad_key_all, grad_value_all)

    back_start = (
        jnp.zeros(shape_heads, jnp.float32),
        jnp.zeros((seqs_here, total_len, flat_width), jnp.float32),
        jnp.zeros((seqs_here, total_len, flat_width), jnp.float32),
    )
    grad_q, grad_key_all, grad_value_all = lax.fori_loop(
        0, total_len // block, back_block, back_start
    )
    grad_key_here, grad_value_here = (
        lax.psum_scatter(
            grad_key_all.astype(jnp.bfloat16), "seq", scatter_dimension=1, tiled=True
        ).astype(jnp.float32),
        lax.psum_scatter(
            grad_value_all.astype(jnp.bfloat16), "seq", scatter_dimension=1, tiled=True
        ).astype(jnp.float32),
    )
    grad_proj = jnp.stack(
        [
            unrotate(grad_q, cosine, sine).reshape(seqs_here, rows_here, flat_width),
            unrotate(grad_key_here.reshape(shape_heads), cosine, sine).reshape(
                seqs_here, rows_here, flat_width
            ),
            grad_value_here,
        ]
    )
    grad_bias_qkv = jnp.sum(grad_proj, axis=(1, 2))
    gradient_projection_input = grad_proj.astype(jnp.bfloat16)
    grad_qkv_w = jnp.einsum(
        "ink,oint->okt",
        first_norm_input,
        gradient_projection_input,
        preferred_element_type=jnp.float32,
    )
    grad_first = jnp.einsum(
        "etbp,eop->tbo",
        gradient_projection_input,
        query_key_value_backward,
        preferred_element_type=jnp.float32,
    )
    grad_first, grad_second = (
        lax.psum(grad_first.astype(jnp.bfloat16), "tensor").astype(jnp.float32),
        lax.psum(grad_second.astype(jnp.bfloat16), "tensor").astype(jnp.float32),
    )
    grad_input = (
        grad_f
        + norm_back(grad_first, first_normed, first_inv, ln_gains[0])
        + norm_back(grad_second, second_normed, second_inv, ln_gains[1])
    )
    gain_terms = jnp.stack(
        [
            jnp.sum(grad_first * first_normed, axis=(0, 1)),
            jnp.sum(grad_second * second_normed, axis=(0, 1)),
        ]
    )
    row_terms = jnp.stack(
        [
            jnp.sum(grad_first, axis=(0, 1)),
            jnp.sum(grad_second, axis=(0, 1)),
            jnp.sum(grad_f, axis=(0, 1)),
            jnp.sum(grad_f, axis=(0, 1)),
        ]
    )
    bias_sums = lax.psum(
        (grad_bias_qkv, jnp.sum(grad_pre, axis=(0, 1)), gain_terms, row_terms), ("dp", "seq")
    )
    weight_sums = (
        lax.psum_scatter(grad_qkv_w, ("dp", "seq"), scatter_dimension=1, tiled=True),
        lax.psum_scatter(gradient_output_weight, ("dp", "seq"), scatter_dimension=1, tiled=True),
        lax.psum_scatter(grad_fc1_w, ("dp", "seq"), scatter_dimension=0, tiled=True),
        lax.psum_scatter(gradient_down_weight, ("dp", "seq"), scatter_dimension=1, tiled=True),
    )
    return (
        output,
        grad_input,
        weight_sums[0],
        weight_sums[1],
        weight_sums[2],
        weight_sums[3],
        bias_sums[0],
        bias_sums[1],
        bias_sums[2],
        bias_sums[3],
    )


MESH = pl.DeviceIdType.MESH
ANY = pl.BlockSpec(memory_space=pl.ANY)
VM = pl.BlockSpec(memory_space=pltpu.VMEM)


def remote(src, dst, send, recv, where):
    return pltpu.make_async_remote_copy(
        src_ref=src, dst_ref=dst, send_sem=send, recv_sem=recv, device_id=where, device_id_type=MESH
    )


def pair_of(d):
    return d + 1 - 2 * lax.rem(d, 2)


def dot_nn(left, right):
    return lax.dot_general(left, right, (((1,), (0,)), ((), ())), preferred_element_type=jnp.float32)


def dot_nt(left, right):
    return lax.dot_general(left, right, (((1,), (1,)), ((), ())), preferred_element_type=jnp.float32)


def dot_tn(left, right):
    return lax.dot_general(left, right, (((0,), (0,)), ((), ())), preferred_element_type=jnp.float32)


def spread(left, right):
    return lax.dot_general(
        left,
        right,
        (((0,), (0,)), ((), ())),
        precision=lax.Precision.HIGHEST,
        preferred_element_type=jnp.float32,
    )


def loop(count, body):
    def step(i, carry):
        body(i)
        return carry

    lax.fori_loop(0, count, step, 0)


def at(index, size):
    return pl.ds(pl.multiple_of(index * size, size), size)


def mega_kernel(dims, *refs):
    f32, bf16 = jnp.float32, jnp.bfloat16
    seqs, rows, width, kr, oc, fh, hh = dims
    length = 2 * rows
    tokens = seqs * length
    heads = fh // HD
    scale = HD ** (-0.5)
    (x, c, seg, pos, wq, wo, w1, w2, qb, f1b, gains, rowb) = refs[:12]
    R = refs[12:16]
    yfin, gfin, bout = refs[16:19]
    (xf, cf, segb, posb, GQ, GO, G1, G2) = refs[19:27]
    (first, second, nrm, tables, qs, ks, vs, gcs, ctx, gproj) = refs[27:37]
    (gacc, hid, slope, ghid) = refs[37:41]
    gW = refs[41:45]
    mid = refs[45:49]
    (part, sibp, chip, ein, xin, fw) = refs[49:55]
    (brow, bpair, bsum, bgot2, bsum2, bgot3) = refs[55:61]
    (s1, r1, s2, r2, ss, sr, sl) = refs[61:68]
    (ts, tr, tl) = refs[68:71]
    (ms, mr, ds_, dr, hs, hr, bs, br, bl) = refs[71:80]
    (ps, pr, es, er, xs, xr, fs, fr, fs2) = refs[80:89]
    (b1s, b1r, b2s, b2r, b3s, b3r) = refs[89:95]
    nseq, nt, ndp = 2, 4, 4
    d, s, t = lax.axis_index("dp"), lax.axis_index("seq"), lax.axis_index("tensor")
    other = 1 - s
    near_x, near_y, corner = pair_of(d), lax.rem(d + 2, 4), 3 - d
    me = d * nseq + s

    barrier = pltpu.get_barrier_semaphore()
    for peer in (near_x, near_y):
        for core in (0, 1):
            pl.semaphore_signal(
                barrier, inc=1, device_id={"dp": peer, "seq": core}, device_id_type=MESH
            )
    pl.semaphore_signal(barrier, inc=1, device_id={"dp": corner}, device_id_type=MESH)
    for k in range(1, nt):
        pl.semaphore_signal(
            barrier, inc=1, device_id={"tensor": lax.rem(t + k, nt)}, device_id_type=MESH
        )
    pl.semaphore_signal(barrier, inc=1, device_id={"seq": other}, device_id_type=MESH)
    pl.semaphore_wait(barrier, 4 + 1 + nt)

    sends = []

    def go(copy):
        copy.start()
        sends.append(copy)
        return copy

    def source(a, half):
        return (
            lambda: wq.at[:, :, at(half, fh)],
            lambda: wo.at[at(half, fh), :],
            lambda: w1.at[:, at(half, hh)],
            lambda: w2.at[at(half, hh), :],
        )[a]()

    def place(bufs, a, index):
        return (
            lambda: bufs[0].at[:, at(index, kr), :],
            lambda: bufs[1].at[:, at(index, oc)],
            lambda: bufs[2].at[at(index, kr), :],
            lambda: bufs[3].at[:, at(index, oc)],
        )[a]()

    full = (GQ, GO, G1, G2)
    hop1, hop2, sibs, locals_ = {}, {}, {}, {}

    def start_hop1(a):
        for way, near in ((0, near_x), (1, near_y)):
            for k, half in ((0, s), (1, other)):
                hop1[a, way, k] = go(
                    remote(
                        source(a, half),
                        place(full, a, me),
                        s1.at[a, way, k],
                        r1.at[a, way, k],
                        {"dp": near, "seq": half},
                    )
                )

    def start_near(a):
        sibs[a] = go(
            remote(source(a, other), place(full, a, me), ss.at[a], sr.at[a], {"seq": other})
        )
        locals_[a] = pltpu.make_async_copy(source(a, s), place(full, a, me), sl.at[a])
        locals_[a].start()

    def start_hop2(a):
        for way in (0, 1):
            for k in (0, 1):
                hop1[a, way, k].wait_recv()
        view = place(full, a, near_x * nseq)
        hop2[a, 0] = go(remote(view, view, s2.at[a, 0], r2.at[a, 0], {"dp": near_y}))
        view = place(full, a, near_y * nseq + 1)
        hop2[a, 1] = go(remote(view, view, s2.at[a, 1], r2.at[a, 1], {"dp": near_x}))

    def wait_all(a):
        hop2[a, 0].wait_recv()
        hop2[a, 1].wait_recv()
        sibs[a].wait_recv()
        locals_[a].wait()

    mine = at(s, rows)
    start_hop1(0)
    start_hop1(1)
    tok = []
    for j, (src, dst) in enumerate(
        ((x, xf.at[:, mine, :]), (pos, posb.at[s]), (seg, segb.at[s]), (c, cf.at[:, mine, :]))
    ):
        copy = pltpu.make_async_copy(src, dst, tl.at[j])
        copy.start()
        tok.append((copy, go(remote(src, dst, ts.at[j], tr.at[j], {"seq": other}))))
    start_near(0)
    start_near(1)
    start_hop1(2)
    start_near(2)
    start_near(3)

    step = 32
    per = rows // step

    def norm_half(half):
        def body(i):
            b, at_row = i // per, pl.multiple_of(half * rows + lax.rem(i, per) * step, step)
            flat_row = pl.multiple_of(b * length + at_row, step)
            values = xf[b, pl.ds(at_row, step), :].astype(f32)
            one, normed, _ = layer_norm(values, gains[0:1, :], rowb[0:1, :])
            span = pl.ds(flat_row, step)
            nrm[span, :] = normed
            first[span, :] = one.astype(bf16)
            second[span, :] = (normed * gains[1:2, :] + rowb[1:2, :]).astype(bf16)

        loop(seqs * per, body)

    tok[0][0].wait()
    norm_half(s)
    tok[0][1].wait_recv()
    norm_half(other)
    for j in (1, 2, 3):
        tok[j][0].wait()
    brow[...] = jnp.zeros_like(brow)
    ones = jnp.ones((16, rows), bf16)
    csum = dot_nn(ones, cf[0, mine, :])
    for b in range(1, seqs):
        csum = csum + dot_nn(ones, cf[b, mine, :])
    brow[6:7, :] = csum[0:1, :]
    for j in (1, 2, 3):
        tok[j][1].wait_recv()

    half_rot = ROT // 2
    lane = lax.broadcasted_iota(jnp.int32, (half_rot, fh), 1)
    lane = lax.rem(lane, HD)
    which = lax.broadcasted_iota(jnp.int32, (half_rot, fh), 0)
    low = (lane == which).astype(f32)
    high = (lane == which + half_rot).astype(f32)
    rest = (lane[0:1, :] >= ROT).astype(f32)
    power = lax.broadcasted_iota(jnp.int32, (half_rot, length), 0).astype(f32)
    freqs = jnp.exp(power * (-2.0 / ROT * math.log(10000.0)))
    for b in range(seqs):
        row = jnp.concatenate([posb[0, b : b + 1, :], posb[1, b : b + 1, :]], axis=1).astype(f32)
        angles = row * freqs
        sine = jnp.sin(angles)
        tables[0, at(b, length), :] = spread(jnp.cos(angles), low + high) + rest
        tables[1, at(b, length), :] = spread(sine, high)
        tables[2, at(b, length), :] = spread(sine, -low)

    start_hop2(0)
    start_hop2(1)
    wait_all(0)
    wait_all(1)
    start_hop1(3)

    def project(b):
        span = at(b, length)
        inputs = first[span, :]
        cosine, sin_a, sin_b = tables[0, span, :], tables[1, span, :], tables[2, span, :]

        def turn(v):
            up, down = pltpu.roll(v, half_rot, 1), pltpu.roll(v, fh - half_rot, 1)
            return v * cosine + up * sin_a + down * sin_b

        bias = lambda j: qb[j : j + 1, at(s, fh)]
        qs[span, :] = turn(dot_nn(inputs, GQ[0]) + bias(0)).astype(bf16)
        ks[span, :] = turn(dot_nn(inputs, GQ[1]) + bias(1)).astype(bf16)
        vs[span, :] = (dot_nn(inputs, GQ[2]) + bias(2)).astype(bf16)
        gcs[span, :] = dot_nt(cf[b], GO[...]).astype(bf16)

    loop(seqs, project)
    start_hop2(2)

    lane_of = lax.broadcasted_iota(jnp.int32, (1, fh), 1) // HD

    def attend(b):
        span = at(b, length)
        q, k, v, gc = qs[span, :], ks[span, :], vs[span, :], gcs[span, :]
        seg_rows = [
            jnp.concatenate(
                [segb[0, n : n + 1, :], segb[1, n : n + 1, :]], axis=1
            ).astype(f32)
            for n in range(seqs)
        ]
        seg_row = seg_rows[0]
        for n in range(1, seqs):
            seg_row = jnp.where(b == n, seg_rows[n], seg_row)
        pick = (lax.broadcasted_iota(jnp.int32, (8, length), 0) == 0).astype(f32)
        seg_col = spread(jnp.broadcast_to(seg_row, (8, length)), pick)
        q_pos = lax.broadcasted_iota(jnp.int32, (length, length), 0)
        k_pos = lax.broadcasted_iota(jnp.int32, (length, length), 1)
        allowed = (seg_col == seg_row) & (k_pos <= q_pos)
        out = []
        for h in range(heads):
            keep = (lane_of == h).astype(bf16)
            scores = dot_nt(q * keep, k) * scale
            row_max = jnp.max(jnp.where(allowed, scores, neg_big), axis=-1, keepdims=True)
            expo = jnp.where(allowed, jnp.exp(scores - row_max), 0.0)
            inv = 1.0 / jnp.sum(expo, axis=-1, keepdims=True)
            mixed = (dot_nn(expo.astype(bf16), v) * inv).astype(bf16) * keep
            gch = gc * keep
            delta = jnp.sum(gch.astype(f32) * mixed.astype(f32), axis=-1, keepdims=True)
            probs = expo * inv
            grad_s = (probs * (dot_nt(gch, v) - delta)).astype(bf16)
            terms = (
                mixed,
                dot_nn(grad_s, k * keep),
                dot_tn(grad_s, q * keep),
                dot_tn(probs.astype(bf16), gch),
            )
            out = [p + q_ for p, q_ in zip(out, terms)] if out else list(terms)
        ctx[span, :] = out[0]
        cosine, sin_a, sin_b = tables[0, span, :], tables[1, span, :], tables[2, span, :]

        def back(v):
            up, down = pltpu.roll(v, half_rot, 1), pltpu.roll(v, fh - half_rot, 1)
            return v * cosine - up * sin_a - down * sin_b

        for j, grad in enumerate((back(out[1] * scale), back(out[2] * scale), out[3])):
            gproj[j, span, :] = grad.astype(bf16)
            spot = pl.ds(pl.multiple_of(j * 2 * fh + s * fh, fh), fh)
            brow[1:2, spot] = brow[1:2, spot] + jnp.sum(grad, axis=0, keepdims=True)

    loop(seqs, attend)

    pairs, mids, lasts = {}, {}, {}

    def start_reduce(a):
        gone = lambda index: place(gW, a, index)
        mids[a, 0] = go(
            remote(gone(corner * 2), mid[a].at[0], ms.at[a, 0], mr.at[a, 0], {"dp": near_x})
        )
        mids[a, 1] = go(
            remote(gone(corner * 2 + 1), mid[a].at[1], ms.at[a, 1], mr.at[a, 1], {"dp": near_y})
        )
        go(
            remote(
                gone(near_x * 2), R[a].at[s, 1], ds_.at[a, 0], dr.at[a, s], {"dp": near_x, "seq": 0}
            )
        )
        go(
            remote(
                gone(near_y * 2 + 1),
                R[a].at[s, 1],
                ds_.at[a, 1],
                dr.at[a, s],
                {"dp": near_y, "seq": 1},
            )
        )
        pairs[a] = go(
            remote(gone(d * 2 + other), R[a].at[s, 0], bs.at[a], br.at[a], {"seq": other})
        )
        lasts[a] = pltpu.make_async_copy(gone(me), R[a].at[s, 0], bl.at[a])
        lasts[a].start()

    def second_reduce(a):
        for way, near, index in ((0, near_y, near_y * 2), (1, near_x, near_x * 2 + 1)):
            mids[a, way].wait_recv()
            mid[a][way] = (
                mid[a][way].astype(f32) + place(gW, a, index)[...].astype(f32)
            ).astype(bf16)
            go(
                remote(
                    mid[a].at[way],
                    R[a].at[s, 2],
                    hs.at[a, way],
                    hr.at[a, s],
                    {"dp": near, "seq": way},
                )
            )

    def finish_reduce(a):
        for h in (0, 1):
            remote(R[a].at[h, 1], R[a].at[h, 1], ds_.at[a, 0], dr.at[a, h], {"dp": near_x}).wait_recv()
            remote(R[a].at[h, 2], R[a].at[h, 2], hs.at[a, 0], hr.at[a, h], {"dp": near_x}).wait_recv()
        pairs[a].wait_recv()
        lasts[a].wait()

    big = 256
    wide = 512

    def qkv_grad(i):
        rows_of = at(i, big)
        lhs = first[:, rows_of]
        for j in range(3):
            gW[0][j, rows_of, :] = dot_tn(lhs, gproj[j]).astype(bf16)

    loop(width // big, qkv_grad)

    def out_grad(i):
        cols = at(i, wide)
        gW[1][:, cols] = dot_tn(ctx[...], cf[:, :, cols].reshape(tokens, wide)).astype(bf16)

    loop(width // wide, out_grad)
    start_reduce(0)
    start_reduce(1)

    tiles = width // wide

    def first_back(i):
        b, n = i // tiles, lax.rem(i, tiles)
        span, cols = at(b, length), at(n, wide)
        grad = dot_nt(gproj[0, span, :], GQ[0, cols, :])
        for j in (1, 2):
            grad = grad + dot_nt(gproj[j, span, :], GQ[j, cols, :])
        gacc[span, cols] = grad * gains[0:1, cols]
        brow[2:3, cols] = brow[2:3, cols] + jnp.sum(grad * nrm[span, cols], axis=0, keepdims=True)
        brow[4:5, cols] = brow[4:5, cols] + jnp.sum(grad, axis=0, keepdims=True)

    loop(seqs * tiles, first_back)

    wait_all(2)
    start_hop2(3)

    def up(b):
        span = at(b, length)
        slope[span, :] = dot_nn(second[span, :], G1[...]) + f1b[:, at(s, hh)]

        def curve(i):
            part_of = pl.ds(pl.multiple_of(b * length + i * step, step), step)
            activ, incline = gelu_pair(slope[part_of, :])
            hid[part_of, :] = activ.astype(bf16)
            slope[part_of, :] = incline

        loop(length // step, curve)

    loop(seqs, up)

    def down_grad(i):
        m, n = i // tiles, lax.rem(i, tiles)
        units, cols = at(m, big), at(n, wide)
        gW[3][units, cols] = dot_tn(
            hid[:, units], cf[:, :, cols].reshape(tokens, wide)
        ).astype(bf16)

    loop(hh // big * tiles, down_grad)

    wait_all(3)

    def branch(i):
        b, n = i // tiles, lax.rem(i, tiles)
        span, cols = at(b, length), at(n, wide)
        total = dot_nn(ctx[span, :], GO[:, cols]) + dot_nn(hid[span, :], G2[:, cols])
        part[0, b, :, cols] = total.astype(bf16)

    loop(seqs * tiles, branch)

    theirs_half = at(other, rows)
    crosses = {}

    def start_cross(j):
        crosses[j] = go(
            remote(part.at[j, :, theirs_half, :], sibp.at[j], ps.at[j], pr.at[j], {"seq": other})
        )

    start_cross(0)
    start_reduce(3)

    def down_back(b):
        span = at(b, length)
        grad = dot_nt(cf[b], G2[...]) * slope[span, :]
        ghid[span, :] = grad.astype(bf16)
        spot = at(s, hh)
        brow[0:1, spot] = brow[0:1, spot] + jnp.sum(grad, axis=0, keepdims=True)

    loop(seqs, down_back)

    side = t // 2
    mi, th = side, 1 - side
    inner = (t == 1) | (t == 2)
    end = (t == 0) | (t == 3)
    pt, facing = {"tensor": pair_of(t)}, {"tensor": 3 - t}
    nc = 2
    cr = rows // nc
    fin = (yfin, gfin)
    chunk = lambda ch: slice(ch * cr, (ch + 1) * cr)

    def to_inner(j, i, b, ch):
        view = (j, b, pl.ds(ch * cr, cr))
        return remote(chip.at[view], ein.at[view], es.at[j, i, ch], er.at[j, i, ch], pt)

    def over(j, ch):
        view = (j, pl.ds(ch * cr, cr))
        return remote(fw.at[view], xin.at[view], xs.at[j, ch], xr.at[j, ch], facing)

    def final(j, b, ch, send, slot, where):
        view = fin[j].at[b, pl.ds(ch * cr, cr)]
        return remote(view, view, send, fr.at[j, slot, ch], where)

    def z_one(j):
        crosses[j].wait_recv()
        for i, b in ((0, th), (1, mi)):
            for ch in range(nc):
                here = pl.ds(pl.multiple_of(s * rows + ch * cr, cr), cr)
                chip[j, b, chunk(ch)] = (
                    part[j, b, here, :].astype(f32) + sibp[j, b, chunk(ch)].astype(f32)
                ).astype(bf16)

                @pl.when(end)
                def _():
                    to_inner(j, i, b, ch).start()

    def z_two(j):
        @pl.when(inner)
        def _():
            for ch in range(nc):
                to_inner(j, 0, th, ch).wait_recv()
                fw[j, chunk(ch)] = (
                    chip[j, th, chunk(ch)].astype(f32) + ein[j, th, chunk(ch)].astype(f32)
                ).astype(bf16)
                over(j, ch).start()

    def z_three(j):
        @pl.when(inner)
        def _():
            for ch in range(nc):
                to_inner(j, 1, mi, ch).wait_recv()
                over(j, ch).wait_recv()
                total = (
                    chip[j, mi, chunk(ch)].astype(f32)
                    + ein[j, mi, chunk(ch)].astype(f32)
                    + xin[j, chunk(ch)].astype(f32)
                )
                here = pl.ds(pl.multiple_of(s * rows + ch * cr, cr), cr)
                inputs = xf[mi, here, :].astype(f32)
                if j == 0:
                    result = inputs + total + rowb[2:3, :] + rowb[3:4, :]
                else:
                    _, normed, inv_std = layer_norm(inputs, 1.0, 0.0)
                    result = norm_back(total, normed, inv_std, 1.0)
                fin[j][mi, chunk(ch)] = result.astype(bf16)
                final(j, mi, ch, fs.at[j, 0, ch], 0, pt).start()
                final(j, mi, ch, fs.at[j, 1, ch], 1, facing).start()

    def z_four(j):
        @pl.when(inner)
        def _():
            for ch in range(nc):
                final(j, th, ch, fs.at[j, 1, ch], 1, facing).wait_recv()
                final(j, th, ch, fs2.at[j, ch], 1, pt).start()

    def z_five(j):
        for ch in range(nc):

            @pl.when(end)
            def _():
                for i, b in ((0, th), (1, mi)):
                    to_inner(j, i, b, ch).wait_send()
                final(j, mi, ch, fs.at[j, 0, ch], 0, pt).wait_recv()
                final(j, th, ch, fs2.at[j, ch], 1, pt).wait_recv()

            @pl.when(inner)
            def _():
                over(j, ch).wait_send()
                final(j, mi, ch, fs.at[j, 0, ch], 0, pt).wait_send()
                final(j, mi, ch, fs.at[j, 1, ch], 1, facing).wait_send()
                final(j, th, ch, fs2.at[j, ch], 1, pt).wait_send()

    z_one(0)

    def second_back(i):
        b, n = i // tiles, lax.rem(i, tiles)
        span, cols = at(b, length), at(n, wide)
        grad = dot_nt(ghid[span, :], G1[cols, :])
        part[1, b, :, cols] = (gacc[span, cols] + grad * gains[1:2, cols]).astype(bf16)
        brow[3:4, cols] = brow[3:4, cols] + jnp.sum(grad * nrm[span, cols], axis=0, keepdims=True)
        brow[5:6, cols] = brow[5:6, cols] + jnp.sum(grad, axis=0, keepdims=True)

    loop(seqs * tiles, second_back)
    start_cross(1)
    bpair_copy = go(remote(brow, bpair, b1s, b1r, {"seq": other}))

    def up_grad(i):
        rows_of = at(i, big)
        gW[2][rows_of, :] = dot_tn(second[:, rows_of], ghid[...]).astype(bf16)

    loop(width // big, up_grad)
    start_reduce(2)
    z_one(1)
    second_reduce(0)
    second_reduce(1)
    z_two(0)
    bpair_copy.wait_recv()
    bsum[...] = brow[...] + bpair[...]
    plane_sends = [
        go(remote(bsum, bgot2.at[d], b2s.at[k], b2r.at[k], {"dp": peer}))
        for k, peer in ((1, near_x), (2, near_y), (3, corner))
    ]
    z_two(1)
    z_three(0)
    second_reduce(3)
    for copy in plane_sends:
        copy.wait_recv()
    bgot2[d] = bsum[...]
    plane = bgot2[0]
    for k in range(1, ndp):
        plane = plane + bgot2[k]
    bsum2[...] = plane
    bout[0] = plane
    z_sends = [
        go(remote(bsum2, bgot3.at[t], b3s.at[k], b3r.at[k], {"tensor": lax.rem(t + k, nt)}))
        for k in range(1, nt)
    ]
    z_three(1)
    second_reduce(2)
    z_four(0)
    z_four(1)
    for copy in z_sends:
        copy.wait_recv()
    bgot3[t] = bsum2[...]
    whole = bgot3[0]
    for k in range(1, nt):
        whole = whole + bgot3[k]
    bout[1] = whole
    z_five(0)
    z_five(1)
    for a in (0, 1, 3, 2):
        finish_reduce(a)
    for copy in sends:
        copy.wait_send()


def mega(x, c, seg, pos, wq, wo, w1, w2, qb, f1b, gains, rowb):
    shape = jax.ShapeDtypeStruct
    f32, bf16 = jnp.float32, jnp.bfloat16
    seqs, rows, width = x.shape
    kr, oc, fh, hh = wq.shape[1], wo.shape[1], wq.shape[2] // 2, w1.shape[1] // 2
    length = rows * 2
    tokens = seqs * length
    nc = 2
    pieces = ((3, kr, fh), (fh, oc), (kr, hh), (hh, oc))
    fulls = ((3, width, fh), (fh, width), (width, hh), (hh, width))
    dma = pltpu.SemaphoreType.DMA
    vm = lambda dims, kind: pltpu.VMEM(dims, kind)
    bias = (8, width)
    scratch = [
        vm((seqs, length, width), bf16),
        vm((seqs, length, width), bf16),
        vm((2,) + seg.shape, jnp.int32),
        vm((2,) + pos.shape, jnp.int32),
        *[vm(f, bf16) for f in fulls],
        vm((tokens, width), bf16),
        vm((tokens, width), bf16),
        vm((tokens, width), f32),
        vm((3, tokens, fh), f32),
        *[vm((tokens, fh), bf16)] * 5,
        vm((3, tokens, fh), bf16),
        vm((tokens, width), f32),
        vm((tokens, hh), bf16),
        vm((tokens, hh), f32),
        vm((tokens, hh), bf16),
        *[vm(f, bf16) for f in fulls],
        *[vm((2,) + p, bf16) for p in pieces],
        vm((2, seqs, length, width), bf16),
        *[vm((2, seqs, rows, width), bf16)] * 3,
        *[vm((2, rows, width), bf16)] * 2,
        vm(bias, f32),
        vm(bias, f32),
        vm(bias, f32),
        vm((4,) + bias, f32),
        vm(bias, f32),
        vm((4,) + bias, f32),
        *[dma((4, 2, 2))] * 2,
        *[dma((4, 2))] * 2,
        *[dma((4,))] * 3,
        *[dma((4,))] * 3,
        *[dma((4, 2))] * 6,
        *[dma((4,))] * 3,
        *[dma((2,))] * 2,
        *[dma((2, 2, nc))] * 2,
        *[dma((2, nc))] * 2,
        *[dma((2, 2, nc))] * 2,
        dma((2, nc)),
        dma,
        dma,
        *[dma((4,))] * 4,
    ]
    return pl.pallas_call(
        functools.partial(mega_kernel, (seqs, rows, width, kr, oc, fh, hh)),
        out_shape=(
            *[shape((2, 3) + p, bf16) for p in pieces],
            shape(x.shape, bf16),
            shape(x.shape, bf16),
            shape((2,) + bias, f32),
        ),
        in_specs=[ANY] * 8 + [VM] * 4,
        out_specs=[ANY] * 4 + [VM] * 3,
        scratch_shapes=scratch,
        compiler_params=pltpu.CompilerParams(
            collective_id=0, has_side_effects=True, vmem_limit_bytes=48 * 2**20
        ),
    )(x, c, seg, pos, wq, wo, w1, w2, qb, f1b, gains, rowb)


def final_kernel(dims, *refs):
    f32 = jnp.float32
    fh, hh = dims
    rq, ro, r1, r2, yf, gf, bb, c = refs[:8]
    out, gin, oq, oo, o1, o2, oqb, of1, ogn, orow = refs[8:]

    def total(ref, *index):
        return (
            ref[(index[0], 0) + index[1:]].astype(f32)
            + ref[(index[0], 1) + index[1:]].astype(f32)
            + ref[(index[0], 2) + index[1:]].astype(f32)
        )

    for h in (0, 1):
        for j in range(3):
            oq[j, :, h * fh : (h + 1) * fh] = total(rq, h, j)
        oo[h * fh : (h + 1) * fh, :] = total(ro, h)
        o1[:, h * hh : (h + 1) * hh] = total(r1, h)
        o2[h * hh : (h + 1) * hh, :] = total(r2, h)
    out[...] = yf[...]
    gin[...] = c[...].astype(f32) + gf[...].astype(f32)
    for j in range(3):
        oqb[j : j + 1, :] = bb[0, 1:2, j * 2 * fh : (j + 1) * 2 * fh]
    of1[...] = bb[0, 0:1, : 2 * hh]
    ogn[...] = bb[1, 2:4, :]
    orow[0:2, :] = bb[1, 4:6, :]
    orow[2:3, :] = bb[0, 6:7, :]
    orow[3:4, :] = bb[0, 6:7, :]


def whole_rows(
    block_input,
    cotangent,
    segments,
    positions,
    w_qkv,
    qkv_bias,
    w_out,
    w_fc1,
    fc1_bias,
    w_fc2,
    ln_gains,
    row_biases,
):
    shape = jax.ShapeDtypeStruct
    f32 = jnp.float32
    got = mega(
        block_input,
        cotangent,
        segments,
        positions,
        w_qkv,
        w_out,
        w_fc1,
        w_fc2,
        qkv_bias,
        fc1_bias.reshape(1, -1),
        ln_gains,
        row_biases,
    )
    outs = pl.pallas_call(
        functools.partial(final_kernel, (w_qkv.shape[2] // 2, w_fc1.shape[1] // 2)),
        out_shape=(
            shape(block_input.shape, block_input.dtype),
            shape(block_input.shape, f32),
            shape(w_qkv.shape, f32),
            shape(w_out.shape, f32),
            shape(w_fc1.shape, f32),
            shape(w_fc2.shape, f32),
            shape(qkv_bias.shape, f32),
            shape((1, fc1_bias.size), f32),
            shape(ln_gains.shape, f32),
            shape(row_biases.shape, f32),
        ),
        in_specs=[VM] * 8,
        out_specs=[VM] * 10,
        compiler_params=pltpu.CompilerParams(vmem_limit_bytes=48 * 2**20),
    )(*got, cotangent)
    return (*outs[:7], outs[7].reshape(fc1_bias.shape), *outs[8:])


def block(mesh, *args):
    seqs, rows, width = args[0].shape
    flat, hidden = args[4].shape[2], args[7].shape[1]
    sizes = mesh.shape
    if (
        (sizes["dp"], sizes["seq"], sizes["tensor"]) == (4, 2, 4)
        and flat == 4 * HD
        and seqs <= 2
        and rows == 128
        and width % 512 == 0
        and max(hidden, 3 * flat) <= width <= 1024
        and hidden % 512 == 0
    ):
        return whole_rows(*args)
    return shards(*args)


def solution(mesh):
    return jax.shard_map(
        functools.partial(block, mesh),
        mesh=mesh,
        in_specs=(
            P("dp", "seq", None),
            P("dp", "seq", None),
            P("dp", "seq"),
            P("dp", "seq"),
            P(None, ("dp", "seq"), "tensor"),
            P(None, "tensor"),
            P("tensor", ("dp", "seq")),
            P(("dp", "seq"), "tensor"),
            P("tensor"),
            P("tensor", ("dp", "seq")),
            P(),
            P(),
        ),
        out_specs=(
            P("dp", "seq", None),
            P("dp", "seq", None),
            P(None, ("dp", "seq"), "tensor"),
            P("tensor", ("dp", "seq")),
            P(("dp", "seq"), "tensor"),
            P("tensor", ("dp", "seq")),
            P(None, "tensor"),
            P("tensor"),
            P(),
            P(),
        ),
        check_vma=False,
    )
```

```python
import functools
import math

import jax
import jax.numpy as jnp
from jax import lax
from jax.experimental import pallas as pl
from jax.experimental.pallas import tpu as pltpu
from jax.sharding import PartitionSpec as P

HD = 64
ROT = 16


norm_eps = 1e-05
neg_big = -1e30
inv_root_two = 0.7071067811865476
inv_root_tau = 0.3989422804014327


def layer_norm(values, gain, shift):
    centred = values - jnp.mean(values, axis=-1, keepdims=True)
    inv_std = lax.rsqrt(jnp.mean(centred * centred, axis=-1, keepdims=True) + norm_eps)
    normed = centred * inv_std
    return (normed * gain + shift, normed, inv_std)


def norm_back(grad_out, normed, inv_std, gain):
    scaled = grad_out * gain
    centre = jnp.mean(scaled, axis=-1, keepdims=True)
    slope = jnp.mean(scaled * normed, axis=-1, keepdims=True)
    return inv_std * (scaled - centre - normed * slope)


def gelu_pair(pre_act):
    cumul = 0.5 * (1.0 + lax.erf(pre_act * inv_root_two))
    return (pre_act * cumul, cumul + pre_act * inv_root_tau * jnp.exp(-0.5 * pre_act * pre_act))


def rotary_tables(positions):
    half_rot = ROT // 2
    freqs = 10000.0 ** (-2.0 * jnp.arange(half_rot).astype(jnp.float32) / ROT)
    angles = positions.astype(jnp.float32)[..., None] * freqs
    cosine = jnp.cos(angles)
    sine = jnp.sin(angles)
    return (
        jnp.concatenate([cosine, cosine], -1)[..., None, :],
        jnp.concatenate([sine, sine], -1)[..., None, :],
    )


def rotate(tensor, cosine, sine):
    half_rot = ROT // 2
    head = tensor[..., :ROT]
    turned = jnp.concatenate([-head[..., half_rot:], head[..., :half_rot]], -1)
    return jnp.concatenate([head * cosine + turned * sine, tensor[..., ROT:]], -1)


def unrotate(grads, cosine, sine):
    half_rot = ROT // 2
    head = grads[..., :ROT]
    times_sine = head * sine
    back = jnp.concatenate([times_sine[..., half_rot:], -times_sine[..., :half_rot]], -1)
    return jnp.concatenate([head * cosine + back, grads[..., ROT:]], -1)


def gather_keys(keys_flat, values_in, segments):
    return (
        lax.all_gather(keys_flat, "seq", axis=1, tiled=True),
        lax.all_gather(values_in, "seq", axis=1, tiled=True),
        lax.all_gather(segments, "seq", axis=1, tiled=True),
    )


def pair_terms(
    query_blk,
    query_pos,
    query_seg,
    key_blk,
    value_blk,
    key_pos,
    key_seg,
    grad_blk,
    log_blk,
    delta_blk,
    scale,
):
    scores = (
        jnp.einsum("sqhd,skhd->shqk", query_blk, key_blk, preferred_element_type=jnp.float32)
        * scale
    )
    same_doc = query_seg[:, None, :, None] == key_seg[:, None, None, :]
    earlier = key_pos[None, None, None, :] <= query_pos[None, None, :, None]
    probs = jnp.where(same_doc & earlier, jnp.exp(scores - log_blk[..., None]), 0.0)
    grad_p = jnp.einsum("sqhd,skhd->shqk", grad_blk, value_blk, preferred_element_type=jnp.float32)
    grad_s = (probs * (grad_p - delta_blk[..., None])).astype(jnp.bfloat16)
    return (probs, grad_s)


def shards(
    block_input,
    cotangent,
    segments,
    positions,
    w_qkv,
    qkv_bias,
    w_out,
    w_fc1,
    fc1_bias,
    w_fc2,
    ln_gains,
    row_biases,
):
    seqs_here, rows_here, width = block_input.shape
    heads_here = w_qkv.shape[2] // HD
    flat_width = heads_here * HD
    scale = HD ** (-0.5)
    shape_heads = (seqs_here, rows_here, heads_here, HD)
    forward_weights = (
        lax.all_gather(w_qkv, ("dp", "seq"), axis=1, tiled=True),
        lax.all_gather(w_out, ("dp", "seq"), axis=1, tiled=True),
        lax.all_gather(w_fc1, ("dp", "seq"), axis=0, tiled=True),
        lax.all_gather(w_fc2, ("dp", "seq"), axis=1, tiled=True),
    )
    query_key_value_gathered, output_weight_gathered, up_weight_gathered, down_weight_gathered = (
        forward_weights
    )
    inputs_f = block_input.astype(jnp.float32)
    first_out, first_normed, first_inv = layer_norm(inputs_f, ln_gains[0], row_biases[0])
    second_out, second_normed, second_inv = layer_norm(inputs_f, ln_gains[1], row_biases[1])
    first_norm_input = first_out.astype(jnp.bfloat16)
    second_norm_input = second_out.astype(jnp.bfloat16)
    projected = (
        jnp.einsum(
            "bxf,kfh->kbxh",
            first_norm_input,
            query_key_value_gathered,
            preferred_element_type=jnp.float32,
        )
        + qkv_bias[:, None, None, :]
    )
    cosine, sine = rotary_tables(positions)
    queries = rotate(projected[0].reshape(shape_heads), cosine, sine).astype(jnp.bfloat16)
    keys_flat = (
        rotate(projected[1].reshape(shape_heads), cosine, sine)
        .astype(jnp.bfloat16)
        .reshape(seqs_here, rows_here, flat_width)
    )
    values_in = projected[2].astype(jnp.bfloat16)
    query_pos = lax.axis_index("seq") * rows_here + jnp.arange(rows_here)

    def block_scores(key_block, seg_block, key_start):
        count = key_block.shape[1]
        keys_heads = key_block.reshape(seqs_here, count, heads_here, HD)
        scores = (
            jnp.einsum("sqhd,skhd->shqk", queries, keys_heads, preferred_element_type=jnp.float32)
            * scale
        )
        key_pos = key_start + jnp.arange(count)
        same_doc = segments[:, None, :, None] == seg_block[:, None, None, :]
        earlier = key_pos[None, None, None, :] <= query_pos[None, None, :, None]
        return (scores, same_doc & earlier)

    start_state = (
        jnp.full((seqs_here, heads_here, rows_here), neg_big, jnp.float32),
        jnp.zeros((seqs_here, heads_here, rows_here), jnp.float32),
        jnp.zeros((seqs_here, heads_here, rows_here, HD), jnp.float32),
    )
    key_part = lax.all_gather(keys_flat, "seq", axis=1, tiled=True)
    value_part = lax.all_gather(values_in, "seq", axis=1, tiled=True)
    seg_part = lax.all_gather(segments, "seq", axis=1, tiled=True)
    count = key_part.shape[1]
    attend_block = math.gcd(count, 512)

    def step_block(block_idx, state):
        run_max, run_sum, accum = state
        offset = block_idx * attend_block
        key_block = lax.dynamic_slice_in_dim(key_part, offset, attend_block, 1)
        value_block = lax.dynamic_slice_in_dim(value_part, offset, attend_block, 1).reshape(
            seqs_here, attend_block, heads_here, HD
        )
        seg_block = lax.dynamic_slice_in_dim(seg_part, offset, attend_block, 1)
        scores, allowed = block_scores(key_block, seg_block, offset)
        new_max = jnp.maximum(run_max, jnp.max(jnp.where(allowed, scores, neg_big), axis=-1))
        factor = jnp.exp(run_max - new_max)
        expo = jnp.where(allowed, jnp.exp(scores - new_max[..., None]), 0.0)
        new_sum = run_sum * factor + jnp.sum(expo, axis=-1)
        update = jnp.einsum(
            "shqk,skhd->shqd",
            expo.astype(jnp.bfloat16),
            value_block,
            preferred_element_type=jnp.float32,
        )
        return (new_max, new_sum, accum * factor[..., None] + update)

    run_max, run_sum, accum = lax.fori_loop(0, count // attend_block, step_block, start_state)
    log_sum = run_max + jnp.log(run_sum)
    attention_context = (
        (accum / run_sum[..., None])
        .transpose(0, 2, 1, 3)
        .reshape(seqs_here, rows_here, flat_width)
        .astype(jnp.bfloat16)
    )
    pre_act = (
        jnp.einsum(
            "vrk,kt->vrt", second_norm_input, up_weight_gathered, preferred_element_type=jnp.float32
        )
        + fc1_bias
    )
    activ, gelu_slope = gelu_pair(pre_act)
    hidden_activation = activ.astype(jnp.bfloat16)
    partial_output_sum = jnp.einsum(
        "qhw,wj->qhj", attention_context, output_weight_gathered, preferred_element_type=jnp.float32
    )
    partial_output_sum = partial_output_sum + jnp.einsum(
        "qzg,gc->qzc", hidden_activation, down_weight_gathered, preferred_element_type=jnp.float32
    )
    branches = lax.psum(partial_output_sum.astype(jnp.bfloat16), "tensor").astype(jnp.float32)
    output = (inputs_f + branches + row_biases[2] + row_biases[3]).astype(jnp.bfloat16)
    query_key_value_backward, output_weight_backward, up_weight_backward, down_weight_backward = (
        lax.all_gather(w_qkv, ("dp", "seq"), axis=1, tiled=True),
        lax.all_gather(w_out, ("dp", "seq"), axis=1, tiled=True),
        lax.all_gather(w_fc1, ("dp", "seq"), axis=0, tiled=True),
        lax.all_gather(w_fc2, ("dp", "seq"), axis=1, tiled=True),
    )
    grad_f = cotangent.astype(jnp.float32)
    gradient_output_weight = jnp.einsum(
        "bxz,bxe->ze", attention_context, cotangent, preferred_element_type=jnp.float32
    )
    grad_context = jnp.einsum(
        "zpi,xi->zpx", cotangent, output_weight_backward, preferred_element_type=jnp.float32
    ).astype(jnp.bfloat16)
    gradient_down_weight = jnp.einsum(
        "tzi,tzo->io", hidden_activation, cotangent, preferred_element_type=jnp.float32
    )
    grad_pre = (
        jnp.einsum(
            "hvg,rg->hvr", cotangent, down_weight_backward, preferred_element_type=jnp.float32
        )
        * gelu_slope
    )
    gradient_hidden_input = grad_pre.astype(jnp.bfloat16)
    grad_fc1_w = jnp.einsum(
        "mxa,mxr->ar", second_norm_input, gradient_hidden_input, preferred_element_type=jnp.float32
    )
    grad_second = jnp.einsum(
        "ikq,uq->iku", gradient_hidden_input, up_weight_backward, preferred_element_type=jnp.float32
    )
    grad_ctx_heads = grad_context.reshape(shape_heads)
    delta = jnp.sum(
        grad_ctx_heads.astype(jnp.float32)
        * attention_context.reshape(shape_heads).astype(jnp.float32),
        axis=-1,
    ).transpose(0, 2, 1)
    key_all, value_all, seg_all = gather_keys(keys_flat, values_in, segments)
    total_len = key_all.shape[1]
    block = math.gcd(total_len, 512)

    def key_slices(offset):
        key_block = lax.dynamic_slice_in_dim(key_all, offset, block, 1).reshape(
            seqs_here, block, heads_here, HD
        )
        value_block = lax.dynamic_slice_in_dim(value_all, offset, block, 1).reshape(
            seqs_here, block, heads_here, HD
        )
        seg_block = lax.dynamic_slice_in_dim(seg_all, offset, block, 1)
        return (key_block, value_block, seg_block)

    def back_block(block_idx, state):
        grad_q, grad_key_all, grad_value_all = state
        offset = block_idx * block
        key_block, value_block, seg_block = key_slices(offset)
        probs, grad_s = pair_terms(
            queries,
            query_pos,
            segments,
            key_block,
            value_block,
            offset + jnp.arange(block),
            seg_block,
            grad_ctx_heads,
            log_sum,
            delta,
            scale,
        )
        grad_v = jnp.einsum(
            "shqk,sqhd->skhd",
            probs.astype(jnp.bfloat16),
            grad_ctx_heads,
            preferred_element_type=jnp.float32,
        )
        grad_q = (
            grad_q
            + jnp.einsum("shqk,skhd->sqhd", grad_s, key_block, preferred_element_type=jnp.float32)
            * scale
        )
        grad_k = (
            jnp.einsum("shqk,sqhd->skhd", grad_s, queries, preferred_element_type=jnp.float32)
            * scale
        )
        grad_key_all = lax.dynamic_update_slice_in_dim(
            grad_key_all, grad_k.reshape(seqs_here, block, flat_width), offset, 1
        )
        grad_value_all = lax.dynamic_update_slice_in_dim(
            grad_value_all, grad_v.reshape(seqs_here, block, flat_width), offset, 1
        )
        return (grad_q, grad_key_all, grad_value_all)

    back_start = (
        jnp.zeros(shape_heads, jnp.float32),
        jnp.zeros((seqs_here, total_len, flat_width), jnp.float32),
        jnp.zeros((seqs_here, total_len, flat_width), jnp.float32),
    )
    grad_q, grad_key_all, grad_value_all = lax.fori_loop(
        0, total_len // block, back_block, back_start
    )
    grad_key_here, grad_value_here = (
        lax.psum_scatter(
            grad_key_all.astype(jnp.bfloat16), "seq", scatter_dimension=1, tiled=True
        ).astype(jnp.float32),
        lax.psum_scatter(
            grad_value_all.astype(jnp.bfloat16), "seq", scatter_dimension=1, tiled=True
        ).astype(jnp.float32),
    )
    grad_proj = jnp.stack(
        [
            unrotate(grad_q, cosine, sine).reshape(seqs_here, rows_here, flat_width),
            unrotate(grad_key_here.reshape(shape_heads), cosine, sine).reshape(
                seqs_here, rows_here, flat_width
            ),
            grad_value_here,
        ]
    )
    grad_bias_qkv = jnp.sum(grad_proj, axis=(1, 2))
    gradient_projection_input = grad_proj.astype(jnp.bfloat16)
    grad_qkv_w = jnp.einsum(
        "ink,oint->okt",
        first_norm_input,
        gradient_projection_input,
        preferred_element_type=jnp.float32,
    )
    grad_first = jnp.einsum(
        "etbp,eop->tbo",
        gradient_projection_input,
        query_key_value_backward,
        preferred_element_type=jnp.float32,
    )
    grad_first, grad_second = (
        lax.psum(grad_first.astype(jnp.bfloat16), "tensor").astype(jnp.float32),
        lax.psum(grad_second.astype(jnp.bfloat16), "tensor").astype(jnp.float32),
    )
    grad_input = (
        grad_f
        + norm_back(grad_first, first_normed, first_inv, ln_gains[0])
        + norm_back(grad_second, second_normed, second_inv, ln_gains[1])
    )
    gain_terms = jnp.stack(
        [
            jnp.sum(grad_first * first_normed, axis=(0, 1)),
            jnp.sum(grad_second * second_normed, axis=(0, 1)),
        ]
    )
    row_terms = jnp.stack(
        [
            jnp.sum(grad_first, axis=(0, 1)),
            jnp.sum(grad_second, axis=(0, 1)),
            jnp.sum(grad_f, axis=(0, 1)),
            jnp.sum(grad_f, axis=(0, 1)),
        ]
    )
    bias_sums = lax.psum(
        (grad_bias_qkv, jnp.sum(grad_pre, axis=(0, 1)), gain_terms, row_terms), ("dp", "seq")
    )
    weight_sums = (
        lax.psum_scatter(grad_qkv_w, ("dp", "seq"), scatter_dimension=1, tiled=True),
        lax.psum_scatter(gradient_output_weight, ("dp", "seq"), scatter_dimension=1, tiled=True),
        lax.psum_scatter(grad_fc1_w, ("dp", "seq"), scatter_dimension=0, tiled=True),
        lax.psum_scatter(gradient_down_weight, ("dp", "seq"), scatter_dimension=1, tiled=True),
    )
    return (
        output,
        grad_input,
        weight_sums[0],
        weight_sums[1],
        weight_sums[2],
        weight_sums[3],
        bias_sums[0],
        bias_sums[1],
        bias_sums[2],
        bias_sums[3],
    )


MESH = pl.DeviceIdType.MESH
ANY = pl.BlockSpec(memory_space=pl.ANY)
VM = pl.BlockSpec(memory_space=pltpu.VMEM)
HBM = pl.BlockSpec(memory_space=pltpu.HBM)


def remote(src, dst, send, recv, where):
    return pltpu.make_async_remote_copy(
        src_ref=src, dst_ref=dst, send_sem=send, recv_sem=recv, device_id=where, device_id_type=MESH
    )


def pair_of(d):
    return d + 1 - 2 * lax.rem(d, 2)


def dot_nn(left, right):
    return lax.dot_general(left, right, (((1,), (0,)), ((), ())), preferred_element_type=jnp.float32)


def dot_nt(left, right):
    return lax.dot_general(left, right, (((1,), (1,)), ((), ())), preferred_element_type=jnp.float32)


def dot_tn(left, right):
    return lax.dot_general(left, right, (((0,), (0,)), ((), ())), preferred_element_type=jnp.float32)


def spread(left, right):
    return lax.dot_general(
        left,
        right,
        (((0,), (0,)), ((), ())),
        precision=lax.Precision.HIGHEST,
        preferred_element_type=jnp.float32,
    )


def loop(count, body):
    def step(i, carry):
        body(i)
        return carry

    lax.fori_loop(0, count, step, 0)


def at(index, size):
    return pl.ds(pl.multiple_of(index * size, size), size)


def mega_kernel(dims, *refs):
    f32, bf16 = jnp.float32, jnp.bfloat16
    seqs, rows, width, kr, oc, fh, hh = dims
    length = 2 * rows
    tokens = seqs * length
    heads = fh // HD
    scale = HD ** (-0.5)
    (x, c, seg, pos, wq, wo, w1, w2, *small) = refs[:12]
    R = refs[12:16]
    yfin, gfin, bout = refs[16:19]
    (xf, cf, segb, posb, GQ, GO, G1, G2) = refs[19:27]
    (first, second, nrm, tables, qs, ks, vs, gcs, ctx, gproj) = refs[27:37]
    (gacc, hid, slope, ghid) = refs[37:41]
    gW = refs[41:45]
    mid = refs[45:49]
    (part, sibp, chip, ein, xin, fw) = refs[49:55]
    (brow, bpair, bsum, bgot2, bsum2, bgot3) = refs[55:61]
    (s1, r1, s2, r2, ss, sr, sl) = refs[61:68]
    (ts, tr, tl) = refs[68:71]
    (ms, mr, ds_, dr, hs, hr, bs, br, bl) = refs[71:80]
    (ps, pr, es, er, xs, xr, fs, fr, fs2) = refs[80:89]
    (b1s, b1r, b2s, b2r, b3s, b3r) = refs[89:95]
    qb, f1b, gains, rowb = refs[95:99]
    small_sem = refs[99]
    nseq, nt, ndp = 2, 4, 4
    d, s, t = lax.axis_index("dp"), lax.axis_index("seq"), lax.axis_index("tensor")
    other = 1 - s
    near_x, near_y, corner = pair_of(d), lax.rem(d + 2, 4), 3 - d
    me = d * nseq + s
    side = t // 2
    mi, th = side, 1 - side
    inner = (t == 1) | (t == 2)
    end = (t == 0) | (t == 3)
    pt, facing = {"tensor": pair_of(t)}, {"tensor": 3 - t}

    small_copies = [
        pltpu.make_async_copy(src, dst, small_sem.at[j])
        for j, (src, dst) in enumerate(zip(small, (qb, f1b, gains, rowb)))
    ]
    local_x = pltpu.make_async_copy(x, xf.at[:, at(s, rows), :], tl.at[0])
    for copy in (local_x, *small_copies):
        copy.start()
    barrier = pltpu.get_barrier_semaphore()
    for peer in (near_x, near_y):
        for core in (0, 1):
            pl.semaphore_signal(
                barrier, inc=1, device_id={"dp": peer, "seq": core}, device_id_type=MESH
            )
    pl.semaphore_signal(barrier, inc=1, device_id={"seq": other}, device_id_type=MESH)
    pl.semaphore_signal(barrier, inc=1, device_id=pt, device_id_type=MESH)

    @pl.when(inner)
    def _():
        pl.semaphore_signal(barrier, inc=1, device_id=facing, device_id_type=MESH)
        pl.semaphore_wait(barrier, 7)

    @pl.when(end)
    def _():
        pl.semaphore_wait(barrier, 6)

    sends = []

    def go(copy):
        copy.start()
        sends.append(copy)
        return copy

    def source(a, half):
        return (
            lambda: wq.at[:, :, at(half, fh)],
            lambda: wo.at[at(half, fh), :],
            lambda: w1.at[:, at(half, hh)],
            lambda: w2.at[at(half, hh), :],
        )[a]()

    def place(bufs, a, index):
        return (
            lambda: bufs[0].at[:, at(index, kr), :],
            lambda: bufs[1].at[:, at(index, oc)],
            lambda: bufs[2].at[at(index, kr), :],
            lambda: bufs[3].at[:, at(index, oc)],
        )[a]()

    full = (GQ, GO, G1, G2)
    sibs, locals_ = {}, {}

    def hop1_copy(a, way, k):
        near, half = (near_x, near_y)[way], (s, other)[k]
        return remote(
            source(a, half),
            place(full, a, me),
            s1.at[a, way, k],
            r1.at[a, way, k],
            {"dp": near, "seq": half},
        )

    def start_hop1(a):
        for way in (0, 1):
            for k in (0, 1):
                hop1_copy(a, way, k).start()

    def start_near(a):
        sibs[a] = go(
            remote(source(a, other), place(full, a, me), ss.at[a], sr.at[a], {"seq": other})
        )
        locals_[a] = pltpu.make_async_copy(source(a, s), place(full, a, me), sl.at[a])
        locals_[a].start()

    def hop2_copy(a, way):
        view = place(full, a, (near_x * nseq, near_y * nseq + 1)[way])
        return remote(view, view, s2.at[a, way], r2.at[a, way], {"dp": (near_y, near_x)[way]})

    def start_hop2(a):
        for way in (0, 1):
            for k in (0, 1):
                hop1_copy(a, way, k).wait_recv()
        for way in (0, 1):
            hop2_copy(a, way).start()

    def wait_all(a):
        hop2_copy(a, 0).wait_recv()
        hop2_copy(a, 1).wait_recv()
        sibs[a].wait_recv()
        locals_[a].wait()

    mine = at(s, rows)
    start_hop1(0)
    start_hop1(1)
    tok = []
    for j, (src, dst) in enumerate(
        ((x, xf.at[:, mine, :]), (pos, posb.at[s]), (seg, segb.at[s]), (c, cf.at[:, mine, :]))
    ):
        copy = local_x
        if j > 0:
            copy = pltpu.make_async_copy(src, dst, tl.at[j])
            copy.start()
        tok.append((copy, go(remote(src, dst, ts.at[j], tr.at[j], {"seq": other}))))
    start_near(0)
    start_near(1)
    start_hop1(2)
    start_near(2)
    start_near(3)

    step = 32
    per = rows // step

    def norm_half(half):
        def body(i):
            b, at_row = i // per, pl.multiple_of(half * rows + lax.rem(i, per) * step, step)
            flat_row = pl.multiple_of(b * length + at_row, step)
            values = xf[b, pl.ds(at_row, step), :].astype(f32)
            one, normed, _ = layer_norm(values, gains[0:1, :], rowb[0:1, :])
            span = pl.ds(flat_row, step)
            nrm[span, :] = normed
            first[span, :] = one.astype(bf16)
            second[span, :] = (normed * gains[1:2, :] + rowb[1:2, :]).astype(bf16)

        loop(seqs * per, body)

    for copy in small_copies:
        copy.wait()
    tok[0][0].wait()
    norm_half(s)
    tok[0][1].wait_recv()
    norm_half(other)
    for j in (1, 2, 3):
        tok[j][0].wait()
    brow[...] = jnp.zeros_like(brow)
    ones = jnp.ones((16, rows), bf16)
    csum = dot_nn(ones, cf[0, mine, :])
    for b in range(1, seqs):
        csum = csum + dot_nn(ones, cf[b, mine, :])
    brow[6:7, :] = csum[0:1, :]
    for j in (1, 2, 3):
        tok[j][1].wait_recv()

    half_rot = ROT // 2
    lane = lax.broadcasted_iota(jnp.int32, (half_rot, fh), 1)
    lane = lax.rem(lane, HD)
    which = lax.broadcasted_iota(jnp.int32, (half_rot, fh), 0)
    low = (lane == which).astype(f32)
    high = (lane == which + half_rot).astype(f32)
    rest = (lane[0:1, :] >= ROT).astype(f32)
    power = lax.broadcasted_iota(jnp.int32, (half_rot, length), 0).astype(f32)
    freqs = jnp.exp(power * (-2.0 / ROT * math.log(10000.0)))
    for b in range(seqs):
        row = jnp.concatenate([posb[0, b : b + 1, :], posb[1, b : b + 1, :]], axis=1).astype(f32)
        angles = row * freqs
        sine = jnp.sin(angles)
        tables[0, at(b, length), :] = spread(jnp.cos(angles), low + high) + rest
        tables[1, at(b, length), :] = spread(sine, high)
        tables[2, at(b, length), :] = spread(sine, -low)

    start_hop2(0)
    start_hop2(1)
    start_hop1(3)
    start_hop2(2)
    wait_all(0)
    wait_all(1)

    def project(b):
        span = at(b, length)
        inputs = first[span, :]
        cosine, sin_a, sin_b = tables[0, span, :], tables[1, span, :], tables[2, span, :]

        def turn(v):
            up, down = pltpu.roll(v, half_rot, 1), pltpu.roll(v, fh - half_rot, 1)
            return v * cosine + up * sin_a + down * sin_b

        bias = lambda j: qb[j : j + 1, at(s, fh)]
        qs[span, :] = turn(dot_nn(inputs, GQ[0]) + bias(0)).astype(bf16)
        ks[span, :] = turn(dot_nn(inputs, GQ[1]) + bias(1)).astype(bf16)
        vs[span, :] = (dot_nn(inputs, GQ[2]) + bias(2)).astype(bf16)
        gcs[span, :] = dot_nt(cf[b], GO[...]).astype(bf16)

    loop(seqs, project)

    lane_of = lax.broadcasted_iota(jnp.int32, (1, fh), 1) // HD

    def attend(b):
        @pl.when(b == seqs - 1)
        def _():
            start_hop2(3)

        span = at(b, length)
        q, k, v, gc = qs[span, :], ks[span, :], vs[span, :], gcs[span, :]
        seg_rows = [
            jnp.concatenate(
                [segb[0, n : n + 1, :], segb[1, n : n + 1, :]], axis=1
            ).astype(f32)
            for n in range(seqs)
        ]
        seg_row = seg_rows[0]
        for n in range(1, seqs):
            seg_row = jnp.where(b == n, seg_rows[n], seg_row)
        pick = (lax.broadcasted_iota(jnp.int32, (8, length), 0) == 0).astype(f32)
        seg_col = spread(jnp.broadcast_to(seg_row, (8, length)), pick)
        q_pos = lax.broadcasted_iota(jnp.int32, (length, length), 0)
        k_pos = lax.broadcasted_iota(jnp.int32, (length, length), 1)
        allowed = (seg_col == seg_row) & (k_pos <= q_pos)
        out = []
        for h in range(heads):
            keep = (lane_of == h).astype(bf16)
            scores = dot_nt(q * keep, k) * scale
            row_max = jnp.max(jnp.where(allowed, scores, neg_big), axis=-1, keepdims=True)
            expo = jnp.where(allowed, jnp.exp(scores - row_max), 0.0)
            inv = 1.0 / jnp.sum(expo, axis=-1, keepdims=True)
            mixed = (dot_nn(expo.astype(bf16), v) * inv).astype(bf16) * keep
            gch = gc * keep
            delta = jnp.sum(gch.astype(f32) * mixed.astype(f32), axis=-1, keepdims=True)
            probs = expo * inv
            grad_s = (probs * (dot_nt(gch, v) - delta)).astype(bf16)
            terms = (
                mixed,
                dot_nn(grad_s, k * keep),
                dot_tn(grad_s, q * keep),
                dot_tn(probs.astype(bf16), gch),
            )
            out = [p + q_ for p, q_ in zip(out, terms)] if out else list(terms)
        ctx[span, :] = out[0]
        cosine, sin_a, sin_b = tables[0, span, :], tables[1, span, :], tables[2, span, :]

        def back(v):
            up, down = pltpu.roll(v, half_rot, 1), pltpu.roll(v, fh - half_rot, 1)
            return v * cosine - up * sin_a - down * sin_b

        for j, grad in enumerate((back(out[1] * scale), back(out[2] * scale), out[3])):
            gproj[j, span, :] = grad.astype(bf16)
            spot = pl.ds(pl.multiple_of(j * 2 * fh + s * fh, fh), fh)
            brow[1:2, spot] = brow[1:2, spot] + jnp.sum(grad, axis=0, keepdims=True)

    loop(seqs, attend)

    pairs, mids, lasts = {}, {}, {}

    def start_reduce(a):
        gone = lambda index: place(gW, a, index)
        mids[a, 0] = go(
            remote(gone(corner * 2), mid[a].at[0], ms.at[a, 0], mr.at[a, 0], {"dp": near_x})
        )
        mids[a, 1] = go(
            remote(gone(corner * 2 + 1), mid[a].at[1], ms.at[a, 1], mr.at[a, 1], {"dp": near_y})
        )
        go(
            remote(
                gone(near_x * 2), R[a].at[s, 1], ds_.at[a, 0], dr.at[a, s], {"dp": near_x, "seq": 0}
            )
        )
        go(
            remote(
                gone(near_y * 2 + 1),
                R[a].at[s, 1],
                ds_.at[a, 1],
                dr.at[a, s],
                {"dp": near_y, "seq": 1},
            )
        )
        pairs[a] = go(
            remote(gone(d * 2 + other), R[a].at[s, 0], bs.at[a], br.at[a], {"seq": other})
        )
        lasts[a] = pltpu.make_async_copy(gone(me), R[a].at[s, 0], bl.at[a])
        lasts[a].start()

    def second_reduce(a):
        for way, near, index in ((0, near_y, near_y * 2), (1, near_x, near_x * 2 + 1)):
            mids[a, way].wait_recv()
            mid[a][way] = (
                mid[a][way].astype(f32) + place(gW, a, index)[...].astype(f32)
            ).astype(bf16)
            go(
                remote(
                    mid[a].at[way],
                    R[a].at[s, 2],
                    hs.at[a, way],
                    hr.at[a, s],
                    {"dp": near, "seq": way},
                )
            )

    def finish_reduce(a):
        for h in (0, 1):
            remote(R[a].at[h, 1], R[a].at[h, 1], ds_.at[a, 0], dr.at[a, h], {"dp": near_x}).wait_recv()
            remote(R[a].at[h, 2], R[a].at[h, 2], hs.at[a, 0], hr.at[a, h], {"dp": near_x}).wait_recv()
        pairs[a].wait_recv()
        lasts[a].wait()

    big = 256
    wide = 512

    def qkv_grad(i):
        rows_of = at(i, big)
        lhs = first[:, rows_of]
        for j in range(3):
            gW[0][j, rows_of, :] = dot_tn(lhs, gproj[j]).astype(bf16)

    loop(width // big, qkv_grad)

    def out_grad(i):
        cols = at(i, wide)
        gW[1][:, cols] = dot_tn(ctx[...], cf[:, :, cols].reshape(tokens, wide)).astype(bf16)

    loop(width // wide, out_grad)
    start_reduce(0)
    start_reduce(1)

    tiles = width // wide

    def first_back(i):
        b, n = i // tiles, lax.rem(i, tiles)
        span, cols = at(b, length), at(n, wide)
        grad = dot_nt(gproj[0, span, :], GQ[0, cols, :])
        for j in (1, 2):
            grad = grad + dot_nt(gproj[j, span, :], GQ[j, cols, :])
        gacc[span, cols] = grad * gains[0:1, cols]
        brow[2:3, cols] = brow[2:3, cols] + jnp.sum(grad * nrm[span, cols], axis=0, keepdims=True)
        brow[4:5, cols] = brow[4:5, cols] + jnp.sum(grad, axis=0, keepdims=True)

    loop(seqs * tiles, first_back)

    wait_all(2)

    def up(b):
        span = at(b, length)
        slope[span, :] = dot_nn(second[span, :], G1[...]) + f1b[:, at(s, hh)]

        def curve(i):
            part_of = pl.ds(pl.multiple_of(b * length + i * step, step), step)
            activ, incline = gelu_pair(slope[part_of, :])
            hid[part_of, :] = activ.astype(bf16)
            slope[part_of, :] = incline

        loop(length // step, curve)

    loop(seqs, up)

    def down_grad(i):
        m, n = i // tiles, lax.rem(i, tiles)
        units, cols = at(m, big), at(n, wide)
        gW[3][units, cols] = dot_tn(
            hid[:, units], cf[:, :, cols].reshape(tokens, wide)
        ).astype(bf16)

    loop(hh // big * tiles, down_grad)

    wait_all(3)

    def branch(i):
        b, n = i // tiles, lax.rem(i, tiles)
        span, cols = at(b, length), at(n, wide)
        total = dot_nn(ctx[span, :], GO[:, cols]) + dot_nn(hid[span, :], G2[:, cols])
        part[0, b, :, cols] = total.astype(bf16)
        cross_tile(0, b, cols)

    theirs_half = at(other, rows)

    def cross_tile(j, b, cols):
        remote(
            part.at[j, b, theirs_half, cols],
            sibp.at[j, b, :, cols],
            ps.at[j],
            pr.at[j],
            {"seq": other},
        ).start()

    def crossed(j):
        return remote(
            part.at[j, :, theirs_half, :], sibp.at[j], ps.at[j], pr.at[j], {"seq": other}
        )

    loop(seqs * tiles, branch)
    start_reduce(3)

    def down_back(b):
        span = at(b, length)
        grad = dot_nt(cf[b], G2[...]) * slope[span, :]
        ghid[span, :] = grad.astype(bf16)
        spot = at(s, hh)
        brow[0:1, spot] = brow[0:1, spot] + jnp.sum(grad, axis=0, keepdims=True)

    loop(seqs, down_back)

    nc = 2
    cr = rows // nc
    fin = (yfin, gfin)
    chunk = lambda ch: slice(ch * cr, (ch + 1) * cr)

    def to_inner(j, i, b, ch):
        view = (j, b, pl.ds(ch * cr, cr))
        return remote(chip.at[view], ein.at[view], es.at[j, i, ch], er.at[j, i, ch], pt)

    def over(j, ch):
        view = (j, pl.ds(ch * cr, cr))
        return remote(fw.at[view], xin.at[view], xs.at[j, ch], xr.at[j, ch], facing)

    def final(j, b, ch, send, slot, where):
        view = fin[j].at[b, pl.ds(ch * cr, cr)]
        return remote(view, view, send, fr.at[j, slot, ch], where)

    def z_one(j):
        crossed(j).wait_recv()
        for i, b in ((0, th), (1, mi)):
            for ch in range(nc):
                here = pl.ds(pl.multiple_of(s * rows + ch * cr, cr), cr)
                chip[j, b, chunk(ch)] = (
                    part[j, b, here, :].astype(f32) + sibp[j, b, chunk(ch)].astype(f32)
                ).astype(bf16)

                @pl.when(end)
                def _():
                    to_inner(j, i, b, ch).start()

    def z_two(j):
        @pl.when(inner)
        def _():
            for ch in range(nc):
                to_inner(j, 0, th, ch).wait_recv()
                fw[j, chunk(ch)] = (
                    chip[j, th, chunk(ch)].astype(f32) + ein[j, th, chunk(ch)].astype(f32)
                ).astype(bf16)
                over(j, ch).start()

    def z_three(j):
        @pl.when(inner)
        def _():
            for ch in range(nc):
                to_inner(j, 1, mi, ch).wait_recv()
                over(j, ch).wait_recv()
                total = (
                    chip[j, mi, chunk(ch)].astype(f32)
                    + ein[j, mi, chunk(ch)].astype(f32)
                    + xin[j, chunk(ch)].astype(f32)
                )
                here = pl.ds(pl.multiple_of(s * rows + ch * cr, cr), cr)
                inputs = xf[mi, here, :].astype(f32)
                if j == 0:
                    result = inputs + total + rowb[2:3, :] + rowb[3:4, :]
                else:
                    _, normed, inv_std = layer_norm(inputs, 1.0, 0.0)
                    result = norm_back(total, normed, inv_std, 1.0)
                fin[j][mi, chunk(ch)] = result.astype(bf16)
                final(j, mi, ch, fs.at[j, 0, ch], 0, pt).start()
                final(j, mi, ch, fs.at[j, 1, ch], 1, facing).start()

    def z_four(j):
        @pl.when(inner)
        def _():
            for ch in range(nc):
                final(j, th, ch, fs.at[j, 1, ch], 1, facing).wait_recv()
                final(j, th, ch, fs2.at[j, ch], 1, pt).start()

    def z_five(j):
        crossed(j).wait_send()
        for ch in range(nc):

            @pl.when(end)
            def _():
                for i, b in ((0, th), (1, mi)):
                    to_inner(j, i, b, ch).wait_send()
                final(j, mi, ch, fs.at[j, 0, ch], 0, pt).wait_recv()
                final(j, th, ch, fs2.at[j, ch], 1, pt).wait_recv()

            @pl.when(inner)
            def _():
                over(j, ch).wait_send()
                final(j, mi, ch, fs.at[j, 0, ch], 0, pt).wait_send()
                final(j, mi, ch, fs.at[j, 1, ch], 1, facing).wait_send()
                final(j, th, ch, fs2.at[j, ch], 1, pt).wait_send()

    z_one(0)

    def second_back(i):
        b, n = i // tiles, lax.rem(i, tiles)
        span, cols = at(b, length), at(n, wide)
        grad = dot_nt(ghid[span, :], G1[cols, :])
        part[1, b, :, cols] = (gacc[span, cols] + grad * gains[1:2, cols]).astype(bf16)
        cross_tile(1, b, cols)
        brow[3:4, cols] = brow[3:4, cols] + jnp.sum(grad * nrm[span, cols], axis=0, keepdims=True)
        brow[5:6, cols] = brow[5:6, cols] + jnp.sum(grad, axis=0, keepdims=True)

    loop(seqs * tiles, second_back)
    bpair_copy = go(remote(brow, bpair, b1s, b1r, {"seq": other}))

    def up_grad(i):
        rows_of = at(i, big)
        gW[2][rows_of, :] = dot_tn(second[:, rows_of], ghid[...]).astype(bf16)

    loop(width // big, up_grad)
    start_reduce(2)
    second_reduce(0)
    second_reduce(1)
    bpair_copy.wait_recv()
    bsum[...] = brow[...] + bpair[...]
    x_send = go(remote(bsum, bgot2.at[0], b2s.at[0], b2r.at[0], {"dp": near_x}))
    z_one(1)
    z_two(0)
    second_reduce(3)
    z_three(0)
    x_send.wait_recv()
    bsum2[...] = bsum[...] + bgot2[0]
    y_send = go(remote(bsum2, bgot2.at[1], b2s.at[1], b2r.at[1], {"dp": near_y}))
    second_reduce(2)
    y_send.wait_recv()
    bgot2[2] = bsum2[...] + bgot2[1]
    bout[0] = bgot2[2]

    def bias_hop(src, dst, where):
        return remote(
            bgot2.at[2] if src == 0 else bgot3.at[3],
            bgot3.at[dst],
            b3s.at[src],
            b3r.at[dst],
            where,
        )

    @pl.when(end)
    def _():
        bias_hop(0, 0, pt).start()

    z_two(1)
    z_four(0)

    @pl.when(inner)
    def _():
        bias_hop(0, 0, pt).wait_recv()
        bgot3[3] = bgot2[2] + bgot3[0]
        bias_hop(1, 1, facing).start()

    z_three(1)

    @pl.when(inner)
    def _():
        bias_hop(1, 1, facing).wait_recv()
        bias_hop(1, 1, facing).wait_send()
        bgot3[3] = bgot3[3] + bgot3[1]
        bias_hop(2, 2, pt).start()
        bout[1] = bgot3[3]

    z_four(1)
    @pl.when(end)
    def _():
        bias_hop(0, 0, pt).wait_send()
        bias_hop(2, 2, pt).wait_recv()
        bout[1] = bgot3[2]

    @pl.when(inner)
    def _():
        bias_hop(2, 2, pt).wait_send()

    z_five(0)
    z_five(1)
    for a in (0, 1, 3, 2):
        finish_reduce(a)
    for a in range(4):
        for way in (0, 1):
            for k in (0, 1):
                hop1_copy(a, way, k).wait_send()
            hop2_copy(a, way).wait_send()
    for copy in sends:
        copy.wait_send()


def mega(x, c, seg, pos, wq, wo, w1, w2, qb, f1b, gains, rowb):
    shape = jax.ShapeDtypeStruct
    f32, bf16 = jnp.float32, jnp.bfloat16
    seqs, rows, width = x.shape
    kr, oc, fh, hh = wq.shape[1], wo.shape[1], wq.shape[2] // 2, w1.shape[1] // 2
    length = rows * 2
    tokens = seqs * length
    nc = 2
    pieces = ((3, kr, fh), (fh, oc), (kr, hh), (hh, oc))
    fulls = ((3, width, fh), (fh, width), (width, hh), (hh, width))
    dma = pltpu.SemaphoreType.DMA
    vm = lambda dims, kind: pltpu.VMEM(dims, kind)
    bias = (8, width)
    scratch = [
        vm((seqs, length, width), bf16),
        vm((seqs, length, width), bf16),
        vm((2,) + seg.shape, jnp.int32),
        vm((2,) + pos.shape, jnp.int32),
        *[vm(f, bf16) for f in fulls],
        vm((tokens, width), bf16),
        vm((tokens, width), bf16),
        vm((tokens, width), f32),
        vm((3, tokens, fh), f32),
        *[vm((tokens, fh), bf16)] * 5,
        vm((3, tokens, fh), bf16),
        vm((tokens, width), f32),
        vm((tokens, hh), bf16),
        vm((tokens, hh), f32),
        vm((tokens, hh), bf16),
        *[vm(f, bf16) for f in fulls],
        *[vm((2,) + p, bf16) for p in pieces],
        vm((2, seqs, length, width), bf16),
        *[vm((2, seqs, rows, width), bf16)] * 3,
        *[vm((2, rows, width), bf16)] * 2,
        vm(bias, f32),
        vm(bias, f32),
        vm(bias, f32),
        vm((4,) + bias, f32),
        vm(bias, f32),
        vm((4,) + bias, f32),
        *[dma((4, 2, 2))] * 2,
        *[dma((4, 2))] * 2,
        *[dma((4,))] * 3,
        *[dma((4,))] * 3,
        *[dma((4, 2))] * 6,
        *[dma((4,))] * 3,
        *[dma((2,))] * 2,
        *[dma((2, 2, nc))] * 2,
        *[dma((2, nc))] * 2,
        *[dma((2, 2, nc))] * 2,
        dma((2, nc)),
        dma,
        dma,
        *[dma((4,))] * 4,
        *[vm(v.shape, f32) for v in (qb, f1b, gains, rowb)],
        dma((4,)),
    ]
    return pl.pallas_call(
        functools.partial(mega_kernel, (seqs, rows, width, kr, oc, fh, hh)),
        out_shape=(
            *[shape((2, 3) + p, bf16) for p in pieces],
            shape(x.shape, bf16),
            shape(x.shape, bf16),
            shape((2,) + bias, f32),
        ),
        in_specs=[HBM] * 12,
        out_specs=[HBM] * 4 + [VM] * 3,
        scratch_shapes=scratch,
        compiler_params=pltpu.CompilerParams(
            collective_id=0, has_side_effects=True, vmem_limit_bytes=63 * 2**20
        ),
    )(x, c, seg, pos, wq, wo, w1, w2, qb, f1b, gains, rowb)


def final_kernel(dims, *refs):
    f32 = jnp.float32
    fh, hh = dims
    rq, ro, r1, r2, yf, gf, bb, c = refs[:8]
    out, gin, oq, oo, o1, o2, oqb, of1, ogn, orow = refs[8:]

    def total(ref, *index):
        return (
            ref[(index[0], 0) + index[1:]].astype(f32)
            + ref[(index[0], 1) + index[1:]].astype(f32)
            + ref[(index[0], 2) + index[1:]].astype(f32)
        )

    for h in (0, 1):
        for j in range(3):
            oq[j, :, h * fh : (h + 1) * fh] = total(rq, h, j)
        oo[h * fh : (h + 1) * fh, :] = total(ro, h)
        o1[:, h * hh : (h + 1) * hh] = total(r1, h)
        o2[h * hh : (h + 1) * hh, :] = total(r2, h)
    out[...] = yf[...]
    gin[...] = c[...].astype(f32) + gf[...].astype(f32)
    for j in range(3):
        oqb[j : j + 1, :] = bb[0, 1:2, j * 2 * fh : (j + 1) * 2 * fh]
    of1[...] = bb[0, 0:1, : 2 * hh]
    ogn[...] = bb[1, 2:4, :]
    orow[0:2, :] = bb[1, 4:6, :]
    orow[2:3, :] = bb[0, 6:7, :]
    orow[3:4, :] = bb[0, 6:7, :]


def whole_rows(
    block_input,
    cotangent,
    segments,
    positions,
    w_qkv,
    qkv_bias,
    w_out,
    w_fc1,
    fc1_bias,
    w_fc2,
    ln_gains,
    row_biases,
):
    shape = jax.ShapeDtypeStruct
    f32 = jnp.float32
    got = mega(
        block_input,
        cotangent,
        segments,
        positions,
        w_qkv,
        w_out,
        w_fc1,
        w_fc2,
        qkv_bias,
        fc1_bias.reshape(1, -1),
        ln_gains,
        row_biases,
    )
    outs = pl.pallas_call(
        functools.partial(final_kernel, (w_qkv.shape[2] // 2, w_fc1.shape[1] // 2)),
        out_shape=(
            shape(block_input.shape, block_input.dtype),
            shape(block_input.shape, f32),
            shape(w_qkv.shape, f32),
            shape(w_out.shape, f32),
            shape(w_fc1.shape, f32),
            shape(w_fc2.shape, f32),
            shape(qkv_bias.shape, f32),
            shape((1, fc1_bias.size), f32),
            shape(ln_gains.shape, f32),
            shape(row_biases.shape, f32),
        ),
        in_specs=[VM] * 8,
        out_specs=[VM] * 10,
        compiler_params=pltpu.CompilerParams(vmem_limit_bytes=63 * 2**20),
    )(*got, cotangent)
    return (*outs[:7], outs[7].reshape(fc1_bias.shape), *outs[8:])


def block(mesh, *args):
    seqs, rows, width = args[0].shape
    flat, hidden = args[4].shape[2], args[7].shape[1]
    sizes = mesh.shape
    if (
        (sizes["dp"], sizes["seq"], sizes["tensor"]) == (4, 2, 4)
        and flat == 4 * HD
        and seqs <= 2
        and rows == 128
        and width % 512 == 0
        and max(hidden, 3 * flat) <= width <= 1024
        and hidden % 512 == 0
    ):
        return whole_rows(*args)
    return shards(*args)


def solution(mesh):
    return jax.shard_map(
        functools.partial(block, mesh),
        mesh=mesh,
        in_specs=(
            P("dp", "seq", None),
            P("dp", "seq", None),
            P("dp", "seq"),
            P("dp", "seq"),
            P(None, ("dp", "seq"), "tensor"),
            P(None, "tensor"),
            P("tensor", ("dp", "seq")),
            P(("dp", "seq"), "tensor"),
            P("tensor"),
            P("tensor", ("dp", "seq")),
            P(),
            P(),
        ),
        out_specs=(
            P("dp", "seq", None),
            P("dp", "seq", None),
            P(None, ("dp", "seq"), "tensor"),
            P("tensor", ("dp", "seq")),
            P(("dp", "seq"), "tensor"),
            P("tensor", ("dp", "seq")),
            P(None, "tensor"),
            P("tensor"),
            P(),
            P(),
        ),
        check_vma=False,
    )
```

```python
import functools
import math

import jax
import jax.numpy as jnp
from jax import lax
from jax.experimental import pallas as pl
from jax.experimental.pallas import tpu as pltpu
from jax.sharding import PartitionSpec as P

HD = 64
ROT = 16


norm_eps = 1e-05
neg_big = -1e30
inv_root_two = 0.7071067811865476
inv_root_tau = 0.3989422804014327


def layer_norm(values, gain, shift):
    centred = values - jnp.mean(values, axis=-1, keepdims=True)
    inv_std = lax.rsqrt(jnp.mean(centred * centred, axis=-1, keepdims=True) + norm_eps)
    normed = centred * inv_std
    return (normed * gain + shift, normed, inv_std)


def norm_back(grad_out, normed, inv_std, gain):
    scaled = grad_out * gain
    centre = jnp.mean(scaled, axis=-1, keepdims=True)
    slope = jnp.mean(scaled * normed, axis=-1, keepdims=True)
    return inv_std * (scaled - centre - normed * slope)


def gelu_pair(pre_act):
    cumul = 0.5 * (1.0 + lax.erf(pre_act * inv_root_two))
    return (pre_act * cumul, cumul + pre_act * inv_root_tau * jnp.exp(-0.5 * pre_act * pre_act))


def rotary_tables(positions):
    half_rot = ROT // 2
    freqs = 10000.0 ** (-2.0 * jnp.arange(half_rot).astype(jnp.float32) / ROT)
    angles = positions.astype(jnp.float32)[..., None] * freqs
    cosine = jnp.cos(angles)
    sine = jnp.sin(angles)
    return (
        jnp.concatenate([cosine, cosine], -1)[..., None, :],
        jnp.concatenate([sine, sine], -1)[..., None, :],
    )


def rotate(tensor, cosine, sine):
    half_rot = ROT // 2
    head = tensor[..., :ROT]
    turned = jnp.concatenate([-head[..., half_rot:], head[..., :half_rot]], -1)
    return jnp.concatenate([head * cosine + turned * sine, tensor[..., ROT:]], -1)


def unrotate(grads, cosine, sine):
    half_rot = ROT // 2
    head = grads[..., :ROT]
    times_sine = head * sine
    back = jnp.concatenate([times_sine[..., half_rot:], -times_sine[..., :half_rot]], -1)
    return jnp.concatenate([head * cosine + back, grads[..., ROT:]], -1)


def gather_keys(keys_flat, values_in, segments):
    return (
        lax.all_gather(keys_flat, "seq", axis=1, tiled=True),
        lax.all_gather(values_in, "seq", axis=1, tiled=True),
        lax.all_gather(segments, "seq", axis=1, tiled=True),
    )


def pair_terms(
    query_blk,
    query_pos,
    query_seg,
    key_blk,
    value_blk,
    key_pos,
    key_seg,
    grad_blk,
    log_blk,
    delta_blk,
    scale,
):
    scores = (
        jnp.einsum("sqhd,skhd->shqk", query_blk, key_blk, preferred_element_type=jnp.float32)
        * scale
    )
    same_doc = query_seg[:, None, :, None] == key_seg[:, None, None, :]
    earlier = key_pos[None, None, None, :] <= query_pos[None, None, :, None]
    probs = jnp.where(same_doc & earlier, jnp.exp(scores - log_blk[..., None]), 0.0)
    grad_p = jnp.einsum("sqhd,skhd->shqk", grad_blk, value_blk, preferred_element_type=jnp.float32)
    grad_s = (probs * (grad_p - delta_blk[..., None])).astype(jnp.bfloat16)
    return (probs, grad_s)


def shards(
    block_input,
    cotangent,
    segments,
    positions,
    w_qkv,
    qkv_bias,
    w_out,
    w_fc1,
    fc1_bias,
    w_fc2,
    ln_gains,
    row_biases,
):
    seqs_here, rows_here, width = block_input.shape
    heads_here = w_qkv.shape[2] // HD
    flat_width = heads_here * HD
    scale = HD ** (-0.5)
    shape_heads = (seqs_here, rows_here, heads_here, HD)
    forward_weights = (
        lax.all_gather(w_qkv, ("dp", "seq"), axis=1, tiled=True),
        lax.all_gather(w_out, ("dp", "seq"), axis=1, tiled=True),
        lax.all_gather(w_fc1, ("dp", "seq"), axis=0, tiled=True),
        lax.all_gather(w_fc2, ("dp", "seq"), axis=1, tiled=True),
    )
    query_key_value_gathered, output_weight_gathered, up_weight_gathered, down_weight_gathered = (
        forward_weights
    )
    inputs_f = block_input.astype(jnp.float32)
    first_out, first_normed, first_inv = layer_norm(inputs_f, ln_gains[0], row_biases[0])
    second_out, second_normed, second_inv = layer_norm(inputs_f, ln_gains[1], row_biases[1])
    first_norm_input = first_out.astype(jnp.bfloat16)
    second_norm_input = second_out.astype(jnp.bfloat16)
    projected = (
        jnp.einsum(
            "bxf,kfh->kbxh",
            first_norm_input,
            query_key_value_gathered,
            preferred_element_type=jnp.float32,
        )
        + qkv_bias[:, None, None, :]
    )
    cosine, sine = rotary_tables(positions)
    queries = rotate(projected[0].reshape(shape_heads), cosine, sine).astype(jnp.bfloat16)
    keys_flat = (
        rotate(projected[1].reshape(shape_heads), cosine, sine)
        .astype(jnp.bfloat16)
        .reshape(seqs_here, rows_here, flat_width)
    )
    values_in = projected[2].astype(jnp.bfloat16)
    query_pos = lax.axis_index("seq") * rows_here + jnp.arange(rows_here)

    def block_scores(key_block, seg_block, key_start):
        count = key_block.shape[1]
        keys_heads = key_block.reshape(seqs_here, count, heads_here, HD)
        scores = (
            jnp.einsum("sqhd,skhd->shqk", queries, keys_heads, preferred_element_type=jnp.float32)
            * scale
        )
        key_pos = key_start + jnp.arange(count)
        same_doc = segments[:, None, :, None] == seg_block[:, None, None, :]
        earlier = key_pos[None, None, None, :] <= query_pos[None, None, :, None]
        return (scores, same_doc & earlier)

    start_state = (
        jnp.full((seqs_here, heads_here, rows_here), neg_big, jnp.float32),
        jnp.zeros((seqs_here, heads_here, rows_here), jnp.float32),
        jnp.zeros((seqs_here, heads_here, rows_here, HD), jnp.float32),
    )
    key_part = lax.all_gather(keys_flat, "seq", axis=1, tiled=True)
    value_part = lax.all_gather(values_in, "seq", axis=1, tiled=True)
    seg_part = lax.all_gather(segments, "seq", axis=1, tiled=True)
    count = key_part.shape[1]
    attend_block = math.gcd(count, 512)

    def step_block(block_idx, state):
        run_max, run_sum, accum = state
        offset = block_idx * attend_block
        key_block = lax.dynamic_slice_in_dim(key_part, offset, attend_block, 1)
        value_block = lax.dynamic_slice_in_dim(value_part, offset, attend_block, 1).reshape(
            seqs_here, attend_block, heads_here, HD
        )
        seg_block = lax.dynamic_slice_in_dim(seg_part, offset, attend_block, 1)
        scores, allowed = block_scores(key_block, seg_block, offset)
        new_max = jnp.maximum(run_max, jnp.max(jnp.where(allowed, scores, neg_big), axis=-1))
        factor = jnp.exp(run_max - new_max)
        expo = jnp.where(allowed, jnp.exp(scores - new_max[..., None]), 0.0)
        new_sum = run_sum * factor + jnp.sum(expo, axis=-1)
        update = jnp.einsum(
            "shqk,skhd->shqd",
            expo.astype(jnp.bfloat16),
            value_block,
            preferred_element_type=jnp.float32,
        )
        return (new_max, new_sum, accum * factor[..., None] + update)

    run_max, run_sum, accum = lax.fori_loop(0, count // attend_block, step_block, start_state)
    log_sum = run_max + jnp.log(run_sum)
    attention_context = (
        (accum / run_sum[..., None])
        .transpose(0, 2, 1, 3)
        .reshape(seqs_here, rows_here, flat_width)
        .astype(jnp.bfloat16)
    )
    pre_act = (
        jnp.einsum(
            "vrk,kt->vrt", second_norm_input, up_weight_gathered, preferred_element_type=jnp.float32
        )
        + fc1_bias
    )
    activ, gelu_slope = gelu_pair(pre_act)
    hidden_activation = activ.astype(jnp.bfloat16)
    partial_output_sum = jnp.einsum(
        "qhw,wj->qhj", attention_context, output_weight_gathered, preferred_element_type=jnp.float32
    )
    partial_output_sum = partial_output_sum + jnp.einsum(
        "qzg,gc->qzc", hidden_activation, down_weight_gathered, preferred_element_type=jnp.float32
    )
    branches = lax.psum(partial_output_sum.astype(jnp.bfloat16), "tensor").astype(jnp.float32)
    output = (inputs_f + branches + row_biases[2] + row_biases[3]).astype(jnp.bfloat16)
    query_key_value_backward, output_weight_backward, up_weight_backward, down_weight_backward = (
        lax.all_gather(w_qkv, ("dp", "seq"), axis=1, tiled=True),
        lax.all_gather(w_out, ("dp", "seq"), axis=1, tiled=True),
        lax.all_gather(w_fc1, ("dp", "seq"), axis=0, tiled=True),
        lax.all_gather(w_fc2, ("dp", "seq"), axis=1, tiled=True),
    )
    grad_f = cotangent.astype(jnp.float32)
    gradient_output_weight = jnp.einsum(
        "bxz,bxe->ze", attention_context, cotangent, preferred_element_type=jnp.float32
    )
    grad_context = jnp.einsum(
        "zpi,xi->zpx", cotangent, output_weight_backward, preferred_element_type=jnp.float32
    ).astype(jnp.bfloat16)
    gradient_down_weight = jnp.einsum(
        "tzi,tzo->io", hidden_activation, cotangent, preferred_element_type=jnp.float32
    )
    grad_pre = (
        jnp.einsum(
            "hvg,rg->hvr", cotangent, down_weight_backward, preferred_element_type=jnp.float32
        )
        * gelu_slope
    )
    gradient_hidden_input = grad_pre.astype(jnp.bfloat16)
    grad_fc1_w = jnp.einsum(
        "mxa,mxr->ar", second_norm_input, gradient_hidden_input, preferred_element_type=jnp.float32
    )
    grad_second = jnp.einsum(
        "ikq,uq->iku", gradient_hidden_input, up_weight_backward, preferred_element_type=jnp.float32
    )
    grad_ctx_heads = grad_context.reshape(shape_heads)
    delta = jnp.sum(
        grad_ctx_heads.astype(jnp.float32)
        * attention_context.reshape(shape_heads).astype(jnp.float32),
        axis=-1,
    ).transpose(0, 2, 1)
    key_all, value_all, seg_all = gather_keys(keys_flat, values_in, segments)
    total_len = key_all.shape[1]
    block = math.gcd(total_len, 512)

    def key_slices(offset):
        key_block = lax.dynamic_slice_in_dim(key_all, offset, block, 1).reshape(
            seqs_here, block, heads_here, HD
        )
        value_block = lax.dynamic_slice_in_dim(value_all, offset, block, 1).reshape(
            seqs_here, block, heads_here, HD
        )
        seg_block = lax.dynamic_slice_in_dim(seg_all, offset, block, 1)
        return (key_block, value_block, seg_block)

    def back_block(block_idx, state):
        grad_q, grad_key_all, grad_value_all = state
        offset = block_idx * block
        key_block, value_block, seg_block = key_slices(offset)
        probs, grad_s = pair_terms(
            queries,
            query_pos,
            segments,
            key_block,
            value_block,
            offset + jnp.arange(block),
            seg_block,
            grad_ctx_heads,
            log_sum,
            delta,
            scale,
        )
        grad_v = jnp.einsum(
            "shqk,sqhd->skhd",
            probs.astype(jnp.bfloat16),
            grad_ctx_heads,
            preferred_element_type=jnp.float32,
        )
        grad_q = (
            grad_q
            + jnp.einsum("shqk,skhd->sqhd", grad_s, key_block, preferred_element_type=jnp.float32)
            * scale
        )
        grad_k = (
            jnp.einsum("shqk,sqhd->skhd", grad_s, queries, preferred_element_type=jnp.float32)
            * scale
        )
        grad_key_all = lax.dynamic_update_slice_in_dim(
            grad_key_all, grad_k.reshape(seqs_here, block, flat_width), offset, 1
        )
        grad_value_all = lax.dynamic_update_slice_in_dim(
            grad_value_all, grad_v.reshape(seqs_here, block, flat_width), offset, 1
        )
        return (grad_q, grad_key_all, grad_value_all)

    back_start = (
        jnp.zeros(shape_heads, jnp.float32),
        jnp.zeros((seqs_here, total_len, flat_width), jnp.float32),
        jnp.zeros((seqs_here, total_len, flat_width), jnp.float32),
    )
    grad_q, grad_key_all, grad_value_all = lax.fori_loop(
        0, total_len // block, back_block, back_start
    )
    grad_key_here, grad_value_here = (
        lax.psum_scatter(
            grad_key_all.astype(jnp.bfloat16), "seq", scatter_dimension=1, tiled=True
        ).astype(jnp.float32),
        lax.psum_scatter(
            grad_value_all.astype(jnp.bfloat16), "seq", scatter_dimension=1, tiled=True
        ).astype(jnp.float32),
    )
    grad_proj = jnp.stack(
        [
            unrotate(grad_q, cosine, sine).reshape(seqs_here, rows_here, flat_width),
            unrotate(grad_key_here.reshape(shape_heads), cosine, sine).reshape(
                seqs_here, rows_here, flat_width
            ),
            grad_value_here,
        ]
    )
    grad_bias_qkv = jnp.sum(grad_proj, axis=(1, 2))
    gradient_projection_input = grad_proj.astype(jnp.bfloat16)
    grad_qkv_w = jnp.einsum(
        "ink,oint->okt",
        first_norm_input,
        gradient_projection_input,
        preferred_element_type=jnp.float32,
    )
    grad_first = jnp.einsum(
        "etbp,eop->tbo",
        gradient_projection_input,
        query_key_value_backward,
        preferred_element_type=jnp.float32,
    )
    grad_first, grad_second = (
        lax.psum(grad_first.astype(jnp.bfloat16), "tensor").astype(jnp.float32),
        lax.psum(grad_second.astype(jnp.bfloat16), "tensor").astype(jnp.float32),
    )
    grad_input = (
        grad_f
        + norm_back(grad_first, first_normed, first_inv, ln_gains[0])
        + norm_back(grad_second, second_normed, second_inv, ln_gains[1])
    )
    gain_terms = jnp.stack(
        [
            jnp.sum(grad_first * first_normed, axis=(0, 1)),
            jnp.sum(grad_second * second_normed, axis=(0, 1)),
        ]
    )
    row_terms = jnp.stack(
        [
            jnp.sum(grad_first, axis=(0, 1)),
            jnp.sum(grad_second, axis=(0, 1)),
            jnp.sum(grad_f, axis=(0, 1)),
            jnp.sum(grad_f, axis=(0, 1)),
        ]
    )
    bias_sums = lax.psum(
        (grad_bias_qkv, jnp.sum(grad_pre, axis=(0, 1)), gain_terms, row_terms), ("dp", "seq")
    )
    weight_sums = (
        lax.psum_scatter(grad_qkv_w, ("dp", "seq"), scatter_dimension=1, tiled=True),
        lax.psum_scatter(gradient_output_weight, ("dp", "seq"), scatter_dimension=1, tiled=True),
        lax.psum_scatter(grad_fc1_w, ("dp", "seq"), scatter_dimension=0, tiled=True),
        lax.psum_scatter(gradient_down_weight, ("dp", "seq"), scatter_dimension=1, tiled=True),
    )
    return (
        output,
        grad_input,
        weight_sums[0],
        weight_sums[1],
        weight_sums[2],
        weight_sums[3],
        bias_sums[0],
        bias_sums[1],
        bias_sums[2],
        bias_sums[3],
    )


MESH = pl.DeviceIdType.MESH
ANY = pl.BlockSpec(memory_space=pl.ANY)
VM = pl.BlockSpec(memory_space=pltpu.VMEM)
HBM = pl.BlockSpec(memory_space=pltpu.HBM)


def remote(src, dst, send, recv, where):
    return pltpu.make_async_remote_copy(
        src_ref=src, dst_ref=dst, send_sem=send, recv_sem=recv, device_id=where, device_id_type=MESH
    )


def pair_of(d):
    return d + 1 - 2 * lax.rem(d, 2)


def dot_nn(left, right):
    return lax.dot_general(left, right, (((1,), (0,)), ((), ())), preferred_element_type=jnp.float32)


def dot_nt(left, right):
    return lax.dot_general(left, right, (((1,), (1,)), ((), ())), preferred_element_type=jnp.float32)


def dot_tn(left, right):
    return lax.dot_general(left, right, (((0,), (0,)), ((), ())), preferred_element_type=jnp.float32)


def spread(left, right):
    return lax.dot_general(
        left,
        right,
        (((0,), (0,)), ((), ())),
        precision=lax.Precision.HIGHEST,
        preferred_element_type=jnp.float32,
    )


def loop(count, body):
    def step(i, carry):
        body(i)
        return carry

    lax.fori_loop(0, count, step, 0)


def at(index, size):
    return pl.ds(pl.multiple_of(index * size, size), size)


def mega_kernel(dims, *refs):
    f32, bf16 = jnp.float32, jnp.bfloat16
    seqs, rows, width, kr, oc, fh, hh = dims
    length = 2 * rows
    tokens = seqs * length
    heads = fh // HD
    scale = HD ** (-0.5)
    (x, c, seg, pos, wq, wo, w1, w2, *small) = refs[:12]
    R = refs[12:16]
    yfin, gfin, bout = refs[16:19]
    (xf, cf, segb, posb, GQ, GO, G1, G2) = refs[19:27]
    (first, second, nrm, tables, qs, ks, vs, gcs, ctx, gproj) = refs[27:37]
    (gacc, hid, slope, ghid) = refs[37:41]
    gW = refs[41:45]
    mid = refs[45:49]
    (part, sibp, chip, ein, xin, fw) = refs[49:55]
    (brow, bpair, bsum, bgot2, bsum2, bgot3) = refs[55:61]
    (s1, r1, s2, r2, ss, sr, sl) = refs[61:68]
    (ts, tr, tl) = refs[68:71]
    (ms, mr, ds_, dr, hs, hr, bs, br, bl) = refs[71:80]
    (ps, pr, es, er, xs, xr, fs, fr, fs2) = refs[80:89]
    (b1s, b1r, b2s, b2r, b3s, b3r) = refs[89:95]
    qb, f1b, gains, rowb = refs[95:99]
    small_sem = refs[99]
    nseq, nt, ndp = 2, 4, 4
    d, s, t = lax.axis_index("dp"), lax.axis_index("seq"), lax.axis_index("tensor")
    other = 1 - s
    near_x, near_y, corner = pair_of(d), lax.rem(d + 2, 4), 3 - d
    me = d * nseq + s
    side = t // 2
    mi, th = side, 1 - side
    inner = (t == 1) | (t == 2)
    end = (t == 0) | (t == 3)
    pt, facing = {"tensor": pair_of(t)}, {"tensor": 3 - t}

    small_copies = [
        pltpu.make_async_copy(src, dst, small_sem.at[j])
        for j, (src, dst) in enumerate(zip(small, (qb, f1b, gains, rowb)))
    ]
    local_x = pltpu.make_async_copy(x, xf.at[:, at(s, rows), :], tl.at[0])
    for copy in (local_x, *small_copies):
        copy.start()
    barrier = pltpu.get_barrier_semaphore()
    for peer in (near_x, near_y):
        for core in (0, 1):
            pl.semaphore_signal(
                barrier, inc=1, device_id={"dp": peer, "seq": core}, device_id_type=MESH
            )
    pl.semaphore_signal(barrier, inc=1, device_id={"seq": other}, device_id_type=MESH)
    pl.semaphore_signal(barrier, inc=1, device_id=pt, device_id_type=MESH)

    @pl.when(inner)
    def _():
        pl.semaphore_signal(barrier, inc=1, device_id=facing, device_id_type=MESH)
        pl.semaphore_wait(barrier, 7)

    @pl.when(end)
    def _():
        pl.semaphore_wait(barrier, 6)

    sends = []

    def go(copy):
        copy.start()
        sends.append(copy)
        return copy

    def source(a, half):
        return (
            lambda: wq.at[:, :, at(half, fh)],
            lambda: wo.at[at(half, fh), :],
            lambda: w1.at[:, at(half, hh)],
            lambda: w2.at[at(half, hh), :],
        )[a]()

    def place(bufs, a, index):
        return (
            lambda: bufs[0].at[:, at(index, kr), :],
            lambda: bufs[1].at[:, at(index, oc)],
            lambda: bufs[2].at[at(index, kr), :],
            lambda: bufs[3].at[:, at(index, oc)],
        )[a]()

    full = (GQ, GO, G1, G2)
    sibs, locals_ = {}, {}

    def hop1_copy(a, way, k):
        near, half = (near_x, near_y)[way], (s, other)[k]
        return remote(
            source(a, half),
            place(full, a, me),
            s1.at[a, way, k],
            r1.at[a, way, k],
            {"dp": near, "seq": half},
        )

    def start_hop1(a):
        for way in (0, 1):
            for k in (0, 1):
                hop1_copy(a, way, k).start()

    def start_near(a):
        sibs[a] = go(
            remote(source(a, other), place(full, a, me), ss.at[a], sr.at[a], {"seq": other})
        )
        locals_[a] = pltpu.make_async_copy(source(a, s), place(full, a, me), sl.at[a])
        locals_[a].start()

    def hop2_copy(a, way):
        view = place(full, a, (near_x * nseq, near_y * nseq + 1)[way])
        return remote(view, view, s2.at[a, way], r2.at[a, way], {"dp": (near_y, near_x)[way]})

    def start_hop2(a):
        for way in (0, 1):
            for k in (0, 1):
                hop1_copy(a, way, k).wait_recv()
        for way in (0, 1):
            hop2_copy(a, way).start()

    def wait_hop2(a):
        hop2_copy(a, 0).wait_recv()
        hop2_copy(a, 1).wait_recv()

    def wait_near(a):
        sibs[a].wait_recv()
        locals_[a].wait()

    def wait_all(a):
        wait_hop2(a)
        wait_near(a)

    mine = at(s, rows)
    start_hop1(0)
    start_hop1(1)
    tok = []
    for j, (src, dst) in enumerate(
        ((x, xf.at[:, mine, :]), (pos, posb.at[s]), (seg, segb.at[s]), (c, cf.at[:, mine, :]))
    ):
        copy = local_x
        if j > 0:
            copy = pltpu.make_async_copy(src, dst, tl.at[j])
            copy.start()
        tok.append((copy, go(remote(src, dst, ts.at[j], tr.at[j], {"seq": other}))))
    start_near(0)
    start_near(1)
    start_hop1(2)
    start_near(2)
    start_near(3)

    step = 32
    per = rows // step

    def norm_half(half):
        def body(i):
            b, at_row = i // per, pl.multiple_of(half * rows + lax.rem(i, per) * step, step)
            flat_row = pl.multiple_of(b * length + at_row, step)
            values = xf[b, pl.ds(at_row, step), :].astype(f32)
            one, normed, _ = layer_norm(values, gains[0:1, :], rowb[0:1, :])
            span = pl.ds(flat_row, step)
            nrm[span, :] = normed
            first[span, :] = one.astype(bf16)
            second[span, :] = (normed * gains[1:2, :] + rowb[1:2, :]).astype(bf16)

        loop(seqs * per, body)

    for copy in small_copies:
        copy.wait()
    tok[0][0].wait()
    norm_half(s)
    tok[0][1].wait_recv()
    norm_half(other)
    brow[...] = jnp.zeros_like(brow)
    start_hop2(0)
    start_hop2(1)
    for j in (1, 2, 3):
        tok[j][0].wait()
        tok[j][1].wait_recv()

    half_rot = ROT // 2
    lane = lax.broadcasted_iota(jnp.int32, (half_rot, fh), 1)
    lane = lax.rem(lane, HD)
    which = lax.broadcasted_iota(jnp.int32, (half_rot, fh), 0)
    low = (lane == which).astype(f32)
    high = (lane == which + half_rot).astype(f32)
    rest = (lane[0:1, :] >= ROT).astype(f32)
    power = lax.broadcasted_iota(jnp.int32, (half_rot, length), 0).astype(f32)
    freqs = jnp.exp(power * (-2.0 / ROT * math.log(10000.0)))
    for b in range(seqs):
        row = jnp.concatenate([posb[0, b : b + 1, :], posb[1, b : b + 1, :]], axis=1).astype(f32)
        angles = row * freqs
        sine = jnp.sin(angles)
        tables[0, at(b, length), :] = spread(jnp.cos(angles), low + high) + rest
        tables[1, at(b, length), :] = spread(sine, high)
        tables[2, at(b, length), :] = spread(sine, -low)

    start_hop2(2)
    start_hop1(3)
    wait_all(0)
    wait_all(1)

    def project(b):
        span = at(b, length)
        inputs = first[span, :]
        cosine, sin_a, sin_b = tables[0, span, :], tables[1, span, :], tables[2, span, :]

        def turn(v):
            up, down = pltpu.roll(v, half_rot, 1), pltpu.roll(v, fh - half_rot, 1)
            return v * cosine + up * sin_a + down * sin_b

        bias = lambda j: qb[j : j + 1, at(s, fh)]
        qs[span, :] = turn(dot_nn(inputs, GQ[0]) + bias(0)).astype(bf16)
        ks[span, :] = turn(dot_nn(inputs, GQ[1]) + bias(1)).astype(bf16)
        vs[span, :] = (dot_nn(inputs, GQ[2]) + bias(2)).astype(bf16)
        gcs[span, :] = dot_nt(cf[b], GO[...]).astype(bf16)

    loop(seqs, project)

    lane_of = lax.broadcasted_iota(jnp.int32, (1, fh), 1) // HD

    def attend(b):
        span = at(b, length)
        q, k, v, gc = qs[span, :], ks[span, :], vs[span, :], gcs[span, :]
        seg_rows = [
            jnp.concatenate(
                [segb[0, n : n + 1, :], segb[1, n : n + 1, :]], axis=1
            ).astype(f32)
            for n in range(seqs)
        ]
        seg_row = seg_rows[0]
        for n in range(1, seqs):
            seg_row = jnp.where(b == n, seg_rows[n], seg_row)
        pick = (lax.broadcasted_iota(jnp.int32, (8, length), 0) == 0).astype(f32)
        seg_col = spread(jnp.broadcast_to(seg_row, (8, length)), pick)
        q_pos = lax.broadcasted_iota(jnp.int32, (length, length), 0)
        k_pos = lax.broadcasted_iota(jnp.int32, (length, length), 1)
        allowed = (seg_col == seg_row) & (k_pos <= q_pos)
        out = []
        for h in range(heads):
            keep = (lane_of == h).astype(bf16)
            scores = dot_nt(q * keep, k) * scale
            row_max = jnp.max(jnp.where(allowed, scores, neg_big), axis=-1, keepdims=True)
            expo = jnp.where(allowed, jnp.exp(scores - row_max), 0.0)
            inv = 1.0 / jnp.sum(expo, axis=-1, keepdims=True)
            mixed = (dot_nn(expo.astype(bf16), v) * inv).astype(bf16) * keep
            gch = gc * keep
            delta = jnp.sum(gch.astype(f32) * mixed.astype(f32), axis=-1, keepdims=True)
            probs = expo * inv
            grad_s = (probs * (dot_nt(gch, v) - delta)).astype(bf16)
            terms = (
                mixed,
                dot_nn(grad_s, k * keep),
                dot_tn(grad_s, q * keep),
                dot_tn(probs.astype(bf16), gch),
            )
            out = [p + q_ for p, q_ in zip(out, terms)] if out else list(terms)
        ctx[span, :] = out[0]
        cosine, sin_a, sin_b = tables[0, span, :], tables[1, span, :], tables[2, span, :]

        def back(v):
            up, down = pltpu.roll(v, half_rot, 1), pltpu.roll(v, fh - half_rot, 1)
            return v * cosine - up * sin_a - down * sin_b

        for j, grad in enumerate((back(out[1] * scale), back(out[2] * scale), out[3])):
            gproj[j, span, :] = grad.astype(bf16)
            spot = pl.ds(pl.multiple_of(j * 2 * fh + s * fh, fh), fh)
            brow[1:2, spot] = brow[1:2, spot] + jnp.sum(grad, axis=0, keepdims=True)

    loop(seqs, attend)

    pairs, mids, lasts = {}, {}, {}

    def start_reduce(a):
        gone = lambda index: place(gW, a, index)
        mids[a, 0] = go(
            remote(gone(corner * 2), mid[a].at[0], ms.at[a, 0], mr.at[a, 0], {"dp": near_x})
        )
        mids[a, 1] = go(
            remote(gone(corner * 2 + 1), mid[a].at[1], ms.at[a, 1], mr.at[a, 1], {"dp": near_y})
        )
        go(
            remote(
                gone(near_x * 2), R[a].at[s, 1], ds_.at[a, 0], dr.at[a, s], {"dp": near_x, "seq": 0}
            )
        )
        go(
            remote(
                gone(near_y * 2 + 1),
                R[a].at[s, 1],
                ds_.at[a, 1],
                dr.at[a, s],
                {"dp": near_y, "seq": 1},
            )
        )
        pairs[a] = go(
            remote(gone(d * 2 + other), R[a].at[s, 0], bs.at[a], br.at[a], {"seq": other})
        )
        lasts[a] = pltpu.make_async_copy(gone(me), R[a].at[s, 0], bl.at[a])
        lasts[a].start()

    def second_reduce(a):
        for way, near, index in ((0, near_y, near_y * 2), (1, near_x, near_x * 2 + 1)):
            mids[a, way].wait_recv()
            mid[a][way] = (
                mid[a][way].astype(f32) + place(gW, a, index)[...].astype(f32)
            ).astype(bf16)
            go(
                remote(
                    mid[a].at[way],
                    R[a].at[s, 2],
                    hs.at[a, way],
                    hr.at[a, s],
                    {"dp": near, "seq": way},
                )
            )

    def finish_reduce(a):
        for h in (0, 1):
            remote(R[a].at[h, 1], R[a].at[h, 1], ds_.at[a, 0], dr.at[a, h], {"dp": near_x}).wait_recv()
            remote(R[a].at[h, 2], R[a].at[h, 2], hs.at[a, 0], hr.at[a, h], {"dp": near_x}).wait_recv()
        pairs[a].wait_recv()
        lasts[a].wait()

    big = 256
    wide = 512

    start_hop2(3)
    wait_all(2)

    def up(b):
        span = at(b, length)
        slope[span, :] = dot_nn(second[span, :], G1[...]) + f1b[:, at(s, hh)]

        def curve(i):
            part_of = pl.ds(pl.multiple_of(b * length + i * step, step), step)
            activ, incline = gelu_pair(slope[part_of, :])
            hid[part_of, :] = activ.astype(bf16)
            slope[part_of, :] = incline

        loop(length // step, curve)

    loop(seqs, up)

    wait_near(3)

    theirs_half = at(other, rows)

    def cross_tile(j, slot, b, cols):
        remote(
            part.at[j, b, theirs_half, cols],
            sibp.at[j, b, :, cols],
            ps.at[slot],
            pr.at[slot],
            {"seq": other},
        ).start()

    def crossed(j, slot, cols):
        return remote(
            part.at[j, :, theirs_half, cols],
            sibp.at[j, :, :, cols],
            ps.at[slot],
            pr.at[slot],
            {"seq": other},
        )

    group = 2 * oc
    groups = [at(chip_of, group) for chip_of in (d, near_x, near_y, corner)]
    early, late, every = pl.ds(0, 3 * group), pl.ds(0, group), pl.ds(0, width)

    def branches_of(b, cols, slot):
        span = at(b, length)
        total = dot_nn(ctx[span, :], GO[:, cols]) + dot_nn(hid[span, :], G2[:, cols])
        part[0, b, :, cols] = total.astype(bf16)
        cross_tile(0, slot, b, cols)

    def branch(b):
        for g in (0, 1, 2):
            branches_of(b, groups[g], 0)

    loop(seqs, branch)

    nc = 4
    cr = rows // nc
    fin = (yfin, gfin)
    whole_span = pl.ds(0, rows)

    def spans(j, ch):
        return (whole_span, groups[ch]) if j == 0 else (pl.ds(ch * cr, cr), every)

    def tokens_of(j, ch):
        if j == 0:
            return at(s, rows)
        return pl.ds(pl.multiple_of(s * rows + ch * cr, cr), cr)

    def to_inner(j, i, b, ch):
        view = (j, b, *spans(j, ch))
        return remote(chip.at[view], ein.at[view], es.at[j, i, ch], er.at[j, i, ch], pt)

    def over(j, ch):
        view = (j, *spans(j, ch))
        return remote(fw.at[view], xin.at[view], xs.at[j, ch], xr.at[j, ch], facing)

    def final(j, b, ch, send, slot, where):
        view = fin[j].at[(b, *spans(j, ch))]
        return remote(view, view, send, fr.at[j, slot, ch], where)

    def z_one(j, slot, cols, which):
        crossed(j, slot, cols).wait_recv()
        for i, b in ((0, th), (1, mi)):
            for ch in which:
                rs, ks_ = spans(j, ch)
                chip[j, b, rs, ks_] = (
                    part[j, b, tokens_of(j, ch), ks_].astype(f32) + sibp[j, b, rs, ks_].astype(f32)
                ).astype(bf16)

                @pl.when(end)
                def _():
                    to_inner(j, i, b, ch).start()

    def z_two(j, which):
        @pl.when(inner)
        def _():
            for ch in which:
                to_inner(j, 0, th, ch).wait_recv()
                rs, ks_ = spans(j, ch)
                fw[j, rs, ks_] = (
                    chip[j, th, rs, ks_].astype(f32) + ein[j, th, rs, ks_].astype(f32)
                ).astype(bf16)
                over(j, ch).start()

    def z_three(j, which):
        @pl.when(inner)
        def _():
            for ch in which:
                to_inner(j, 1, mi, ch).wait_recv()
                over(j, ch).wait_recv()
                rs, ks_ = spans(j, ch)
                total = (
                    chip[j, mi, rs, ks_].astype(f32)
                    + ein[j, mi, rs, ks_].astype(f32)
                    + xin[j, rs, ks_].astype(f32)
                )
                inputs = xf[mi, tokens_of(j, ch), ks_].astype(f32)
                if j == 0:
                    result = inputs + total + rowb[2:3, ks_] + rowb[3:4, ks_]
                else:
                    _, normed, inv_std = layer_norm(inputs, 1.0, 0.0)
                    result = norm_back(total, normed, inv_std, 1.0)
                fin[j][mi, rs, ks_] = result.astype(bf16)
                final(j, mi, ch, fs.at[j, 0, ch], 0, pt).start()
                final(j, mi, ch, fs.at[j, 1, ch], 1, facing).start()

    def z_four(j, which):
        @pl.when(inner)
        def _():
            for ch in which:
                final(j, th, ch, fs.at[j, 1, ch], 1, facing).wait_recv()
                final(j, th, ch, fs2.at[j, ch], 1, pt).start()

    def z_five(j):
        for slot, cols in (((0, early), (2, late)), ((1, every),))[j]:
            crossed(j, slot, cols).wait_send()
        for ch in range(nc):

            @pl.when(end)
            def _():
                for i, b in ((0, th), (1, mi)):
                    to_inner(j, i, b, ch).wait_send()
                final(j, mi, ch, fs.at[j, 0, ch], 0, pt).wait_recv()
                final(j, th, ch, fs2.at[j, ch], 1, pt).wait_recv()

            @pl.when(inner)
            def _():
                over(j, ch).wait_send()
                final(j, mi, ch, fs.at[j, 0, ch], 0, pt).wait_send()
                final(j, mi, ch, fs.at[j, 1, ch], 1, facing).wait_send()
                final(j, th, ch, fs2.at[j, ch], 1, pt).wait_send()


    tiles = width // wide


    def qkv_grad(i):
        rows_of = at(i, big)
        lhs = first[:, rows_of]
        for j in range(3):
            gW[0][j, rows_of, :] = dot_tn(lhs, gproj[j]).astype(bf16)

    loop(width // big, qkv_grad)

    z_one(0, 0, early, (0, 1, 2))

    def out_grad(i):
        cols = at(i, wide)
        gW[1][:, cols] = dot_tn(ctx[...], cf[:, :, cols].reshape(tokens, wide)).astype(bf16)

    loop(width // wide, out_grad)
    start_reduce(0)
    start_reduce(1)

    def first_back(i):
        b, n = i // tiles, lax.rem(i, tiles)
        span, cols = at(b, length), at(n, wide)
        grad = dot_nt(gproj[0, span, :], GQ[0, cols, :])
        for j in (1, 2):
            grad = grad + dot_nt(gproj[j, span, :], GQ[j, cols, :])
        gacc[span, cols] = grad * gains[0:1, cols]
        brow[2:3, cols] = brow[2:3, cols] + jnp.sum(grad * nrm[span, cols], axis=0, keepdims=True)
        brow[4:5, cols] = brow[4:5, cols] + jnp.sum(grad, axis=0, keepdims=True)

    loop(seqs * tiles, first_back)

    def down_grad(i):
        m, n = i // tiles, lax.rem(i, tiles)
        units, cols = at(m, big), at(n, wide)
        gW[3][units, cols] = dot_tn(
            hid[:, units], cf[:, :, cols].reshape(tokens, wide)
        ).astype(bf16)

    loop(hh // big * tiles, down_grad)

    start_reduce(3)
    ones = jnp.ones((16, rows), bf16)
    csum = dot_nn(ones, cf[0, mine, :])
    for b in range(1, seqs):
        csum = csum + dot_nn(ones, cf[b, mine, :])
    brow[6:7, :] = csum[0:1, :]
    wait_hop2(3)

    def late_branch(b):
        branches_of(b, groups[3], 2)

    loop(seqs, late_branch)

    def down_back(b):
        span = at(b, length)
        grad = dot_nt(cf[b], G2[...]) * slope[span, :]
        ghid[span, :] = grad.astype(bf16)
        spot = at(s, hh)
        brow[0:1, spot] = brow[0:1, spot] + jnp.sum(grad, axis=0, keepdims=True)

    loop(seqs, down_back)

    z_one(0, 2, late, (3,))
    z_two(0, (0, 1, 2))

    def second_back(i):
        b, n = i // tiles, lax.rem(i, tiles)
        span, cols = at(b, length), at(n, wide)
        grad = dot_nt(ghid[span, :], G1[cols, :])
        part[1, b, :, cols] = (gacc[span, cols] + grad * gains[1:2, cols]).astype(bf16)
        cross_tile(1, 1, b, cols)
        brow[3:4, cols] = brow[3:4, cols] + jnp.sum(grad * nrm[span, cols], axis=0, keepdims=True)
        brow[5:6, cols] = brow[5:6, cols] + jnp.sum(grad, axis=0, keepdims=True)

    loop(seqs * tiles, second_back)
    bpair_copy = go(remote(brow, bpair, b1s, b1r, {"seq": other}))

    bpair_copy.wait_recv()
    bsum[...] = brow[...] + bpair[...]

    def bias_hop(src, dst, where):
        return remote(
            bsum if src == 0 else bgot3.at[3], bgot3.at[dst], b3s.at[src], b3r.at[dst], where
        )

    @pl.when(end)
    def _():
        bias_hop(0, 0, pt).start()

    z_one(1, 1, every, range(nc))
    z_three(0, (0, 1, 2))
    z_two(0, (3,))

    def up_grad(i):
        rows_of = at(i, big)
        gW[2][rows_of, :] = dot_tn(second[:, rows_of], ghid[...]).astype(bf16)

    loop(width // big, up_grad)
    start_reduce(2)
    second_reduce(0)
    second_reduce(1)

    @pl.when(inner)
    def _():
        bias_hop(0, 0, pt).wait_recv()
        bgot3[3] = bsum[...] + bgot3[0]
        bias_hop(1, 1, facing).start()

    z_two(1, (0,))
    z_four(0, (0,))
    z_two(1, (1,))
    z_three(0, (3,))
    z_four(0, (1,))
    second_reduce(3)
    z_two(1, (2,))
    z_four(0, (2,))
    z_two(1, (3,))

    @pl.when(inner)
    def _():
        bias_hop(1, 1, facing).wait_recv()
        bias_hop(1, 1, facing).wait_send()
        bgot3[3] = bgot3[3] + bgot3[1]
        bias_hop(2, 2, pt).start()
        bsum2[2:6, :] = bgot3[3, 2:6, :]

    @pl.when(end)
    def _():
        bias_hop(2, 2, pt).wait_recv()
        bsum2[2:6, :] = bgot3[2, 2:6, :]

    bsum2[0:2, :] = bsum[0:2, :]
    bsum2[6:8, :] = bsum[6:8, :]
    x_send = go(remote(bsum2, bgot2.at[0], b2s.at[0], b2r.at[0], {"dp": near_x}))
    z_three(1, (0,))
    z_four(0, (3,))
    z_three(1, (1, 2))
    second_reduce(2)
    z_three(1, (3,))
    x_send.wait_recv()
    bgot2[2] = bsum2[...] + bgot2[0]
    y_send = go(remote(bgot2.at[2], bgot2.at[1], b2s.at[1], b2r.at[1], {"dp": near_y}))
    z_four(1, range(nc))
    y_send.wait_recv()
    bout[...] = bgot2[2] + bgot2[1]

    @pl.when(end)
    def _():
        bias_hop(0, 0, pt).wait_send()

    @pl.when(inner)
    def _():
        bias_hop(2, 2, pt).wait_send()

    z_five(0)
    z_five(1)
    for a in (0, 1, 3, 2):
        finish_reduce(a)
    for a in range(4):
        for way in (0, 1):
            for k in (0, 1):
                hop1_copy(a, way, k).wait_send()
            hop2_copy(a, way).wait_send()
    for copy in sends:
        copy.wait_send()


def mega(x, c, seg, pos, wq, wo, w1, w2, qb, f1b, gains, rowb):
    shape = jax.ShapeDtypeStruct
    f32, bf16 = jnp.float32, jnp.bfloat16
    seqs, rows, width = x.shape
    kr, oc, fh, hh = wq.shape[1], wo.shape[1], wq.shape[2] // 2, w1.shape[1] // 2
    length = rows * 2
    tokens = seqs * length
    nc = 4
    pieces = ((3, kr, fh), (fh, oc), (kr, hh), (hh, oc))
    fulls = ((3, width, fh), (fh, width), (width, hh), (hh, width))
    dma = pltpu.SemaphoreType.DMA
    vm = lambda dims, kind: pltpu.VMEM(dims, kind)
    bias = (8, width)
    scratch = [
        vm((seqs, length, width), bf16),
        vm((seqs, length, width), bf16),
        vm((2,) + seg.shape, jnp.int32),
        vm((2,) + pos.shape, jnp.int32),
        *[vm(f, bf16) for f in fulls],
        vm((tokens, width), bf16),
        vm((tokens, width), bf16),
        vm((tokens, width), f32),
        vm((3, tokens, fh), f32),
        *[vm((tokens, fh), bf16)] * 5,
        vm((3, tokens, fh), bf16),
        vm((tokens, width), f32),
        vm((tokens, hh), bf16),
        vm((tokens, hh), f32),
        vm((tokens, hh), bf16),
        *[vm(f, bf16) for f in fulls],
        *[vm((2,) + p, bf16) for p in pieces],
        vm((2, seqs, length, width), bf16),
        *[vm((2, seqs, rows, width), bf16)] * 3,
        *[vm((2, rows, width), bf16)] * 2,
        vm(bias, f32),
        vm(bias, f32),
        vm(bias, f32),
        vm((4,) + bias, f32),
        vm(bias, f32),
        vm((4,) + bias, f32),
        *[dma((4, 2, 2))] * 2,
        *[dma((4, 2))] * 2,
        *[dma((4,))] * 3,
        *[dma((4,))] * 3,
        *[dma((4, 2))] * 6,
        *[dma((4,))] * 3,
        *[dma((3,))] * 2,
        *[dma((2, 2, nc))] * 2,
        *[dma((2, nc))] * 2,
        *[dma((2, 2, nc))] * 2,
        dma((2, nc)),
        dma,
        dma,
        *[dma((4,))] * 4,
        *[vm(v.shape, f32) for v in (qb, f1b, gains, rowb)],
        dma((4,)),
    ]
    return pl.pallas_call(
        functools.partial(mega_kernel, (seqs, rows, width, kr, oc, fh, hh)),
        out_shape=(
            *[shape((2, 3) + p, bf16) for p in pieces],
            shape(x.shape, bf16),
            shape(x.shape, bf16),
            shape(bias, f32),
        ),
        in_specs=[HBM] * 12,
        out_specs=[HBM] * 4 + [VM] * 3,
        scratch_shapes=scratch,
        compiler_params=pltpu.CompilerParams(
            collective_id=0, has_side_effects=True, vmem_limit_bytes=63 * 2**20
        ),
    )(x, c, seg, pos, wq, wo, w1, w2, qb, f1b, gains, rowb)


def final_kernel(dims, *refs):
    f32 = jnp.float32
    fh, hh = dims
    rq, ro, r1, r2, yf, gf, bb, c = range(8)
    hbm_in, hbm_out = refs[:8], refs[8:18]
    vin, vout = refs[18:26], refs[26:36]
    in_sem, out_sem = refs[36:]
    out, gin, oq, oo, o1, o2, oqb, of1, ogn, orow = range(10)
    loads = [pltpu.make_async_copy(hbm_in[i], vin[i], in_sem.at[i]) for i in range(8)]
    straight = pltpu.make_async_copy(vin[yf], hbm_out[out], out_sem.at[out])
    stores = [pltpu.make_async_copy(vout[i], hbm_out[i], out_sem.at[i]) for i in range(10)]
    for i in (yf, r1, r2, c, gf, rq, ro, bb):
        loads[i].start()

    def total(ref, *index):
        return (
            ref[(index[0], 0) + index[1:]].astype(f32)
            + ref[(index[0], 1) + index[1:]].astype(f32)
            + ref[(index[0], 2) + index[1:]].astype(f32)
        )

    loads[yf].wait()
    straight.start()
    loads[r1].wait()
    for h in (0, 1):
        vout[o1][:, h * hh : (h + 1) * hh] = total(vin[r1], h)
    stores[o1].start()
    loads[r2].wait()
    for h in (0, 1):
        vout[o2][h * hh : (h + 1) * hh, :] = total(vin[r2], h)
    stores[o2].start()
    loads[c].wait()
    loads[gf].wait()
    vout[gin][...] = vin[c][...].astype(f32) + vin[gf][...].astype(f32)
    stores[gin].start()
    loads[rq].wait()
    for h in (0, 1):
        for j in range(3):
            vout[oq][j, :, h * fh : (h + 1) * fh] = total(vin[rq], h, j)
    stores[oq].start()
    loads[ro].wait()
    for h in (0, 1):
        vout[oo][h * fh : (h + 1) * fh, :] = total(vin[ro], h)
    stores[oo].start()
    loads[bb].wait()
    rows = vin[bb]
    for j in range(3):
        vout[oqb][j : j + 1, :] = rows[1:2, j * 2 * fh : (j + 1) * 2 * fh]
    vout[of1][...] = rows[0:1, : 2 * hh]
    vout[ogn][...] = rows[2:4, :]
    vout[orow][0:2, :] = rows[4:6, :]
    vout[orow][2:3, :] = rows[6:7, :]
    vout[orow][3:4, :] = rows[6:7, :]
    for i in (oqb, of1, ogn, orow):
        stores[i].start()
    straight.wait()
    for i in range(1, 10):
        stores[i].wait()


def whole_rows(
    block_input,
    cotangent,
    segments,
    positions,
    w_qkv,
    qkv_bias,
    w_out,
    w_fc1,
    fc1_bias,
    w_fc2,
    ln_gains,
    row_biases,
):
    shape = jax.ShapeDtypeStruct
    f32 = jnp.float32
    got = mega(
        block_input,
        cotangent,
        segments,
        positions,
        w_qkv,
        w_out,
        w_fc1,
        w_fc2,
        qkv_bias,
        fc1_bias.reshape(1, -1),
        ln_gains,
        row_biases,
    )
    shapes = (
        shape(block_input.shape, block_input.dtype),
        shape(block_input.shape, f32),
        shape(w_qkv.shape, f32),
        shape(w_out.shape, f32),
        shape(w_fc1.shape, f32),
        shape(w_fc2.shape, f32),
        shape(qkv_bias.shape, f32),
        shape((1, fc1_bias.size), f32),
        shape(ln_gains.shape, f32),
        shape(row_biases.shape, f32),
    )
    operands = (*got, cotangent)
    outs = pl.pallas_call(
        functools.partial(final_kernel, (w_qkv.shape[2] // 2, w_fc1.shape[1] // 2)),
        out_shape=shapes,
        in_specs=[HBM] * len(operands),
        out_specs=[HBM] * len(shapes),
        scratch_shapes=[
            *[pltpu.VMEM(v.shape, v.dtype) for v in operands],
            *[pltpu.VMEM(v.shape, v.dtype) for v in shapes],
            pltpu.SemaphoreType.DMA((len(operands),)),
            pltpu.SemaphoreType.DMA((len(shapes),)),
        ],
        compiler_params=pltpu.CompilerParams(vmem_limit_bytes=63 * 2**20),
    )(*operands)
    return (*outs[:7], outs[7].reshape(fc1_bias.shape), *outs[8:])


def block(mesh, *args):
    seqs, rows, width = args[0].shape
    flat, hidden = args[4].shape[2], args[7].shape[1]
    sizes = mesh.shape
    if (
        (sizes["dp"], sizes["seq"], sizes["tensor"]) == (4, 2, 4)
        and flat == 4 * HD
        and seqs <= 2
        and rows == 128
        and width % 512 == 0
        and max(hidden, 3 * flat) <= width <= 1024
        and hidden % 512 == 0
    ):
        return whole_rows(*args)
    return shards(*args)


def solution(mesh):
    return jax.shard_map(
        functools.partial(block, mesh),
        mesh=mesh,
        in_specs=(
            P("dp", "seq", None),
            P("dp", "seq", None),
            P("dp", "seq"),
            P("dp", "seq"),
            P(None, ("dp", "seq"), "tensor"),
            P(None, "tensor"),
            P("tensor", ("dp", "seq")),
            P(("dp", "seq"), "tensor"),
            P("tensor"),
            P("tensor", ("dp", "seq")),
            P(),
            P(),
        ),
        out_specs=(
            P("dp", "seq", None),
            P("dp", "seq", None),
            P(None, ("dp", "seq"), "tensor"),
            P("tensor", ("dp", "seq")),
            P(("dp", "seq"), "tensor"),
            P("tensor", ("dp", "seq")),
            P(None, "tensor"),
            P("tensor"),
            P(),
            P(),
        ),
        check_vma=False,
    )
```

```python
import functools
import math

import jax
import jax.numpy as jnp
from jax import lax
from jax.experimental import pallas as pl
from jax.experimental.pallas import tpu as pltpu
from jax.sharding import PartitionSpec as P

HD = 64
ROT = 16


norm_eps = 1e-05
neg_big = -1e30
inv_root_two = 0.7071067811865476
inv_root_tau = 0.3989422804014327


def layer_norm(values, gain, shift):
    centred = values - jnp.mean(values, axis=-1, keepdims=True)
    inv_std = lax.rsqrt(jnp.mean(centred * centred, axis=-1, keepdims=True) + norm_eps)
    normed = centred * inv_std
    return (normed * gain + shift, normed, inv_std)


def norm_back(grad_out, normed, inv_std, gain):
    scaled = grad_out * gain
    centre = jnp.mean(scaled, axis=-1, keepdims=True)
    slope = jnp.mean(scaled * normed, axis=-1, keepdims=True)
    return inv_std * (scaled - centre - normed * slope)


def gelu_pair(pre_act):
    cumul = 0.5 * (1.0 + lax.erf(pre_act * inv_root_two))
    return (pre_act * cumul, cumul + pre_act * inv_root_tau * jnp.exp(-0.5 * pre_act * pre_act))


def rotary_tables(positions):
    half_rot = ROT // 2
    freqs = 10000.0 ** (-2.0 * jnp.arange(half_rot).astype(jnp.float32) / ROT)
    angles = positions.astype(jnp.float32)[..., None] * freqs
    cosine = jnp.cos(angles)
    sine = jnp.sin(angles)
    return (
        jnp.concatenate([cosine, cosine], -1)[..., None, :],
        jnp.concatenate([sine, sine], -1)[..., None, :],
    )


def rotate(tensor, cosine, sine):
    half_rot = ROT // 2
    head = tensor[..., :ROT]
    turned = jnp.concatenate([-head[..., half_rot:], head[..., :half_rot]], -1)
    return jnp.concatenate([head * cosine + turned * sine, tensor[..., ROT:]], -1)


def unrotate(grads, cosine, sine):
    half_rot = ROT // 2
    head = grads[..., :ROT]
    times_sine = head * sine
    back = jnp.concatenate([times_sine[..., half_rot:], -times_sine[..., :half_rot]], -1)
    return jnp.concatenate([head * cosine + back, grads[..., ROT:]], -1)


def gather_keys(keys_flat, values_in, segments):
    return (
        lax.all_gather(keys_flat, "seq", axis=1, tiled=True),
        lax.all_gather(values_in, "seq", axis=1, tiled=True),
        lax.all_gather(segments, "seq", axis=1, tiled=True),
    )


def pair_terms(
    query_blk,
    query_pos,
    query_seg,
    key_blk,
    value_blk,
    key_pos,
    key_seg,
    grad_blk,
    log_blk,
    delta_blk,
    scale,
):
    scores = (
        jnp.einsum("sqhd,skhd->shqk", query_blk, key_blk, preferred_element_type=jnp.float32)
        * scale
    )
    same_doc = query_seg[:, None, :, None] == key_seg[:, None, None, :]
    earlier = key_pos[None, None, None, :] <= query_pos[None, None, :, None]
    probs = jnp.where(same_doc & earlier, jnp.exp(scores - log_blk[..., None]), 0.0)
    grad_p = jnp.einsum("sqhd,skhd->shqk", grad_blk, value_blk, preferred_element_type=jnp.float32)
    grad_s = (probs * (grad_p - delta_blk[..., None])).astype(jnp.bfloat16)
    return (probs, grad_s)


def shards(
    block_input,
    cotangent,
    segments,
    positions,
    w_qkv,
    qkv_bias,
    w_out,
    w_fc1,
    fc1_bias,
    w_fc2,
    ln_gains,
    row_biases,
):
    seqs_here, rows_here, width = block_input.shape
    heads_here = w_qkv.shape[2] // HD
    flat_width = heads_here * HD
    scale = HD ** (-0.5)
    shape_heads = (seqs_here, rows_here, heads_here, HD)
    forward_weights = (
        lax.all_gather(w_qkv, ("dp", "seq"), axis=1, tiled=True),
        lax.all_gather(w_out, ("dp", "seq"), axis=1, tiled=True),
        lax.all_gather(w_fc1, ("dp", "seq"), axis=0, tiled=True),
        lax.all_gather(w_fc2, ("dp", "seq"), axis=1, tiled=True),
    )
    query_key_value_gathered, output_weight_gathered, up_weight_gathered, down_weight_gathered = (
        forward_weights
    )
    inputs_f = block_input.astype(jnp.float32)
    first_out, first_normed, first_inv = layer_norm(inputs_f, ln_gains[0], row_biases[0])
    second_out, second_normed, second_inv = layer_norm(inputs_f, ln_gains[1], row_biases[1])
    first_norm_input = first_out.astype(jnp.bfloat16)
    second_norm_input = second_out.astype(jnp.bfloat16)
    projected = (
        jnp.einsum(
            "bxf,kfh->kbxh",
            first_norm_input,
            query_key_value_gathered,
            preferred_element_type=jnp.float32,
        )
        + qkv_bias[:, None, None, :]
    )
    cosine, sine = rotary_tables(positions)
    queries = rotate(projected[0].reshape(shape_heads), cosine, sine).astype(jnp.bfloat16)
    keys_flat = (
        rotate(projected[1].reshape(shape_heads), cosine, sine)
        .astype(jnp.bfloat16)
        .reshape(seqs_here, rows_here, flat_width)
    )
    values_in = projected[2].astype(jnp.bfloat16)
    query_pos = lax.axis_index("seq") * rows_here + jnp.arange(rows_here)

    def block_scores(key_block, seg_block, key_start):
        count = key_block.shape[1]
        keys_heads = key_block.reshape(seqs_here, count, heads_here, HD)
        scores = (
            jnp.einsum("sqhd,skhd->shqk", queries, keys_heads, preferred_element_type=jnp.float32)
            * scale
        )
        key_pos = key_start + jnp.arange(count)
        same_doc = segments[:, None, :, None] == seg_block[:, None, None, :]
        earlier = key_pos[None, None, None, :] <= query_pos[None, None, :, None]
        return (scores, same_doc & earlier)

    start_state = (
        jnp.full((seqs_here, heads_here, rows_here), neg_big, jnp.float32),
        jnp.zeros((seqs_here, heads_here, rows_here), jnp.float32),
        jnp.zeros((seqs_here, heads_here, rows_here, HD), jnp.float32),
    )
    key_part = lax.all_gather(keys_flat, "seq", axis=1, tiled=True)
    value_part = lax.all_gather(values_in, "seq", axis=1, tiled=True)
    seg_part = lax.all_gather(segments, "seq", axis=1, tiled=True)
    count = key_part.shape[1]
    attend_block = math.gcd(count, 512)

    def step_block(block_idx, state):
        run_max, run_sum, accum = state
        offset = block_idx * attend_block
        key_block = lax.dynamic_slice_in_dim(key_part, offset, attend_block, 1)
        value_block = lax.dynamic_slice_in_dim(value_part, offset, attend_block, 1).reshape(
            seqs_here, attend_block, heads_here, HD
        )
        seg_block = lax.dynamic_slice_in_dim(seg_part, offset, attend_block, 1)
        scores, allowed = block_scores(key_block, seg_block, offset)
        new_max = jnp.maximum(run_max, jnp.max(jnp.where(allowed, scores, neg_big), axis=-1))
        factor = jnp.exp(run_max - new_max)
        expo = jnp.where(allowed, jnp.exp(scores - new_max[..., None]), 0.0)
        new_sum = run_sum * factor + jnp.sum(expo, axis=-1)
        update = jnp.einsum(
            "shqk,skhd->shqd",
            expo.astype(jnp.bfloat16),
            value_block,
            preferred_element_type=jnp.float32,
        )
        return (new_max, new_sum, accum * factor[..., None] + update)

    run_max, run_sum, accum = lax.fori_loop(0, count // attend_block, step_block, start_state)
    log_sum = run_max + jnp.log(run_sum)
    attention_context = (
        (accum / run_sum[..., None])
        .transpose(0, 2, 1, 3)
        .reshape(seqs_here, rows_here, flat_width)
        .astype(jnp.bfloat16)
    )
    pre_act = (
        jnp.einsum(
            "vrk,kt->vrt", second_norm_input, up_weight_gathered, preferred_element_type=jnp.float32
        )
        + fc1_bias
    )
    activ, gelu_slope = gelu_pair(pre_act)
    hidden_activation = activ.astype(jnp.bfloat16)
    partial_output_sum = jnp.einsum(
        "qhw,wj->qhj", attention_context, output_weight_gathered, preferred_element_type=jnp.float32
    )
    partial_output_sum = partial_output_sum + jnp.einsum(
        "qzg,gc->qzc", hidden_activation, down_weight_gathered, preferred_element_type=jnp.float32
    )
    branches = lax.psum(partial_output_sum.astype(jnp.bfloat16), "tensor").astype(jnp.float32)
    output = (inputs_f + branches + row_biases[2] + row_biases[3]).astype(jnp.bfloat16)
    query_key_value_backward, output_weight_backward, up_weight_backward, down_weight_backward = (
        lax.all_gather(w_qkv, ("dp", "seq"), axis=1, tiled=True),
        lax.all_gather(w_out, ("dp", "seq"), axis=1, tiled=True),
        lax.all_gather(w_fc1, ("dp", "seq"), axis=0, tiled=True),
        lax.all_gather(w_fc2, ("dp", "seq"), axis=1, tiled=True),
    )
    grad_f = cotangent.astype(jnp.float32)
    gradient_output_weight = jnp.einsum(
        "bxz,bxe->ze", attention_context, cotangent, preferred_element_type=jnp.float32
    )
    grad_context = jnp.einsum(
        "zpi,xi->zpx", cotangent, output_weight_backward, preferred_element_type=jnp.float32
    ).astype(jnp.bfloat16)
    gradient_down_weight = jnp.einsum(
        "tzi,tzo->io", hidden_activation, cotangent, preferred_element_type=jnp.float32
    )
    grad_pre = (
        jnp.einsum(
            "hvg,rg->hvr", cotangent, down_weight_backward, preferred_element_type=jnp.float32
        )
        * gelu_slope
    )
    gradient_hidden_input = grad_pre.astype(jnp.bfloat16)
    grad_fc1_w = jnp.einsum(
        "mxa,mxr->ar", second_norm_input, gradient_hidden_input, preferred_element_type=jnp.float32
    )
    grad_second = jnp.einsum(
        "ikq,uq->iku", gradient_hidden_input, up_weight_backward, preferred_element_type=jnp.float32
    )
    grad_ctx_heads = grad_context.reshape(shape_heads)
    delta = jnp.sum(
        grad_ctx_heads.astype(jnp.float32)
        * attention_context.reshape(shape_heads).astype(jnp.float32),
        axis=-1,
    ).transpose(0, 2, 1)
    key_all, value_all, seg_all = gather_keys(keys_flat, values_in, segments)
    total_len = key_all.shape[1]
    block = math.gcd(total_len, 512)

    def key_slices(offset):
        key_block = lax.dynamic_slice_in_dim(key_all, offset, block, 1).reshape(
            seqs_here, block, heads_here, HD
        )
        value_block = lax.dynamic_slice_in_dim(value_all, offset, block, 1).reshape(
            seqs_here, block, heads_here, HD
        )
        seg_block = lax.dynamic_slice_in_dim(seg_all, offset, block, 1)
        return (key_block, value_block, seg_block)

    def back_block(block_idx, state):
        grad_q, grad_key_all, grad_value_all = state
        offset = block_idx * block
        key_block, value_block, seg_block = key_slices(offset)
        probs, grad_s = pair_terms(
            queries,
            query_pos,
            segments,
            key_block,
            value_block,
            offset + jnp.arange(block),
            seg_block,
            grad_ctx_heads,
            log_sum,
            delta,
            scale,
        )
        grad_v = jnp.einsum(
            "shqk,sqhd->skhd",
            probs.astype(jnp.bfloat16),
            grad_ctx_heads,
            preferred_element_type=jnp.float32,
        )
        grad_q = (
            grad_q
            + jnp.einsum("shqk,skhd->sqhd", grad_s, key_block, preferred_element_type=jnp.float32)
            * scale
        )
        grad_k = (
            jnp.einsum("shqk,sqhd->skhd", grad_s, queries, preferred_element_type=jnp.float32)
            * scale
        )
        grad_key_all = lax.dynamic_update_slice_in_dim(
            grad_key_all, grad_k.reshape(seqs_here, block, flat_width), offset, 1
        )
        grad_value_all = lax.dynamic_update_slice_in_dim(
            grad_value_all, grad_v.reshape(seqs_here, block, flat_width), offset, 1
        )
        return (grad_q, grad_key_all, grad_value_all)

    back_start = (
        jnp.zeros(shape_heads, jnp.float32),
        jnp.zeros((seqs_here, total_len, flat_width), jnp.float32),
        jnp.zeros((seqs_here, total_len, flat_width), jnp.float32),
    )
    grad_q, grad_key_all, grad_value_all = lax.fori_loop(
        0, total_len // block, back_block, back_start
    )
    grad_key_here, grad_value_here = (
        lax.psum_scatter(
            grad_key_all.astype(jnp.bfloat16), "seq", scatter_dimension=1, tiled=True
        ).astype(jnp.float32),
        lax.psum_scatter(
            grad_value_all.astype(jnp.bfloat16), "seq", scatter_dimension=1, tiled=True
        ).astype(jnp.float32),
    )
    grad_proj = jnp.stack(
        [
            unrotate(grad_q, cosine, sine).reshape(seqs_here, rows_here, flat_width),
            unrotate(grad_key_here.reshape(shape_heads), cosine, sine).reshape(
                seqs_here, rows_here, flat_width
            ),
            grad_value_here,
        ]
    )
    grad_bias_qkv = jnp.sum(grad_proj, axis=(1, 2))
    gradient_projection_input = grad_proj.astype(jnp.bfloat16)
    grad_qkv_w = jnp.einsum(
        "ink,oint->okt",
        first_norm_input,
        gradient_projection_input,
        preferred_element_type=jnp.float32,
    )
    grad_first = jnp.einsum(
        "etbp,eop->tbo",
        gradient_projection_input,
        query_key_value_backward,
        preferred_element_type=jnp.float32,
    )
    grad_first, grad_second = (
        lax.psum(grad_first.astype(jnp.bfloat16), "tensor").astype(jnp.float32),
        lax.psum(grad_second.astype(jnp.bfloat16), "tensor").astype(jnp.float32),
    )
    grad_input = (
        grad_f
        + norm_back(grad_first, first_normed, first_inv, ln_gains[0])
        + norm_back(grad_second, second_normed, second_inv, ln_gains[1])
    )
    gain_terms = jnp.stack(
        [
            jnp.sum(grad_first * first_normed, axis=(0, 1)),
            jnp.sum(grad_second * second_normed, axis=(0, 1)),
        ]
    )
    row_terms = jnp.stack(
        [
            jnp.sum(grad_first, axis=(0, 1)),
            jnp.sum(grad_second, axis=(0, 1)),
            jnp.sum(grad_f, axis=(0, 1)),
            jnp.sum(grad_f, axis=(0, 1)),
        ]
    )
    bias_sums = lax.psum(
        (grad_bias_qkv, jnp.sum(grad_pre, axis=(0, 1)), gain_terms, row_terms), ("dp", "seq")
    )
    weight_sums = (
        lax.psum_scatter(grad_qkv_w, ("dp", "seq"), scatter_dimension=1, tiled=True),
        lax.psum_scatter(gradient_output_weight, ("dp", "seq"), scatter_dimension=1, tiled=True),
        lax.psum_scatter(grad_fc1_w, ("dp", "seq"), scatter_dimension=0, tiled=True),
        lax.psum_scatter(gradient_down_weight, ("dp", "seq"), scatter_dimension=1, tiled=True),
    )
    return (
        output,
        grad_input,
        weight_sums[0],
        weight_sums[1],
        weight_sums[2],
        weight_sums[3],
        bias_sums[0],
        bias_sums[1],
        bias_sums[2],
        bias_sums[3],
    )


MESH = pl.DeviceIdType.MESH
ANY = pl.BlockSpec(memory_space=pl.ANY)
VM = pl.BlockSpec(memory_space=pltpu.VMEM)
HBM = pl.BlockSpec(memory_space=pltpu.HBM)


def remote(src, dst, send, recv, where):
    return pltpu.make_async_remote_copy(
        src_ref=src, dst_ref=dst, send_sem=send, recv_sem=recv, device_id=where, device_id_type=MESH
    )


def pair_of(d):
    return d + 1 - 2 * lax.rem(d, 2)


def dot_nn(left, right):
    return lax.dot_general(left, right, (((1,), (0,)), ((), ())), preferred_element_type=jnp.float32)


def dot_nt(left, right):
    return lax.dot_general(left, right, (((1,), (1,)), ((), ())), preferred_element_type=jnp.float32)


def dot_tn(left, right):
    return lax.dot_general(left, right, (((0,), (0,)), ((), ())), preferred_element_type=jnp.float32)


def spread(left, right):
    return lax.dot_general(
        left,
        right,
        (((0,), (0,)), ((), ())),
        precision=lax.Precision.HIGHEST,
        preferred_element_type=jnp.float32,
    )


def loop(count, body):
    def step(i, carry):
        body(i)
        return carry

    lax.fori_loop(0, count, step, 0)


def at(index, size):
    return pl.ds(pl.multiple_of(index * size, size), size)


def mega_kernel(dims, *refs):
    f32, bf16 = jnp.float32, jnp.bfloat16
    seqs, rows, width, kr, oc, fh, hh = dims
    length = 2 * rows
    tokens = seqs * length
    heads = fh // HD
    scale = HD ** (-0.5)
    (x, c, seg, pos, wq, wo, w1, w2, *small) = refs[:12]
    R = refs[12:16]
    yfin, gfin, bout = refs[16:19]
    (xf, cf, segb, posb, GQ, GO, G1, G2) = refs[19:27]
    (first, second, nrm, tables, qs, ks, vs, gcs, ctx, gproj) = refs[27:37]
    (gacc, hid, slope, ghid) = refs[37:41]
    gW = refs[41:45]
    mid = refs[45:49]
    (part, sibp, chip, ein, xin, fw) = refs[49:55]
    (brow, bpair, bsum, bgot2, bsum2, bgot3) = refs[55:61]
    (s1, r1, s2, r2, ss, sr, sl) = refs[61:68]
    (ts, tr, tl) = refs[68:71]
    (ms, mr, ds_, dr, hs, hr, bs, br, bl) = refs[71:80]
    (ps, pr, es, er, xs, xr, fs, fr, fs2) = refs[80:89]
    (b1s, b1r, b2s, b2r, b3s, b3r) = refs[89:95]
    qb, f1b, gains, rowb = refs[95:99]
    small_sem = refs[99]
    nseq, nt, ndp = 2, 4, 4
    d, s, t = lax.axis_index("dp"), lax.axis_index("seq"), lax.axis_index("tensor")
    other = 1 - s
    near_x, near_y, corner = pair_of(d), lax.rem(d + 2, 4), 3 - d
    me = d * nseq + s
    side = t // 2
    mi, th = side, 1 - side
    inner = (t == 1) | (t == 2)
    end = (t == 0) | (t == 3)
    pt, facing = {"tensor": pair_of(t)}, {"tensor": 3 - t}

    small_copies = [
        pltpu.make_async_copy(src, dst, small_sem.at[j])
        for j, (src, dst) in enumerate(zip(small, (qb, f1b, gains, rowb)))
    ]
    local_x = pltpu.make_async_copy(x, xf.at[:, at(s, rows), :], tl.at[0])
    for copy in (local_x, *small_copies):
        copy.start()
    barrier = pltpu.get_barrier_semaphore()
    for peer in (near_x, near_y):
        for core in (0, 1):
            pl.semaphore_signal(
                barrier, inc=1, device_id={"dp": peer, "seq": core}, device_id_type=MESH
            )
    pl.semaphore_signal(barrier, inc=1, device_id={"seq": other}, device_id_type=MESH)
    pl.semaphore_signal(barrier, inc=1, device_id=pt, device_id_type=MESH)

    @pl.when(inner)
    def _():
        pl.semaphore_signal(barrier, inc=1, device_id=facing, device_id_type=MESH)
        pl.semaphore_wait(barrier, 7)

    @pl.when(end)
    def _():
        pl.semaphore_wait(barrier, 6)

    sends = []

    def go(copy):
        copy.start()
        sends.append(copy)
        return copy

    def source(a, half):
        return (
            lambda: wq.at[:, :, at(half, fh)],
            lambda: wo.at[at(half, fh), :],
            lambda: w1.at[:, at(half, hh)],
            lambda: w2.at[at(half, hh), :],
        )[a]()

    def place(bufs, a, index):
        return (
            lambda: bufs[0].at[:, at(index, kr), :],
            lambda: bufs[1].at[:, at(index, oc)],
            lambda: bufs[2].at[at(index, kr), :],
            lambda: bufs[3].at[:, at(index, oc)],
        )[a]()

    full = (GQ, GO, G1, G2)
    sibs, locals_ = {}, {}

    def hop1_copy(a, way, k):
        near, half = (near_x, near_y)[way], (s, other)[k]
        return remote(
            source(a, half),
            place(full, a, me),
            s1.at[a, way, k],
            r1.at[a, way, k],
            {"dp": near, "seq": half},
        )

    def start_hop1(a):
        for way in (0, 1):
            for k in (0, 1):
                hop1_copy(a, way, k).start()

    def start_near(a):
        sibs[a] = go(
            remote(source(a, other), place(full, a, me), ss.at[a], sr.at[a], {"seq": other})
        )
        locals_[a] = pltpu.make_async_copy(source(a, s), place(full, a, me), sl.at[a])
        locals_[a].start()

    def hop2_copy(a, way):
        view = place(full, a, (near_x * nseq, near_y * nseq + 1)[way])
        return remote(view, view, s2.at[a, way], r2.at[a, way], {"dp": (near_y, near_x)[way]})

    def start_hop2(a):
        for way in (0, 1):
            for k in (0, 1):
                hop1_copy(a, way, k).wait_recv()
        for way in (0, 1):
            hop2_copy(a, way).start()

    def wait_hop2(a):
        hop2_copy(a, 0).wait_recv()
        hop2_copy(a, 1).wait_recv()

    def wait_near(a):
        sibs[a].wait_recv()
        locals_[a].wait()

    def wait_all(a):
        wait_hop2(a)
        wait_near(a)

    mine = at(s, rows)
    start_hop1(0)
    start_hop1(1)
    tok = []
    for j, (src, dst) in enumerate(
        ((x, xf.at[:, mine, :]), (pos, posb.at[s]), (seg, segb.at[s]), (c, cf.at[:, mine, :]))
    ):
        copy = local_x
        if j > 0:
            copy = pltpu.make_async_copy(src, dst, tl.at[j])
            copy.start()
        tok.append((copy, go(remote(src, dst, ts.at[j], tr.at[j], {"seq": other}))))
    start_near(0)
    start_near(1)
    start_hop1(2)
    start_near(2)
    start_near(3)

    step = 32
    per = rows // step

    def norm_half(half):
        def body(i):
            b, at_row = i // per, pl.multiple_of(half * rows + lax.rem(i, per) * step, step)
            flat_row = pl.multiple_of(b * length + at_row, step)
            values = xf[b, pl.ds(at_row, step), :].astype(f32)
            one, normed, _ = layer_norm(values, gains[0:1, :], rowb[0:1, :])
            span = pl.ds(flat_row, step)
            nrm[span, :] = normed
            first[span, :] = one.astype(bf16)
            second[span, :] = (normed * gains[1:2, :] + rowb[1:2, :]).astype(bf16)

        loop(seqs * per, body)

    for copy in small_copies:
        copy.wait()
    tok[0][0].wait()
    norm_half(s)
    tok[0][1].wait_recv()
    norm_half(other)
    brow[...] = jnp.zeros_like(brow)
    start_hop2(0)
    start_hop2(1)
    for j in (1, 2, 3):
        tok[j][0].wait()
        tok[j][1].wait_recv()

    half_rot = ROT // 2
    lane = lax.broadcasted_iota(jnp.int32, (half_rot, fh), 1)
    lane = lax.rem(lane, HD)
    which = lax.broadcasted_iota(jnp.int32, (half_rot, fh), 0)
    low = (lane == which).astype(f32)
    high = (lane == which + half_rot).astype(f32)
    rest = (lane[0:1, :] >= ROT).astype(f32)
    power = lax.broadcasted_iota(jnp.int32, (half_rot, length), 0).astype(f32)
    freqs = jnp.exp(power * (-2.0 / ROT * math.log(10000.0)))
    for b in range(seqs):
        row = jnp.concatenate([posb[0, b : b + 1, :], posb[1, b : b + 1, :]], axis=1).astype(f32)
        angles = row * freqs
        sine = jnp.sin(angles)
        tables[0, at(b, length), :] = spread(jnp.cos(angles), low + high) + rest
        tables[1, at(b, length), :] = spread(sine, high)
        tables[2, at(b, length), :] = spread(sine, -low)

    start_hop2(2)
    start_hop1(3)
    wait_all(0)
    wait_all(1)

    def project(b):
        span = at(b, length)
        inputs = first[span, :]
        cosine, sin_a, sin_b = tables[0, span, :], tables[1, span, :], tables[2, span, :]

        def turn(v):
            up, down = pltpu.roll(v, half_rot, 1), pltpu.roll(v, fh - half_rot, 1)
            return v * cosine + up * sin_a + down * sin_b

        bias = lambda j: qb[j : j + 1, at(s, fh)]
        three = dot_nn(inputs, jnp.concatenate([GQ[0], GQ[1], GQ[2]], axis=1))
        qs[span, :] = turn(three[:, :fh] + bias(0)).astype(bf16)
        ks[span, :] = turn(three[:, fh : 2 * fh] + bias(1)).astype(bf16)
        vs[span, :] = (three[:, 2 * fh :] + bias(2)).astype(bf16)
        gcs[span, :] = dot_nt(cf[b], GO[...]).astype(bf16)

    loop(seqs, project)

    lane_of = lax.broadcasted_iota(jnp.int32, (1, fh), 1) // HD

    def attend(b):
        span = at(b, length)
        q, k, v, gc = qs[span, :], ks[span, :], vs[span, :], gcs[span, :]
        seg_rows = [
            jnp.concatenate(
                [segb[0, n : n + 1, :], segb[1, n : n + 1, :]], axis=1
            ).astype(f32)
            for n in range(seqs)
        ]
        seg_row = seg_rows[0]
        for n in range(1, seqs):
            seg_row = jnp.where(b == n, seg_rows[n], seg_row)
        pick = (lax.broadcasted_iota(jnp.int32, (8, length), 0) == 0).astype(f32)
        seg_col = spread(jnp.broadcast_to(seg_row, (8, length)), pick)
        q_pos = lax.broadcasted_iota(jnp.int32, (length, length), 0)
        k_pos = lax.broadcasted_iota(jnp.int32, (length, length), 1)
        allowed = (seg_col == seg_row) & (k_pos <= q_pos)
        out = []
        for h in range(heads):
            keep = (lane_of == h).astype(bf16)
            scores = dot_nt(q * keep, k) * scale
            row_max = jnp.max(jnp.where(allowed, scores, neg_big), axis=-1, keepdims=True)
            expo = jnp.where(allowed, jnp.exp(scores - row_max), 0.0)
            inv = 1.0 / jnp.sum(expo, axis=-1, keepdims=True)
            mixed = (dot_nn(expo.astype(bf16), v) * inv).astype(bf16) * keep
            gch = gc * keep
            delta = jnp.sum(gch.astype(f32) * mixed.astype(f32), axis=-1, keepdims=True)
            probs = expo * inv
            grad_s = (probs * (dot_nt(gch, v) - delta)).astype(bf16)
            terms = (
                mixed,
                dot_nn(grad_s, k * keep),
                dot_tn(grad_s, q * keep),
                dot_tn(probs.astype(bf16), gch),
            )
            out = [p + q_ for p, q_ in zip(out, terms)] if out else list(terms)
        ctx[span, :] = out[0]
        cosine, sin_a, sin_b = tables[0, span, :], tables[1, span, :], tables[2, span, :]

        def back(v):
            up, down = pltpu.roll(v, half_rot, 1), pltpu.roll(v, fh - half_rot, 1)
            return v * cosine - up * sin_a - down * sin_b

        for j, grad in enumerate((back(out[1] * scale), back(out[2] * scale), out[3])):
            gproj[j, span, :] = grad.astype(bf16)
            spot = pl.ds(pl.multiple_of(j * 2 * fh + s * fh, fh), fh)
            brow[1:2, spot] = brow[1:2, spot] + jnp.sum(grad, axis=0, keepdims=True)

    loop(seqs, attend)

    pairs, mids, lasts = {}, {}, {}

    def start_reduce(a):
        gone = lambda index: place(gW, a, index)
        mids[a, 0] = go(
            remote(gone(corner * 2), mid[a].at[0], ms.at[a, 0], mr.at[a, 0], {"dp": near_x})
        )
        mids[a, 1] = go(
            remote(gone(corner * 2 + 1), mid[a].at[1], ms.at[a, 1], mr.at[a, 1], {"dp": near_y})
        )
        go(
            remote(
                gone(near_x * 2), R[a].at[s, 1], ds_.at[a, 0], dr.at[a, s], {"dp": near_x, "seq": 0}
            )
        )
        go(
            remote(
                gone(near_y * 2 + 1),
                R[a].at[s, 1],
                ds_.at[a, 1],
                dr.at[a, s],
                {"dp": near_y, "seq": 1},
            )
        )
        pairs[a] = go(
            remote(gone(d * 2 + other), R[a].at[s, 0], bs.at[a], br.at[a], {"seq": other})
        )
        lasts[a] = pltpu.make_async_copy(gone(me), R[a].at[s, 0], bl.at[a])
        lasts[a].start()

    def second_reduce(a):
        for way, near, index in ((0, near_y, near_y * 2), (1, near_x, near_x * 2 + 1)):
            mids[a, way].wait_recv()
            mid[a][way] = (
                mid[a][way].astype(f32) + place(gW, a, index)[...].astype(f32)
            ).astype(bf16)
            go(
                remote(
                    mid[a].at[way],
                    R[a].at[s, 2],
                    hs.at[a, way],
                    hr.at[a, s],
                    {"dp": near, "seq": way},
                )
            )

    def finish_reduce(a):
        for h in (0, 1):
            remote(R[a].at[h, 1], R[a].at[h, 1], ds_.at[a, 0], dr.at[a, h], {"dp": near_x}).wait_recv()
            remote(R[a].at[h, 2], R[a].at[h, 2], hs.at[a, 0], hr.at[a, h], {"dp": near_x}).wait_recv()
        pairs[a].wait_recv()
        lasts[a].wait()

    big = 256
    wide = 512

    start_hop2(3)
    wait_all(2)

    def up(b):
        span = at(b, length)
        slope[span, :] = dot_nn(second[span, :], G1[...]) + f1b[:, at(s, hh)]

        def curve(i):
            part_of = pl.ds(pl.multiple_of(b * length + i * step, step), step)
            activ, incline = gelu_pair(slope[part_of, :])
            hid[part_of, :] = activ.astype(bf16)
            slope[part_of, :] = incline

        loop(length // step, curve)

    loop(seqs, up)

    wait_near(3)

    theirs_half = at(other, rows)

    def cross_tile(j, slot, b, cols):
        remote(
            part.at[j, b, theirs_half, cols],
            sibp.at[j, b, :, cols],
            ps.at[slot],
            pr.at[slot],
            {"seq": other},
        ).start()

    def crossed(j, slot, cols):
        return remote(
            part.at[j, :, theirs_half, cols],
            sibp.at[j, :, :, cols],
            ps.at[slot],
            pr.at[slot],
            {"seq": other},
        )

    group = 2 * oc
    groups = [at(chip_of, group) for chip_of in (d, near_x, near_y, corner)]
    early, late, every = pl.ds(0, 3 * group), pl.ds(0, group), pl.ds(0, width)

    def branches_of(b, cols, slot):
        span = at(b, length)
        total = dot_nn(ctx[span, :], GO[:, cols]) + dot_nn(hid[span, :], G2[:, cols])
        part[0, b, :, cols] = total.astype(bf16)
        cross_tile(0, slot, b, cols)

    def branch(b):
        for g in (0, 1, 2):
            branches_of(b, groups[g], 0)

    loop(seqs, branch)

    nc = 4
    cr = rows // nc
    fin = (yfin, gfin)
    whole_span = pl.ds(0, rows)

    def spans(j, ch):
        return (whole_span, groups[ch]) if j == 0 else (pl.ds(ch * cr, cr), every)

    def tokens_of(j, ch):
        if j == 0:
            return at(s, rows)
        return pl.ds(pl.multiple_of(s * rows + ch * cr, cr), cr)

    def to_inner(j, i, b, ch):
        view = (j, b, *spans(j, ch))
        return remote(chip.at[view], ein.at[view], es.at[j, i, ch], er.at[j, i, ch], pt)

    def over(j, ch):
        view = (j, *spans(j, ch))
        return remote(fw.at[view], xin.at[view], xs.at[j, ch], xr.at[j, ch], facing)

    def final(j, b, ch, send, slot, where):
        view = fin[j].at[(b, *spans(j, ch))]
        return remote(view, view, send, fr.at[j, slot, ch], where)

    def z_one(j, slot, cols, which):
        crossed(j, slot, cols).wait_recv()
        for i, b in ((0, th), (1, mi)):
            for ch in which:
                rs, ks_ = spans(j, ch)
                chip[j, b, rs, ks_] = (
                    part[j, b, tokens_of(j, ch), ks_].astype(f32) + sibp[j, b, rs, ks_].astype(f32)
                ).astype(bf16)

                @pl.when(end)
                def _():
                    to_inner(j, i, b, ch).start()

    def z_two(j, which):
        @pl.when(inner)
        def _():
            for ch in which:
                to_inner(j, 0, th, ch).wait_recv()
                rs, ks_ = spans(j, ch)
                fw[j, rs, ks_] = (
                    chip[j, th, rs, ks_].astype(f32) + ein[j, th, rs, ks_].astype(f32)
                ).astype(bf16)
                over(j, ch).start()

    def z_three(j, which):
        @pl.when(inner)
        def _():
            for ch in which:
                to_inner(j, 1, mi, ch).wait_recv()
                over(j, ch).wait_recv()
                rs, ks_ = spans(j, ch)
                total = (
                    chip[j, mi, rs, ks_].astype(f32)
                    + ein[j, mi, rs, ks_].astype(f32)
                    + xin[j, rs, ks_].astype(f32)
                )
                inputs = xf[mi, tokens_of(j, ch), ks_].astype(f32)
                if j == 0:
                    result = inputs + total + rowb[2:3, ks_] + rowb[3:4, ks_]
                else:
                    _, normed, inv_std = layer_norm(inputs, 1.0, 0.0)
                    result = norm_back(total, normed, inv_std, 1.0)
                fin[j][mi, rs, ks_] = result.astype(bf16)
                final(j, mi, ch, fs.at[j, 0, ch], 0, pt).start()
                final(j, mi, ch, fs.at[j, 1, ch], 1, facing).start()

    def z_four(j, which):
        @pl.when(inner)
        def _():
            for ch in which:
                final(j, th, ch, fs.at[j, 1, ch], 1, facing).wait_recv()
                final(j, th, ch, fs2.at[j, ch], 1, pt).start()

    def z_five(j):
        for slot, cols in (((0, early), (2, late)), ((1, every),))[j]:
            crossed(j, slot, cols).wait_send()
        for ch in range(nc):

            @pl.when(end)
            def _():
                for i, b in ((0, th), (1, mi)):
                    to_inner(j, i, b, ch).wait_send()
                final(j, mi, ch, fs.at[j, 0, ch], 0, pt).wait_recv()
                final(j, th, ch, fs2.at[j, ch], 1, pt).wait_recv()

            @pl.when(inner)
            def _():
                over(j, ch).wait_send()
                final(j, mi, ch, fs.at[j, 0, ch], 0, pt).wait_send()
                final(j, mi, ch, fs.at[j, 1, ch], 1, facing).wait_send()
                final(j, th, ch, fs2.at[j, ch], 1, pt).wait_send()


    tiles = width // wide


    def qkv_grad(i):
        rows_of = at(i, big)
        lhs = first[:, rows_of]
        three = dot_tn(lhs, jnp.concatenate([gproj[0], gproj[1], gproj[2]], axis=1))
        for j in range(3):
            gW[0][j, rows_of, :] = three[:, j * fh : (j + 1) * fh].astype(bf16)

    loop(width // big, qkv_grad)

    z_one(0, 0, early, (0, 1, 2))

    def out_grad(i):
        cols = at(i, wide)
        gW[1][:, cols] = dot_tn(ctx[...], cf[:, :, cols].reshape(tokens, wide)).astype(bf16)

    loop(width // wide, out_grad)
    start_reduce(0)
    start_reduce(1)

    def first_back(i):
        b, n = i // tiles, lax.rem(i, tiles)
        span, cols = at(b, length), at(n, wide)
        grad = dot_nt(
            jnp.concatenate([gproj[j, span, :] for j in range(3)], axis=1),
            jnp.concatenate([GQ[j, cols, :] for j in range(3)], axis=1),
        )
        gacc[span, cols] = grad * gains[0:1, cols]
        brow[2:3, cols] = brow[2:3, cols] + jnp.sum(grad * nrm[span, cols], axis=0, keepdims=True)
        brow[4:5, cols] = brow[4:5, cols] + jnp.sum(grad, axis=0, keepdims=True)

    loop(seqs * tiles, first_back)

    def down_grad(i):
        m, n = i // tiles, lax.rem(i, tiles)
        units, cols = at(m, big), at(n, wide)
        gW[3][units, cols] = dot_tn(
            hid[:, units], cf[:, :, cols].reshape(tokens, wide)
        ).astype(bf16)

    loop(hh // big * tiles, down_grad)

    start_reduce(3)
    ones = jnp.ones((16, rows), bf16)
    csum = dot_nn(ones, cf[0, mine, :])
    for b in range(1, seqs):
        csum = csum + dot_nn(ones, cf[b, mine, :])
    brow[6:7, :] = csum[0:1, :]
    wait_hop2(3)

    def late_branch(b):
        branches_of(b, groups[3], 2)

    loop(seqs, late_branch)

    def down_back(b):
        span = at(b, length)
        grad = dot_nt(cf[b], G2[...]) * slope[span, :]
        ghid[span, :] = grad.astype(bf16)
        spot = at(s, hh)
        brow[0:1, spot] = brow[0:1, spot] + jnp.sum(grad, axis=0, keepdims=True)

    loop(seqs, down_back)

    z_one(0, 2, late, (3,))
    z_two(0, (0, 1, 2))

    def second_back(i):
        b, n = i // tiles, lax.rem(i, tiles)
        span, cols = at(b, length), at(n, wide)
        grad = dot_nt(ghid[span, :], G1[cols, :])
        part[1, b, :, cols] = (gacc[span, cols] + grad * gains[1:2, cols]).astype(bf16)
        cross_tile(1, 1, b, cols)
        brow[3:4, cols] = brow[3:4, cols] + jnp.sum(grad * nrm[span, cols], axis=0, keepdims=True)
        brow[5:6, cols] = brow[5:6, cols] + jnp.sum(grad, axis=0, keepdims=True)

    loop(seqs * tiles, second_back)
    bpair_copy = go(remote(brow, bpair, b1s, b1r, {"seq": other}))

    bpair_copy.wait_recv()
    bsum[...] = brow[...] + bpair[...]

    def bias_hop(src, dst, where):
        return remote(
            bsum if src == 0 else bgot3.at[3], bgot3.at[dst], b3s.at[src], b3r.at[dst], where
        )

    @pl.when(end)
    def _():
        bias_hop(0, 0, pt).start()

    z_one(1, 1, every, range(nc))
    z_three(0, (0, 1, 2))
    z_two(0, (3,))

    def up_grad(i):
        rows_of = at(i, big)
        gW[2][rows_of, :] = dot_tn(second[:, rows_of], ghid[...]).astype(bf16)

    loop(width // big, up_grad)
    start_reduce(2)
    second_reduce(0)
    second_reduce(1)

    @pl.when(inner)
    def _():
        bias_hop(0, 0, pt).wait_recv()
        bgot3[3] = bsum[...] + bgot3[0]
        bias_hop(1, 1, facing).start()

    z_two(1, (0,))
    z_four(0, (0,))
    z_two(1, (1,))
    z_three(0, (3,))
    z_four(0, (1,))
    second_reduce(3)
    z_two(1, (2,))
    z_four(0, (2,))
    z_two(1, (3,))

    @pl.when(inner)
    def _():
        bias_hop(1, 1, facing).wait_recv()
        bias_hop(1, 1, facing).wait_send()
        bgot3[3] = bgot3[3] + bgot3[1]
        bias_hop(2, 2, pt).start()
        bsum2[2:6, :] = bgot3[3, 2:6, :]

    @pl.when(end)
    def _():
        bias_hop(2, 2, pt).wait_recv()
        bsum2[2:6, :] = bgot3[2, 2:6, :]

    bsum2[0:2, :] = bsum[0:2, :]
    bsum2[6:8, :] = bsum[6:8, :]
    x_send = go(remote(bsum2, bgot2.at[0], b2s.at[0], b2r.at[0], {"dp": near_x}))
    z_three(1, (0,))
    z_four(0, (3,))
    z_three(1, (1, 2))
    second_reduce(2)
    z_three(1, (3,))
    x_send.wait_recv()
    bgot2[2] = bsum2[...] + bgot2[0]
    y_send = go(remote(bgot2.at[2], bgot2.at[1], b2s.at[1], b2r.at[1], {"dp": near_y}))
    z_four(1, range(nc))
    y_send.wait_recv()
    bout[...] = bgot2[2] + bgot2[1]

    @pl.when(end)
    def _():
        bias_hop(0, 0, pt).wait_send()

    @pl.when(inner)
    def _():
        bias_hop(2, 2, pt).wait_send()

    z_five(0)
    z_five(1)
    for a in (0, 1, 3, 2):
        finish_reduce(a)
    for a in range(4):
        for way in (0, 1):
            for k in (0, 1):
                hop1_copy(a, way, k).wait_send()
            hop2_copy(a, way).wait_send()
    for copy in sends:
        copy.wait_send()


def mega(x, c, seg, pos, wq, wo, w1, w2, qb, f1b, gains, rowb):
    shape = jax.ShapeDtypeStruct
    f32, bf16 = jnp.float32, jnp.bfloat16
    seqs, rows, width = x.shape
    kr, oc, fh, hh = wq.shape[1], wo.shape[1], wq.shape[2] // 2, w1.shape[1] // 2
    length = rows * 2
    tokens = seqs * length
    nc = 4
    pieces = ((3, kr, fh), (fh, oc), (kr, hh), (hh, oc))
    fulls = ((3, width, fh), (fh, width), (width, hh), (hh, width))
    dma = pltpu.SemaphoreType.DMA
    vm = lambda dims, kind: pltpu.VMEM(dims, kind)
    bias = (8, width)
    scratch = [
        vm((seqs, length, width), bf16),
        vm((seqs, length, width), bf16),
        vm((2,) + seg.shape, jnp.int32),
        vm((2,) + pos.shape, jnp.int32),
        *[vm(f, bf16) for f in fulls],
        vm((tokens, width), bf16),
        vm((tokens, width), bf16),
        vm((tokens, width), f32),
        vm((3, tokens, fh), f32),
        *[vm((tokens, fh), bf16)] * 5,
        vm((3, tokens, fh), bf16),
        vm((tokens, width), f32),
        vm((tokens, hh), bf16),
        vm((tokens, hh), f32),
        vm((tokens, hh), bf16),
        *[vm(f, bf16) for f in fulls],
        *[vm((2,) + p, bf16) for p in pieces],
        vm((2, seqs, length, width), bf16),
        *[vm((2, seqs, rows, width), bf16)] * 3,
        *[vm((2, rows, width), bf16)] * 2,
        vm(bias, f32),
        vm(bias, f32),
        vm(bias, f32),
        vm((4,) + bias, f32),
        vm(bias, f32),
        vm((4,) + bias, f32),
        *[dma((4, 2, 2))] * 2,
        *[dma((4, 2))] * 2,
        *[dma((4,))] * 3,
        *[dma((4,))] * 3,
        *[dma((4, 2))] * 6,
        *[dma((4,))] * 3,
        *[dma((3,))] * 2,
        *[dma((2, 2, nc))] * 2,
        *[dma((2, nc))] * 2,
        *[dma((2, 2, nc))] * 2,
        dma((2, nc)),
        dma,
        dma,
        *[dma((4,))] * 4,
        *[vm(v.shape, f32) for v in (qb, f1b, gains, rowb)],
        dma((4,)),
    ]
    return pl.pallas_call(
        functools.partial(mega_kernel, (seqs, rows, width, kr, oc, fh, hh)),
        out_shape=(
            *[shape((2, 3) + p, bf16) for p in pieces],
            shape(x.shape, bf16),
            shape(x.shape, bf16),
            shape(bias, f32),
        ),
        in_specs=[HBM] * 12,
        out_specs=[HBM] * 4 + [VM] * 3,
        scratch_shapes=scratch,
        compiler_params=pltpu.CompilerParams(
            collective_id=0, has_side_effects=True, vmem_limit_bytes=63 * 2**20
        ),
    )(x, c, seg, pos, wq, wo, w1, w2, qb, f1b, gains, rowb)


def final_kernel(dims, *refs):
    f32 = jnp.float32
    fh, hh = dims
    rq, ro, r1, r2, yf, gf, bb, c = range(8)
    hbm_in, hbm_out = refs[:8], refs[8:18]
    vin, vout = refs[18:26], refs[26:36]
    in_sem, out_sem = refs[36:]
    out, gin, oq, oo, o1, o2, oqb, of1, ogn, orow = range(10)
    loads = [pltpu.make_async_copy(hbm_in[i], vin[i], in_sem.at[i]) for i in range(8)]
    straight = pltpu.make_async_copy(vin[yf], hbm_out[out], out_sem.at[out])
    stores = [pltpu.make_async_copy(vout[i], hbm_out[i], out_sem.at[i]) for i in range(10)]
    for i in (yf, r1, r2, c, gf, rq, ro, bb):
        loads[i].start()

    def total(ref, *index):
        return (
            ref[(index[0], 0) + index[1:]].astype(f32)
            + ref[(index[0], 1) + index[1:]].astype(f32)
            + ref[(index[0], 2) + index[1:]].astype(f32)
        )

    loads[yf].wait()
    straight.start()
    loads[r1].wait()
    for h in (0, 1):
        vout[o1][:, h * hh : (h + 1) * hh] = total(vin[r1], h)
    stores[o1].start()
    loads[r2].wait()
    for h in (0, 1):
        vout[o2][h * hh : (h + 1) * hh, :] = total(vin[r2], h)
    stores[o2].start()
    loads[c].wait()
    loads[gf].wait()
    vout[gin][...] = vin[c][...].astype(f32) + vin[gf][...].astype(f32)
    stores[gin].start()
    loads[rq].wait()
    for h in (0, 1):
        for j in range(3):
            vout[oq][j, :, h * fh : (h + 1) * fh] = total(vin[rq], h, j)
    stores[oq].start()
    loads[ro].wait()
    for h in (0, 1):
        vout[oo][h * fh : (h + 1) * fh, :] = total(vin[ro], h)
    stores[oo].start()
    loads[bb].wait()
    rows = vin[bb]
    for j in range(3):
        vout[oqb][j : j + 1, :] = rows[1:2, j * 2 * fh : (j + 1) * 2 * fh]
    vout[of1][...] = rows[0:1, : 2 * hh]
    vout[ogn][...] = rows[2:4, :]
    vout[orow][0:2, :] = rows[4:6, :]
    vout[orow][2:3, :] = rows[6:7, :]
    vout[orow][3:4, :] = rows[6:7, :]
    for i in (oqb, of1, ogn, orow):
        stores[i].start()
    straight.wait()
    for i in range(1, 10):
        stores[i].wait()


def whole_rows(
    block_input,
    cotangent,
    segments,
    positions,
    w_qkv,
    qkv_bias,
    w_out,
    w_fc1,
    fc1_bias,
    w_fc2,
    ln_gains,
    row_biases,
):
    shape = jax.ShapeDtypeStruct
    f32 = jnp.float32
    got = mega(
        block_input,
        cotangent,
        segments,
        positions,
        w_qkv,
        w_out,
        w_fc1,
        w_fc2,
        qkv_bias,
        fc1_bias.reshape(1, -1),
        ln_gains,
        row_biases,
    )
    shapes = (
        shape(block_input.shape, block_input.dtype),
        shape(block_input.shape, f32),
        shape(w_qkv.shape, f32),
        shape(w_out.shape, f32),
        shape(w_fc1.shape, f32),
        shape(w_fc2.shape, f32),
        shape(qkv_bias.shape, f32),
        shape((1, fc1_bias.size), f32),
        shape(ln_gains.shape, f32),
        shape(row_biases.shape, f32),
    )
    operands = (*got, cotangent)
    outs = pl.pallas_call(
        functools.partial(final_kernel, (w_qkv.shape[2] // 2, w_fc1.shape[1] // 2)),
        out_shape=shapes,
        in_specs=[HBM] * len(operands),
        out_specs=[HBM] * len(shapes),
        scratch_shapes=[
            *[pltpu.VMEM(v.shape, v.dtype) for v in operands],
            *[pltpu.VMEM(v.shape, v.dtype) for v in shapes],
            pltpu.SemaphoreType.DMA((len(operands),)),
            pltpu.SemaphoreType.DMA((len(shapes),)),
        ],
        compiler_params=pltpu.CompilerParams(vmem_limit_bytes=63 * 2**20),
    )(*operands)
    return (*outs[:7], outs[7].reshape(fc1_bias.shape), *outs[8:])


def block(mesh, *args):
    seqs, rows, width = args[0].shape
    flat, hidden = args[4].shape[2], args[7].shape[1]
    sizes = mesh.shape
    if (
        (sizes["dp"], sizes["seq"], sizes["tensor"]) == (4, 2, 4)
        and flat == 4 * HD
        and seqs <= 2
        and rows == 128
        and width % 512 == 0
        and max(hidden, 3 * flat) <= width <= 1024
        and hidden % 512 == 0
    ):
        return whole_rows(*args)
    return shards(*args)


def solution(mesh):
    return jax.shard_map(
        functools.partial(block, mesh),
        mesh=mesh,
        in_specs=(
            P("dp", "seq", None),
            P("dp", "seq", None),
            P("dp", "seq"),
            P("dp", "seq"),
            P(None, ("dp", "seq"), "tensor"),
            P(None, "tensor"),
            P("tensor", ("dp", "seq")),
            P(("dp", "seq"), "tensor"),
            P("tensor"),
            P("tensor", ("dp", "seq")),
            P(),
            P(),
        ),
        out_specs=(
            P("dp", "seq", None),
            P("dp", "seq", None),
            P(None, ("dp", "seq"), "tensor"),
            P("tensor", ("dp", "seq")),
            P(("dp", "seq"), "tensor"),
            P("tensor", ("dp", "seq")),
            P(None, "tensor"),
            P("tensor"),
            P(),
            P(),
        ),
        check_vma=False,
    )
```

```python
import functools
import math

import jax
import jax.numpy as jnp
from jax import lax
from jax.experimental import pallas as pl
from jax.experimental.pallas import tpu as pltpu
from jax.sharding import PartitionSpec as P

HD = 64
ROT = 16


norm_eps = 1e-05
neg_big = -1e30
inv_root_two = 0.7071067811865476
inv_root_tau = 0.3989422804014327


def layer_norm(values, gain, shift):
    centred = values - jnp.mean(values, axis=-1, keepdims=True)
    inv_std = lax.rsqrt(jnp.mean(centred * centred, axis=-1, keepdims=True) + norm_eps)
    normed = centred * inv_std
    return (normed * gain + shift, normed, inv_std)


def norm_back(grad_out, normed, inv_std, gain):
    scaled = grad_out * gain
    centre = jnp.mean(scaled, axis=-1, keepdims=True)
    slope = jnp.mean(scaled * normed, axis=-1, keepdims=True)
    return inv_std * (scaled - centre - normed * slope)


def gelu_pair(pre_act):
    cumul = 0.5 * (1.0 + lax.erf(pre_act * inv_root_two))
    return (pre_act * cumul, cumul + pre_act * inv_root_tau * jnp.exp(-0.5 * pre_act * pre_act))


def rotary_tables(positions):
    half_rot = ROT // 2
    freqs = 10000.0 ** (-2.0 * jnp.arange(half_rot).astype(jnp.float32) / ROT)
    angles = positions.astype(jnp.float32)[..., None] * freqs
    cosine = jnp.cos(angles)
    sine = jnp.sin(angles)
    return (
        jnp.concatenate([cosine, cosine], -1)[..., None, :],
        jnp.concatenate([sine, sine], -1)[..., None, :],
    )


def rotate(tensor, cosine, sine):
    half_rot = ROT // 2
    head = tensor[..., :ROT]
    turned = jnp.concatenate([-head[..., half_rot:], head[..., :half_rot]], -1)
    return jnp.concatenate([head * cosine + turned * sine, tensor[..., ROT:]], -1)


def unrotate(grads, cosine, sine):
    half_rot = ROT // 2
    head = grads[..., :ROT]
    times_sine = head * sine
    back = jnp.concatenate([times_sine[..., half_rot:], -times_sine[..., :half_rot]], -1)
    return jnp.concatenate([head * cosine + back, grads[..., ROT:]], -1)


def gather_keys(keys_flat, values_in, segments):
    return (
        lax.all_gather(keys_flat, "seq", axis=1, tiled=True),
        lax.all_gather(values_in, "seq", axis=1, tiled=True),
        lax.all_gather(segments, "seq", axis=1, tiled=True),
    )


def pair_terms(
    query_blk,
    query_pos,
    query_seg,
    key_blk,
    value_blk,
    key_pos,
    key_seg,
    grad_blk,
    log_blk,
    delta_blk,
    scale,
):
    scores = (
        jnp.einsum("sqhd,skhd->shqk", query_blk, key_blk, preferred_element_type=jnp.float32)
        * scale
    )
    same_doc = query_seg[:, None, :, None] == key_seg[:, None, None, :]
    earlier = key_pos[None, None, None, :] <= query_pos[None, None, :, None]
    probs = jnp.where(same_doc & earlier, jnp.exp(scores - log_blk[..., None]), 0.0)
    grad_p = jnp.einsum("sqhd,skhd->shqk", grad_blk, value_blk, preferred_element_type=jnp.float32)
    grad_s = (probs * (grad_p - delta_blk[..., None])).astype(jnp.bfloat16)
    return (probs, grad_s)


def shards(
    block_input,
    cotangent,
    segments,
    positions,
    w_qkv,
    qkv_bias,
    w_out,
    w_fc1,
    fc1_bias,
    w_fc2,
    ln_gains,
    row_biases,
):
    seqs_here, rows_here, width = block_input.shape
    heads_here = w_qkv.shape[2] // HD
    flat_width = heads_here * HD
    scale = HD ** (-0.5)
    shape_heads = (seqs_here, rows_here, heads_here, HD)
    forward_weights = (
        lax.all_gather(w_qkv, ("dp", "seq"), axis=1, tiled=True),
        lax.all_gather(w_out, ("dp", "seq"), axis=1, tiled=True),
        lax.all_gather(w_fc1, ("dp", "seq"), axis=0, tiled=True),
        lax.all_gather(w_fc2, ("dp", "seq"), axis=1, tiled=True),
    )
    query_key_value_gathered, output_weight_gathered, up_weight_gathered, down_weight_gathered = (
        forward_weights
    )
    inputs_f = block_input.astype(jnp.float32)
    first_out, first_normed, first_inv = layer_norm(inputs_f, ln_gains[0], row_biases[0])
    second_out, second_normed, second_inv = layer_norm(inputs_f, ln_gains[1], row_biases[1])
    first_norm_input = first_out.astype(jnp.bfloat16)
    second_norm_input = second_out.astype(jnp.bfloat16)
    projected = (
        jnp.einsum(
            "bxf,kfh->kbxh",
            first_norm_input,
            query_key_value_gathered,
            preferred_element_type=jnp.float32,
        )
        + qkv_bias[:, None, None, :]
    )
    cosine, sine = rotary_tables(positions)
    queries = rotate(projected[0].reshape(shape_heads), cosine, sine).astype(jnp.bfloat16)
    keys_flat = (
        rotate(projected[1].reshape(shape_heads), cosine, sine)
        .astype(jnp.bfloat16)
        .reshape(seqs_here, rows_here, flat_width)
    )
    values_in = projected[2].astype(jnp.bfloat16)
    query_pos = lax.axis_index("seq") * rows_here + jnp.arange(rows_here)

    def block_scores(key_block, seg_block, key_start):
        count = key_block.shape[1]
        keys_heads = key_block.reshape(seqs_here, count, heads_here, HD)
        scores = (
            jnp.einsum("sqhd,skhd->shqk", queries, keys_heads, preferred_element_type=jnp.float32)
            * scale
        )
        key_pos = key_start + jnp.arange(count)
        same_doc = segments[:, None, :, None] == seg_block[:, None, None, :]
        earlier = key_pos[None, None, None, :] <= query_pos[None, None, :, None]
        return (scores, same_doc & earlier)

    start_state = (
        jnp.full((seqs_here, heads_here, rows_here), neg_big, jnp.float32),
        jnp.zeros((seqs_here, heads_here, rows_here), jnp.float32),
        jnp.zeros((seqs_here, heads_here, rows_here, HD), jnp.float32),
    )
    key_part = lax.all_gather(keys_flat, "seq", axis=1, tiled=True)
    value_part = lax.all_gather(values_in, "seq", axis=1, tiled=True)
    seg_part = lax.all_gather(segments, "seq", axis=1, tiled=True)
    count = key_part.shape[1]
    attend_block = math.gcd(count, 512)

    def step_block(block_idx, state):
        run_max, run_sum, accum = state
        offset = block_idx * attend_block
        key_block = lax.dynamic_slice_in_dim(key_part, offset, attend_block, 1)
        value_block = lax.dynamic_slice_in_dim(value_part, offset, attend_block, 1).reshape(
            seqs_here, attend_block, heads_here, HD
        )
        seg_block = lax.dynamic_slice_in_dim(seg_part, offset, attend_block, 1)
        scores, allowed = block_scores(key_block, seg_block, offset)
        new_max = jnp.maximum(run_max, jnp.max(jnp.where(allowed, scores, neg_big), axis=-1))
        factor = jnp.exp(run_max - new_max)
        expo = jnp.where(allowed, jnp.exp(scores - new_max[..., None]), 0.0)
        new_sum = run_sum * factor + jnp.sum(expo, axis=-1)
        update = jnp.einsum(
            "shqk,skhd->shqd",
            expo.astype(jnp.bfloat16),
            value_block,
            preferred_element_type=jnp.float32,
        )
        return (new_max, new_sum, accum * factor[..., None] + update)

    run_max, run_sum, accum = lax.fori_loop(0, count // attend_block, step_block, start_state)
    log_sum = run_max + jnp.log(run_sum)
    attention_context = (
        (accum / run_sum[..., None])
        .transpose(0, 2, 1, 3)
        .reshape(seqs_here, rows_here, flat_width)
        .astype(jnp.bfloat16)
    )
    pre_act = (
        jnp.einsum(
            "vrk,kt->vrt", second_norm_input, up_weight_gathered, preferred_element_type=jnp.float32
        )
        + fc1_bias
    )
    activ, gelu_slope = gelu_pair(pre_act)
    hidden_activation = activ.astype(jnp.bfloat16)
    partial_output_sum = jnp.einsum(
        "qhw,wj->qhj", attention_context, output_weight_gathered, preferred_element_type=jnp.float32
    )
    partial_output_sum = partial_output_sum + jnp.einsum(
        "qzg,gc->qzc", hidden_activation, down_weight_gathered, preferred_element_type=jnp.float32
    )
    branches = lax.psum(partial_output_sum.astype(jnp.bfloat16), "tensor").astype(jnp.float32)
    output = (inputs_f + branches + row_biases[2] + row_biases[3]).astype(jnp.bfloat16)
    query_key_value_backward, output_weight_backward, up_weight_backward, down_weight_backward = (
        lax.all_gather(w_qkv, ("dp", "seq"), axis=1, tiled=True),
        lax.all_gather(w_out, ("dp", "seq"), axis=1, tiled=True),
        lax.all_gather(w_fc1, ("dp", "seq"), axis=0, tiled=True),
        lax.all_gather(w_fc2, ("dp", "seq"), axis=1, tiled=True),
    )
    grad_f = cotangent.astype(jnp.float32)
    gradient_output_weight = jnp.einsum(
        "bxz,bxe->ze", attention_context, cotangent, preferred_element_type=jnp.float32
    )
    grad_context = jnp.einsum(
        "zpi,xi->zpx", cotangent, output_weight_backward, preferred_element_type=jnp.float32
    ).astype(jnp.bfloat16)
    gradient_down_weight = jnp.einsum(
        "tzi,tzo->io", hidden_activation, cotangent, preferred_element_type=jnp.float32
    )
    grad_pre = (
        jnp.einsum(
            "hvg,rg->hvr", cotangent, down_weight_backward, preferred_element_type=jnp.float32
        )
        * gelu_slope
    )
    gradient_hidden_input = grad_pre.astype(jnp.bfloat16)
    grad_fc1_w = jnp.einsum(
        "mxa,mxr->ar", second_norm_input, gradient_hidden_input, preferred_element_type=jnp.float32
    )
    grad_second = jnp.einsum(
        "ikq,uq->iku", gradient_hidden_input, up_weight_backward, preferred_element_type=jnp.float32
    )
    grad_ctx_heads = grad_context.reshape(shape_heads)
    delta = jnp.sum(
        grad_ctx_heads.astype(jnp.float32)
        * attention_context.reshape(shape_heads).astype(jnp.float32),
        axis=-1,
    ).transpose(0, 2, 1)
    key_all, value_all, seg_all = gather_keys(keys_flat, values_in, segments)
    total_len = key_all.shape[1]
    block = math.gcd(total_len, 512)

    def key_slices(offset):
        key_block = lax.dynamic_slice_in_dim(key_all, offset, block, 1).reshape(
            seqs_here, block, heads_here, HD
        )
        value_block = lax.dynamic_slice_in_dim(value_all, offset, block, 1).reshape(
            seqs_here, block, heads_here, HD
        )
        seg_block = lax.dynamic_slice_in_dim(seg_all, offset, block, 1)
        return (key_block, value_block, seg_block)

    def back_block(block_idx, state):
        grad_q, grad_key_all, grad_value_all = state
        offset = block_idx * block
        key_block, value_block, seg_block = key_slices(offset)
        probs, grad_s = pair_terms(
            queries,
            query_pos,
            segments,
            key_block,
            value_block,
            offset + jnp.arange(block),
            seg_block,
            grad_ctx_heads,
            log_sum,
            delta,
            scale,
        )
        grad_v = jnp.einsum(
            "shqk,sqhd->skhd",
            probs.astype(jnp.bfloat16),
            grad_ctx_heads,
            preferred_element_type=jnp.float32,
        )
        grad_q = (
            grad_q
            + jnp.einsum("shqk,skhd->sqhd", grad_s, key_block, preferred_element_type=jnp.float32)
            * scale
        )
        grad_k = (
            jnp.einsum("shqk,sqhd->skhd", grad_s, queries, preferred_element_type=jnp.float32)
            * scale
        )
        grad_key_all = lax.dynamic_update_slice_in_dim(
            grad_key_all, grad_k.reshape(seqs_here, block, flat_width), offset, 1
        )
        grad_value_all = lax.dynamic_update_slice_in_dim(
            grad_value_all, grad_v.reshape(seqs_here, block, flat_width), offset, 1
        )
        return (grad_q, grad_key_all, grad_value_all)

    back_start = (
        jnp.zeros(shape_heads, jnp.float32),
        jnp.zeros((seqs_here, total_len, flat_width), jnp.float32),
        jnp.zeros((seqs_here, total_len, flat_width), jnp.float32),
    )
    grad_q, grad_key_all, grad_value_all = lax.fori_loop(
        0, total_len // block, back_block, back_start
    )
    grad_key_here, grad_value_here = (
        lax.psum_scatter(
            grad_key_all.astype(jnp.bfloat16), "seq", scatter_dimension=1, tiled=True
        ).astype(jnp.float32),
        lax.psum_scatter(
            grad_value_all.astype(jnp.bfloat16), "seq", scatter_dimension=1, tiled=True
        ).astype(jnp.float32),
    )
    grad_proj = jnp.stack(
        [
            unrotate(grad_q, cosine, sine).reshape(seqs_here, rows_here, flat_width),
            unrotate(grad_key_here.reshape(shape_heads), cosine, sine).reshape(
                seqs_here, rows_here, flat_width
            ),
            grad_value_here,
        ]
    )
    grad_bias_qkv = jnp.sum(grad_proj, axis=(1, 2))
    gradient_projection_input = grad_proj.astype(jnp.bfloat16)
    grad_qkv_w = jnp.einsum(
        "ink,oint->okt",
        first_norm_input,
        gradient_projection_input,
        preferred_element_type=jnp.float32,
    )
    grad_first = jnp.einsum(
        "etbp,eop->tbo",
        gradient_projection_input,
        query_key_value_backward,
        preferred_element_type=jnp.float32,
    )
    grad_first, grad_second = (
        lax.psum(grad_first.astype(jnp.bfloat16), "tensor").astype(jnp.float32),
        lax.psum(grad_second.astype(jnp.bfloat16), "tensor").astype(jnp.float32),
    )
    grad_input = (
        grad_f
        + norm_back(grad_first, first_normed, first_inv, ln_gains[0])
        + norm_back(grad_second, second_normed, second_inv, ln_gains[1])
    )
    gain_terms = jnp.stack(
        [
            jnp.sum(grad_first * first_normed, axis=(0, 1)),
            jnp.sum(grad_second * second_normed, axis=(0, 1)),
        ]
    )
    row_terms = jnp.stack(
        [
            jnp.sum(grad_first, axis=(0, 1)),
            jnp.sum(grad_second, axis=(0, 1)),
            jnp.sum(grad_f, axis=(0, 1)),
            jnp.sum(grad_f, axis=(0, 1)),
        ]
    )
    bias_sums = lax.psum(
        (grad_bias_qkv, jnp.sum(grad_pre, axis=(0, 1)), gain_terms, row_terms), ("dp", "seq")
    )
    weight_sums = (
        lax.psum_scatter(grad_qkv_w, ("dp", "seq"), scatter_dimension=1, tiled=True),
        lax.psum_scatter(gradient_output_weight, ("dp", "seq"), scatter_dimension=1, tiled=True),
        lax.psum_scatter(grad_fc1_w, ("dp", "seq"), scatter_dimension=0, tiled=True),
        lax.psum_scatter(gradient_down_weight, ("dp", "seq"), scatter_dimension=1, tiled=True),
    )
    return (
        output,
        grad_input,
        weight_sums[0],
        weight_sums[1],
        weight_sums[2],
        weight_sums[3],
        bias_sums[0],
        bias_sums[1],
        bias_sums[2],
        bias_sums[3],
    )


MESH = pl.DeviceIdType.MESH
ANY = pl.BlockSpec(memory_space=pl.ANY)
VM = pl.BlockSpec(memory_space=pltpu.VMEM)
HBM = pl.BlockSpec(memory_space=pltpu.HBM)


def remote(src, dst, send, recv, where):
    return pltpu.make_async_remote_copy(
        src_ref=src, dst_ref=dst, send_sem=send, recv_sem=recv, device_id=where, device_id_type=MESH
    )


def pair_of(d):
    return d + 1 - 2 * lax.rem(d, 2)


def dot_nn(left, right):
    return lax.dot_general(left, right, (((1,), (0,)), ((), ())), preferred_element_type=jnp.float32)


def dot_nt(left, right):
    return lax.dot_general(left, right, (((1,), (1,)), ((), ())), preferred_element_type=jnp.float32)


def dot_tn(left, right):
    return lax.dot_general(left, right, (((0,), (0,)), ((), ())), preferred_element_type=jnp.float32)


def spread(left, right):
    return lax.dot_general(
        left,
        right,
        (((0,), (0,)), ((), ())),
        precision=lax.Precision.HIGHEST,
        preferred_element_type=jnp.float32,
    )


def loop(count, body):
    def step(i, carry):
        body(i)
        return carry

    lax.fori_loop(0, count, step, 0)


def at(index, size):
    return pl.ds(pl.multiple_of(index * size, size), size)


def mega_kernel(dims, *refs):
    f32, bf16 = jnp.float32, jnp.bfloat16
    seqs, rows, width, kr, oc, fh, hh = dims
    length = 2 * rows
    tokens = seqs * length
    heads = fh // HD
    scale = HD ** (-0.5)
    (x, c, seg, pos, wq, wo, w1, w2, *small) = refs[:12]
    R = refs[12:16]
    yfin, gfin, bout = refs[16:19]
    (xf, cf, segb, posb, GQ, GO, G1, G2) = refs[19:27]
    (first, second, nrm, tables, qs, ks, vs, gcs, ctx, gproj) = refs[27:37]
    (gacc, hid, slope, ghid) = refs[37:41]
    gW = refs[41:45]
    mid = refs[45:49]
    (part, sibp, chip, ein, xin, fw) = refs[49:55]
    (brow, bpair, bsum, bgot2, bsum2, bgot3) = refs[55:61]
    (s1, r1, s2, r2, ss, sr, sl) = refs[61:68]
    (ts, tr, tl) = refs[68:71]
    (ms, mr, ds_, dr, hs, hr, bs, br, bl) = refs[71:80]
    (ps, pr, es, er, xs, xr, fs, fr, fs2) = refs[80:89]
    (b1s, b1r, b2s, b2r, b3s, b3r) = refs[89:95]
    qb, f1b, gains, rowb = refs[95:99]
    small_sem = refs[99]
    nseq, nt, ndp = 2, 4, 4
    d, s, t = lax.axis_index("dp"), lax.axis_index("seq"), lax.axis_index("tensor")
    other = 1 - s
    near_x, near_y, corner = pair_of(d), lax.rem(d + 2, 4), 3 - d
    me = d * nseq + s
    side = t // 2
    mi, th = side, 1 - side
    inner = (t == 1) | (t == 2)
    end = (t == 0) | (t == 3)
    pt, facing = {"tensor": pair_of(t)}, {"tensor": 3 - t}

    small_copies = [
        pltpu.make_async_copy(src, dst, small_sem.at[j])
        for j, (src, dst) in enumerate(zip(small, (qb, f1b, gains, rowb)))
    ]
    local_x = pltpu.make_async_copy(x, xf.at[:, at(s, rows), :], tl.at[0])
    for copy in (local_x, *small_copies):
        copy.start()
    barrier = pltpu.get_barrier_semaphore()
    for peer in (near_x, near_y):
        for core in (0, 1):
            pl.semaphore_signal(
                barrier, inc=1, device_id={"dp": peer, "seq": core}, device_id_type=MESH
            )
    pl.semaphore_signal(barrier, inc=1, device_id={"seq": other}, device_id_type=MESH)
    pl.semaphore_signal(barrier, inc=1, device_id=pt, device_id_type=MESH)

    @pl.when(inner)
    def _():
        pl.semaphore_signal(barrier, inc=1, device_id=facing, device_id_type=MESH)
        pl.semaphore_wait(barrier, 7)

    @pl.when(end)
    def _():
        pl.semaphore_wait(barrier, 6)

    sends = []

    def go(copy):
        copy.start()
        sends.append(copy)
        return copy

    def source(a, half):
        return (
            lambda: wq.at[:, :, at(half, fh)],
            lambda: wo.at[at(half, fh), :],
            lambda: w1.at[:, at(half, hh)],
            lambda: w2.at[at(half, hh), :],
        )[a]()

    def place(bufs, a, index):
        return (
            lambda: bufs[0].at[:, at(index, kr), :],
            lambda: bufs[1].at[:, at(index, oc)],
            lambda: bufs[2].at[at(index, kr), :],
            lambda: bufs[3].at[:, at(index, oc)],
        )[a]()

    full = (GQ, GO, G1, G2)
    sibs, locals_ = {}, {}

    def hop1_copy(a, way, k):
        near, half = (near_x, near_y)[way], (s, other)[k]
        return remote(
            source(a, half),
            place(full, a, me),
            s1.at[a, way, k],
            r1.at[a, way, k],
            {"dp": near, "seq": half},
        )

    def start_hop1(a):
        for way in (0, 1):
            for k in (0, 1):
                hop1_copy(a, way, k).start()

    def start_near(a):
        sibs[a] = go(
            remote(source(a, other), place(full, a, me), ss.at[a], sr.at[a], {"seq": other})
        )
        locals_[a] = pltpu.make_async_copy(source(a, s), place(full, a, me), sl.at[a])
        locals_[a].start()

    def hop2_copy(a, way):
        view = place(full, a, (near_x * nseq, near_y * nseq + 1)[way])
        return remote(view, view, s2.at[a, way], r2.at[a, way], {"dp": (near_y, near_x)[way]})

    def start_hop2(a):
        for way in (0, 1):
            for k in (0, 1):
                hop1_copy(a, way, k).wait_recv()
        for way in (0, 1):
            hop2_copy(a, way).start()

    def wait_hop2(a):
        hop2_copy(a, 0).wait_recv()
        hop2_copy(a, 1).wait_recv()

    def wait_near(a):
        sibs[a].wait_recv()
        locals_[a].wait()

    def wait_all(a):
        wait_hop2(a)
        wait_near(a)

    mine = at(s, rows)
    start_hop1(0)
    start_hop1(1)
    tok = []
    for j, (src, dst) in enumerate(
        ((x, xf.at[:, mine, :]), (pos, posb.at[s]), (seg, segb.at[s]), (c, cf.at[:, mine, :]))
    ):
        copy = local_x
        if j > 0:
            copy = pltpu.make_async_copy(src, dst, tl.at[j])
            copy.start()
        tok.append((copy, go(remote(src, dst, ts.at[j], tr.at[j], {"seq": other}))))
    start_near(0)
    start_near(1)
    start_hop1(2)
    start_near(2)
    start_near(3)

    step = 32
    per = rows // step

    def norm_half(half):
        def body(i):
            b, at_row = i // per, pl.multiple_of(half * rows + lax.rem(i, per) * step, step)
            flat_row = pl.multiple_of(b * length + at_row, step)
            values = xf[b, pl.ds(at_row, step), :].astype(f32)
            one, normed, _ = layer_norm(values, gains[0:1, :], rowb[0:1, :])
            span = pl.ds(flat_row, step)
            nrm[span, :] = normed
            first[span, :] = one.astype(bf16)
            second[span, :] = (normed * gains[1:2, :] + rowb[1:2, :]).astype(bf16)

        loop(seqs * per, body)

    for copy in small_copies:
        copy.wait()
    tok[0][0].wait()
    norm_half(s)
    tok[0][1].wait_recv()
    norm_half(other)
    brow[...] = jnp.zeros_like(brow)
    start_hop2(0)
    start_hop2(1)
    for j in (1, 2, 3):
        tok[j][0].wait()
        tok[j][1].wait_recv()

    half_rot = ROT // 2
    lane = lax.broadcasted_iota(jnp.int32, (half_rot, fh), 1)
    lane = lax.rem(lane, HD)
    which = lax.broadcasted_iota(jnp.int32, (half_rot, fh), 0)
    low = (lane == which).astype(f32)
    high = (lane == which + half_rot).astype(f32)
    rest = (lane[0:1, :] >= ROT).astype(f32)
    power = lax.broadcasted_iota(jnp.int32, (half_rot, length), 0).astype(f32)
    freqs = jnp.exp(power * (-2.0 / ROT * math.log(10000.0)))
    for b in range(seqs):
        row = jnp.concatenate([posb[0, b : b + 1, :], posb[1, b : b + 1, :]], axis=1).astype(f32)
        angles = row * freqs
        sine = jnp.sin(angles)
        tables[0, at(b, length), :] = spread(jnp.cos(angles), low + high) + rest
        tables[1, at(b, length), :] = spread(sine, high)
        tables[2, at(b, length), :] = spread(sine, -low)

    start_hop2(2)
    start_hop1(3)
    wait_all(0)
    wait_all(1)

    def project(b):
        span = at(b, length)
        inputs = first[span, :]
        cosine, sin_a, sin_b = tables[0, span, :], tables[1, span, :], tables[2, span, :]

        def turn(v):
            up, down = pltpu.roll(v, half_rot, 1), pltpu.roll(v, fh - half_rot, 1)
            return v * cosine + up * sin_a + down * sin_b

        bias = lambda j: qb[j : j + 1, at(s, fh)]
        three = dot_nn(inputs, jnp.concatenate([GQ[0], GQ[1], GQ[2]], axis=1))
        qs[span, :] = turn(three[:, :fh] + bias(0)).astype(bf16)
        ks[span, :] = turn(three[:, fh : 2 * fh] + bias(1)).astype(bf16)
        vs[span, :] = (three[:, 2 * fh :] + bias(2)).astype(bf16)
        gcs[span, :] = dot_nt(cf[b], GO[...]).astype(bf16)

    loop(seqs, project)

    lane_of = lax.broadcasted_iota(jnp.int32, (1, fh), 1) // HD

    def attend(b):
        span = at(b, length)
        q, k, v, gc = qs[span, :], ks[span, :], vs[span, :], gcs[span, :]
        seg_rows = [
            jnp.concatenate(
                [segb[0, n : n + 1, :], segb[1, n : n + 1, :]], axis=1
            ).astype(f32)
            for n in range(seqs)
        ]
        seg_row = seg_rows[0]
        for n in range(1, seqs):
            seg_row = jnp.where(b == n, seg_rows[n], seg_row)
        pick = (lax.broadcasted_iota(jnp.int32, (8, length), 0) == 0).astype(f32)
        seg_col = spread(jnp.broadcast_to(seg_row, (8, length)), pick)
        q_pos = lax.broadcasted_iota(jnp.int32, (length, length), 0)
        k_pos = lax.broadcasted_iota(jnp.int32, (length, length), 1)
        allowed = (seg_col == seg_row) & (k_pos <= q_pos)
        out = []
        for h in range(heads):
            keep = (lane_of == h).astype(bf16)
            scores = dot_nt(q * keep, k) * scale
            row_max = jnp.max(jnp.where(allowed, scores, neg_big), axis=-1, keepdims=True)
            expo = jnp.where(allowed, jnp.exp(scores - row_max), 0.0)
            inv = 1.0 / jnp.sum(expo, axis=-1, keepdims=True)
            mixed = (dot_nn(expo.astype(bf16), v) * inv).astype(bf16) * keep
            gch = gc * keep
            delta = jnp.sum(gch.astype(f32) * mixed.astype(f32), axis=-1, keepdims=True)
            probs = expo * inv
            grad_s = (probs * (dot_nt(gch, v) - delta)).astype(bf16)
            terms = (
                mixed,
                dot_nn(grad_s, k * keep),
                dot_tn(grad_s, q * keep),
                dot_tn(probs.astype(bf16), gch),
            )
            out = [p + q_ for p, q_ in zip(out, terms)] if out else list(terms)
        ctx[span, :] = out[0]
        cosine, sin_a, sin_b = tables[0, span, :], tables[1, span, :], tables[2, span, :]

        def back(v):
            up, down = pltpu.roll(v, half_rot, 1), pltpu.roll(v, fh - half_rot, 1)
            return v * cosine - up * sin_a - down * sin_b

        for j, grad in enumerate((back(out[1] * scale), back(out[2] * scale), out[3])):
            gproj[j, span, :] = grad.astype(bf16)
            spot = pl.ds(pl.multiple_of(j * 2 * fh + s * fh, fh), fh)
            brow[1:2, spot] = brow[1:2, spot] + jnp.sum(grad, axis=0, keepdims=True)

    loop(seqs, attend)

    pairs, mids, lasts = {}, {}, {}

    def start_reduce(a):
        gone = lambda index: place(gW, a, index)
        mids[a, 0] = go(
            remote(gone(corner * 2), mid[a].at[0], ms.at[a, 0], mr.at[a, 0], {"dp": near_x})
        )
        mids[a, 1] = go(
            remote(gone(corner * 2 + 1), mid[a].at[1], ms.at[a, 1], mr.at[a, 1], {"dp": near_y})
        )
        go(
            remote(
                gone(near_x * 2), R[a].at[s, 1], ds_.at[a, 0], dr.at[a, s], {"dp": near_x, "seq": 0}
            )
        )
        go(
            remote(
                gone(near_y * 2 + 1),
                R[a].at[s, 1],
                ds_.at[a, 1],
                dr.at[a, s],
                {"dp": near_y, "seq": 1},
            )
        )
        pairs[a] = go(
            remote(gone(d * 2 + other), R[a].at[s, 0], bs.at[a], br.at[a], {"seq": other})
        )
        lasts[a] = pltpu.make_async_copy(gone(me), R[a].at[s, 0], bl.at[a])
        lasts[a].start()

    def second_reduce(a):
        for way, near, index in ((0, near_y, near_y * 2), (1, near_x, near_x * 2 + 1)):
            mids[a, way].wait_recv()
            mid[a][way] = (
                mid[a][way].astype(f32) + place(gW, a, index)[...].astype(f32)
            ).astype(bf16)
            go(
                remote(
                    mid[a].at[way],
                    R[a].at[s, 2],
                    hs.at[a, way],
                    hr.at[a, s],
                    {"dp": near, "seq": way},
                )
            )

    def finish_reduce(a):
        for h in (0, 1):
            remote(R[a].at[h, 1], R[a].at[h, 1], ds_.at[a, 0], dr.at[a, h], {"dp": near_x}).wait_recv()
            remote(R[a].at[h, 2], R[a].at[h, 2], hs.at[a, 0], hr.at[a, h], {"dp": near_x}).wait_recv()
        pairs[a].wait_recv()
        lasts[a].wait()

    big = 512
    wide = 512

    start_hop2(3)
    wait_all(2)

    def up(b):
        span = at(b, length)
        slope[span, :] = dot_nn(second[span, :], G1[...]) + f1b[:, at(s, hh)]

        def curve(i):
            part_of = pl.ds(pl.multiple_of(b * length + i * step, step), step)
            activ, incline = gelu_pair(slope[part_of, :])
            hid[part_of, :] = activ.astype(bf16)
            slope[part_of, :] = incline

        loop(length // step, curve)

    loop(seqs, up)

    wait_near(3)

    theirs_half = at(other, rows)

    def cross_tile(j, slot, b, cols):
        remote(
            part.at[j, b, theirs_half, cols],
            sibp.at[j, b, :, cols],
            ps.at[slot],
            pr.at[slot],
            {"seq": other},
        ).start()

    def crossed(j, slot, cols):
        return remote(
            part.at[j, :, theirs_half, cols],
            sibp.at[j, :, :, cols],
            ps.at[slot],
            pr.at[slot],
            {"seq": other},
        )

    group = 2 * oc
    groups = [at(chip_of, group) for chip_of in (d, near_x, near_y, corner)]
    early, late, every = pl.ds(0, 3 * group), pl.ds(0, group), pl.ds(0, width)

    def branches_of(b, cols, slot):
        span = at(b, length)
        total = dot_nn(ctx[span, :], GO[:, cols]) + dot_nn(hid[span, :], G2[:, cols])
        part[0, b, :, cols] = total.astype(bf16)
        cross_tile(0, slot, b, cols)

    def branch(b):
        for g in (0, 1, 2):
            branches_of(b, groups[g], 0)

    loop(seqs, branch)

    nc = 4
    cr = rows // nc
    fin = (yfin, gfin)
    whole_span = pl.ds(0, rows)

    def spans(j, ch):
        return (whole_span, groups[ch]) if j == 0 else (pl.ds(ch * cr, cr), every)

    def tokens_of(j, ch):
        if j == 0:
            return at(s, rows)
        return pl.ds(pl.multiple_of(s * rows + ch * cr, cr), cr)

    def to_inner(j, i, b, ch):
        view = (j, b, *spans(j, ch))
        return remote(chip.at[view], ein.at[view], es.at[j, i, ch], er.at[j, i, ch], pt)

    def over(j, ch):
        view = (j, *spans(j, ch))
        return remote(fw.at[view], xin.at[view], xs.at[j, ch], xr.at[j, ch], facing)

    def final(j, b, ch, send, slot, where):
        view = fin[j].at[(b, *spans(j, ch))]
        return remote(view, view, send, fr.at[j, slot, ch], where)

    def z_one(j, slot, cols, which):
        crossed(j, slot, cols).wait_recv()
        for i, b in ((0, th), (1, mi)):
            for ch in which:
                rs, ks_ = spans(j, ch)
                chip[j, b, rs, ks_] = (
                    part[j, b, tokens_of(j, ch), ks_].astype(f32) + sibp[j, b, rs, ks_].astype(f32)
                ).astype(bf16)

                @pl.when(end)
                def _():
                    to_inner(j, i, b, ch).start()

    def z_two(j, which):
        @pl.when(inner)
        def _():
            for ch in which:
                to_inner(j, 0, th, ch).wait_recv()
                rs, ks_ = spans(j, ch)
                fw[j, rs, ks_] = (
                    chip[j, th, rs, ks_].astype(f32) + ein[j, th, rs, ks_].astype(f32)
                ).astype(bf16)
                over(j, ch).start()

    def z_three(j, which):
        @pl.when(inner)
        def _():
            for ch in which:
                to_inner(j, 1, mi, ch).wait_recv()
                over(j, ch).wait_recv()
                rs, ks_ = spans(j, ch)
                total = (
                    chip[j, mi, rs, ks_].astype(f32)
                    + ein[j, mi, rs, ks_].astype(f32)
                    + xin[j, rs, ks_].astype(f32)
                )
                inputs = xf[mi, tokens_of(j, ch), ks_].astype(f32)
                if j == 0:
                    result = inputs + total + rowb[2:3, ks_] + rowb[3:4, ks_]
                else:
                    _, normed, inv_std = layer_norm(inputs, 1.0, 0.0)
                    result = norm_back(total, normed, inv_std, 1.0)
                fin[j][mi, rs, ks_] = result.astype(bf16)
                final(j, mi, ch, fs.at[j, 0, ch], 0, pt).start()
                final(j, mi, ch, fs.at[j, 1, ch], 1, facing).start()

    def z_four(j, which):
        @pl.when(inner)
        def _():
            for ch in which:
                final(j, th, ch, fs.at[j, 1, ch], 1, facing).wait_recv()
                final(j, th, ch, fs2.at[j, ch], 1, pt).start()

    def z_five(j):
        for slot, cols in (((0, early), (2, late)), ((1, every),))[j]:
            crossed(j, slot, cols).wait_send()
        for ch in range(nc):

            @pl.when(end)
            def _():
                for i, b in ((0, th), (1, mi)):
                    to_inner(j, i, b, ch).wait_send()
                final(j, mi, ch, fs.at[j, 0, ch], 0, pt).wait_recv()
                final(j, th, ch, fs2.at[j, ch], 1, pt).wait_recv()

            @pl.when(inner)
            def _():
                over(j, ch).wait_send()
                final(j, mi, ch, fs.at[j, 0, ch], 0, pt).wait_send()
                final(j, mi, ch, fs.at[j, 1, ch], 1, facing).wait_send()
                final(j, th, ch, fs2.at[j, ch], 1, pt).wait_send()


    tiles = width // wide


    def qkv_grad(i):
        rows_of = at(i, big)
        lhs = first[:, rows_of]
        three = dot_tn(lhs, jnp.concatenate([gproj[0], gproj[1], gproj[2]], axis=1))
        for j in range(3):
            gW[0][j, rows_of, :] = three[:, j * fh : (j + 1) * fh].astype(bf16)

    loop(width // big, qkv_grad)

    z_one(0, 0, early, (0, 1, 2))

    def out_grad(i):
        cols = at(i, wide)
        gW[1][:, cols] = dot_tn(ctx[...], cf[:, :, cols].reshape(tokens, wide)).astype(bf16)

    loop(width // wide, out_grad)
    start_reduce(0)
    start_reduce(1)

    def first_back(i):
        b, n = i // tiles, lax.rem(i, tiles)
        span, cols = at(b, length), at(n, wide)
        grad = dot_nt(
            jnp.concatenate([gproj[j, span, :] for j in range(3)], axis=1),
            jnp.concatenate([GQ[j, cols, :] for j in range(3)], axis=1),
        )
        gacc[span, cols] = grad * gains[0:1, cols]
        brow[2:3, cols] = brow[2:3, cols] + jnp.sum(grad * nrm[span, cols], axis=0, keepdims=True)
        brow[4:5, cols] = brow[4:5, cols] + jnp.sum(grad, axis=0, keepdims=True)

    loop(seqs * tiles, first_back)

    def down_grad(i):
        m, n = i // tiles, lax.rem(i, tiles)
        units, cols = at(m, big), at(n, wide)
        gW[3][units, cols] = dot_tn(
            hid[:, units], cf[:, :, cols].reshape(tokens, wide)
        ).astype(bf16)

    loop(hh // big * tiles, down_grad)

    start_reduce(3)
    ones = jnp.ones((16, rows), bf16)
    csum = dot_nn(ones, cf[0, mine, :])
    for b in range(1, seqs):
        csum = csum + dot_nn(ones, cf[b, mine, :])
    brow[6:7, :] = csum[0:1, :]
    wait_hop2(3)

    def late_branch(b):
        branches_of(b, groups[3], 2)

    loop(seqs, late_branch)

    def down_back(b):
        span = at(b, length)
        grad = dot_nt(cf[b], G2[...]) * slope[span, :]
        ghid[span, :] = grad.astype(bf16)
        spot = at(s, hh)
        brow[0:1, spot] = brow[0:1, spot] + jnp.sum(grad, axis=0, keepdims=True)

    loop(seqs, down_back)

    z_one(0, 2, late, (3,))
    z_two(0, (0, 1, 2))

    def second_back(i):
        b, n = i // tiles, lax.rem(i, tiles)
        span, cols = at(b, length), at(n, wide)
        grad = dot_nt(ghid[span, :], G1[cols, :])
        part[1, b, :, cols] = (gacc[span, cols] + grad * gains[1:2, cols]).astype(bf16)
        cross_tile(1, 1, b, cols)
        brow[3:4, cols] = brow[3:4, cols] + jnp.sum(grad * nrm[span, cols], axis=0, keepdims=True)
        brow[5:6, cols] = brow[5:6, cols] + jnp.sum(grad, axis=0, keepdims=True)

    loop(seqs * tiles, second_back)
    bpair_copy = go(remote(brow, bpair, b1s, b1r, {"seq": other}))

    bpair_copy.wait_recv()
    bsum[...] = brow[...] + bpair[...]

    def bias_hop(src, dst, where):
        return remote(
            bsum if src == 0 else bgot3.at[3], bgot3.at[dst], b3s.at[src], b3r.at[dst], where
        )

    @pl.when(end)
    def _():
        bias_hop(0, 0, pt).start()

    z_one(1, 1, every, range(nc))
    z_three(0, (0, 1, 2))
    z_two(0, (3,))

    def up_grad(i):
        rows_of = at(i, big)
        gW[2][rows_of, :] = dot_tn(second[:, rows_of], ghid[...]).astype(bf16)

    loop(width // big, up_grad)
    start_reduce(2)
    second_reduce(0)
    second_reduce(1)

    @pl.when(inner)
    def _():
        bias_hop(0, 0, pt).wait_recv()
        bgot3[3] = bsum[...] + bgot3[0]
        bias_hop(1, 1, facing).start()

    z_two(1, (0,))
    z_four(0, (0,))
    z_two(1, (1,))
    z_three(0, (3,))
    z_four(0, (1,))
    second_reduce(3)
    z_two(1, (2,))
    z_four(0, (2,))
    z_two(1, (3,))

    @pl.when(inner)
    def _():
        bias_hop(1, 1, facing).wait_recv()
        bias_hop(1, 1, facing).wait_send()
        bgot3[3] = bgot3[3] + bgot3[1]
        bias_hop(2, 2, pt).start()
        bsum2[2:6, :] = bgot3[3, 2:6, :]

    @pl.when(end)
    def _():
        bias_hop(2, 2, pt).wait_recv()
        bsum2[2:6, :] = bgot3[2, 2:6, :]

    bsum2[0:2, :] = bsum[0:2, :]
    bsum2[6:8, :] = bsum[6:8, :]
    x_send = go(remote(bsum2, bgot2.at[0], b2s.at[0], b2r.at[0], {"dp": near_x}))
    z_three(1, (0,))
    z_four(0, (3,))
    z_three(1, (1, 2))
    second_reduce(2)
    z_three(1, (3,))
    x_send.wait_recv()
    bgot2[2] = bsum2[...] + bgot2[0]
    y_send = go(remote(bgot2.at[2], bgot2.at[1], b2s.at[1], b2r.at[1], {"dp": near_y}))
    z_four(1, range(nc))
    y_send.wait_recv()
    bout[...] = bgot2[2] + bgot2[1]

    @pl.when(end)
    def _():
        bias_hop(0, 0, pt).wait_send()

    @pl.when(inner)
    def _():
        bias_hop(2, 2, pt).wait_send()

    z_five(0)
    z_five(1)
    for a in (0, 1, 3, 2):
        finish_reduce(a)
    for a in range(4):
        for way in (0, 1):
            for k in (0, 1):
                hop1_copy(a, way, k).wait_send()
            hop2_copy(a, way).wait_send()
    for copy in sends:
        copy.wait_send()


def mega(x, c, seg, pos, wq, wo, w1, w2, qb, f1b, gains, rowb):
    shape = jax.ShapeDtypeStruct
    f32, bf16 = jnp.float32, jnp.bfloat16
    seqs, rows, width = x.shape
    kr, oc, fh, hh = wq.shape[1], wo.shape[1], wq.shape[2] // 2, w1.shape[1] // 2
    length = rows * 2
    tokens = seqs * length
    nc = 4
    pieces = ((3, kr, fh), (fh, oc), (kr, hh), (hh, oc))
    fulls = ((3, width, fh), (fh, width), (width, hh), (hh, width))
    dma = pltpu.SemaphoreType.DMA
    vm = lambda dims, kind: pltpu.VMEM(dims, kind)
    bias = (8, width)
    scratch = [
        vm((seqs, length, width), bf16),
        vm((seqs, length, width), bf16),
        vm((2,) + seg.shape, jnp.int32),
        vm((2,) + pos.shape, jnp.int32),
        *[vm(f, bf16) for f in fulls],
        vm((tokens, width), bf16),
        vm((tokens, width), bf16),
        vm((tokens, width), f32),
        vm((3, tokens, fh), f32),
        *[vm((tokens, fh), bf16)] * 5,
        vm((3, tokens, fh), bf16),
        vm((tokens, width), f32),
        vm((tokens, hh), bf16),
        vm((tokens, hh), f32),
        vm((tokens, hh), bf16),
        *[vm(f, bf16) for f in fulls],
        *[vm((2,) + p, bf16) for p in pieces],
        vm((2, seqs, length, width), bf16),
        *[vm((2, seqs, rows, width), bf16)] * 3,
        *[vm((2, rows, width), bf16)] * 2,
        vm(bias, f32),
        vm(bias, f32),
        vm(bias, f32),
        vm((4,) + bias, f32),
        vm(bias, f32),
        vm((4,) + bias, f32),
        *[dma((4, 2, 2))] * 2,
        *[dma((4, 2))] * 2,
        *[dma((4,))] * 3,
        *[dma((4,))] * 3,
        *[dma((4, 2))] * 6,
        *[dma((4,))] * 3,
        *[dma((3,))] * 2,
        *[dma((2, 2, nc))] * 2,
        *[dma((2, nc))] * 2,
        *[dma((2, 2, nc))] * 2,
        dma((2, nc)),
        dma,
        dma,
        *[dma((4,))] * 4,
        *[vm(v.shape, f32) for v in (qb, f1b, gains, rowb)],
        dma((4,)),
    ]
    return pl.pallas_call(
        functools.partial(mega_kernel, (seqs, rows, width, kr, oc, fh, hh)),
        out_shape=(
            *[shape((2, 3) + p, bf16) for p in pieces],
            shape(x.shape, bf16),
            shape(x.shape, bf16),
            shape(bias, f32),
        ),
        in_specs=[HBM] * 12,
        out_specs=[HBM] * 4 + [VM] * 3,
        scratch_shapes=scratch,
        compiler_params=pltpu.CompilerParams(
            collective_id=0, has_side_effects=True, vmem_limit_bytes=63 * 2**20
        ),
    )(x, c, seg, pos, wq, wo, w1, w2, qb, f1b, gains, rowb)


def final_kernel(dims, *refs):
    f32 = jnp.float32
    fh, hh = dims
    rq, ro, r1, r2, yf, gf, bb, c = range(8)
    hbm_in, hbm_out = refs[:8], refs[8:18]
    vin, vout = refs[18:26], refs[26:36]
    in_sem, out_sem = refs[36:]
    out, gin, oq, oo, o1, o2, oqb, of1, ogn, orow = range(10)
    loads = [pltpu.make_async_copy(hbm_in[i], vin[i], in_sem.at[i]) for i in range(8)]
    straight = pltpu.make_async_copy(vin[yf], hbm_out[out], out_sem.at[out])
    stores = [pltpu.make_async_copy(vout[i], hbm_out[i], out_sem.at[i]) for i in range(10)]
    for i in (yf, r1, r2, c, gf, rq, ro, bb):
        loads[i].start()

    def total(ref, *index):
        return (
            ref[(index[0], 0) + index[1:]].astype(f32)
            + ref[(index[0], 1) + index[1:]].astype(f32)
            + ref[(index[0], 2) + index[1:]].astype(f32)
        )

    loads[yf].wait()
    straight.start()
    loads[r1].wait()
    for h in (0, 1):
        vout[o1][:, h * hh : (h + 1) * hh] = total(vin[r1], h)
    stores[o1].start()
    loads[r2].wait()
    for h in (0, 1):
        vout[o2][h * hh : (h + 1) * hh, :] = total(vin[r2], h)
    stores[o2].start()
    loads[c].wait()
    loads[gf].wait()
    vout[gin][...] = vin[c][...].astype(f32) + vin[gf][...].astype(f32)
    stores[gin].start()
    loads[rq].wait()
    for h in (0, 1):
        for j in range(3):
            vout[oq][j, :, h * fh : (h + 1) * fh] = total(vin[rq], h, j)
    stores[oq].start()
    loads[ro].wait()
    for h in (0, 1):
        vout[oo][h * fh : (h + 1) * fh, :] = total(vin[ro], h)
    stores[oo].start()
    loads[bb].wait()
    rows = vin[bb]
    for j in range(3):
        vout[oqb][j : j + 1, :] = rows[1:2, j * 2 * fh : (j + 1) * 2 * fh]
    vout[of1][...] = rows[0:1, : 2 * hh]
    vout[ogn][...] = rows[2:4, :]
    vout[orow][0:2, :] = rows[4:6, :]
    vout[orow][2:3, :] = rows[6:7, :]
    vout[orow][3:4, :] = rows[6:7, :]
    for i in (oqb, of1, ogn, orow):
        stores[i].start()
    straight.wait()
    for i in range(1, 10):
        stores[i].wait()


def whole_rows(
    block_input,
    cotangent,
    segments,
    positions,
    w_qkv,
    qkv_bias,
    w_out,
    w_fc1,
    fc1_bias,
    w_fc2,
    ln_gains,
    row_biases,
):
    shape = jax.ShapeDtypeStruct
    f32 = jnp.float32
    got = mega(
        block_input,
        cotangent,
        segments,
        positions,
        w_qkv,
        w_out,
        w_fc1,
        w_fc2,
        qkv_bias,
        fc1_bias.reshape(1, -1),
        ln_gains,
        row_biases,
    )
    shapes = (
        shape(block_input.shape, block_input.dtype),
        shape(block_input.shape, f32),
        shape(w_qkv.shape, f32),
        shape(w_out.shape, f32),
        shape(w_fc1.shape, f32),
        shape(w_fc2.shape, f32),
        shape(qkv_bias.shape, f32),
        shape((1, fc1_bias.size), f32),
        shape(ln_gains.shape, f32),
        shape(row_biases.shape, f32),
    )
    operands = (*got, cotangent)
    outs = pl.pallas_call(
        functools.partial(final_kernel, (w_qkv.shape[2] // 2, w_fc1.shape[1] // 2)),
        out_shape=shapes,
        in_specs=[HBM] * len(operands),
        out_specs=[HBM] * len(shapes),
        scratch_shapes=[
            *[pltpu.VMEM(v.shape, v.dtype) for v in operands],
            *[pltpu.VMEM(v.shape, v.dtype) for v in shapes],
            pltpu.SemaphoreType.DMA((len(operands),)),
            pltpu.SemaphoreType.DMA((len(shapes),)),
        ],
        compiler_params=pltpu.CompilerParams(vmem_limit_bytes=63 * 2**20),
    )(*operands)
    return (*outs[:7], outs[7].reshape(fc1_bias.shape), *outs[8:])


def block(mesh, *args):
    seqs, rows, width = args[0].shape
    flat, hidden = args[4].shape[2], args[7].shape[1]
    sizes = mesh.shape
    if (
        (sizes["dp"], sizes["seq"], sizes["tensor"]) == (4, 2, 4)
        and flat == 4 * HD
        and seqs <= 2
        and rows == 128
        and width % 512 == 0
        and max(hidden, 3 * flat) <= width <= 1024
        and hidden % 512 == 0
    ):
        return whole_rows(*args)
    return shards(*args)


def solution(mesh):
    return jax.shard_map(
        functools.partial(block, mesh),
        mesh=mesh,
        in_specs=(
            P("dp", "seq", None),
            P("dp", "seq", None),
            P("dp", "seq"),
            P("dp", "seq"),
            P(None, ("dp", "seq"), "tensor"),
            P(None, "tensor"),
            P("tensor", ("dp", "seq")),
            P(("dp", "seq"), "tensor"),
            P("tensor"),
            P("tensor", ("dp", "seq")),
            P(),
            P(),
        ),
        out_specs=(
            P("dp", "seq", None),
            P("dp", "seq", None),
            P(None, ("dp", "seq"), "tensor"),
            P("tensor", ("dp", "seq")),
            P(("dp", "seq"), "tensor"),
            P("tensor", ("dp", "seq")),
            P(None, "tensor"),
            P("tensor"),
            P(),
            P(),
        ),
        check_vma=False,
    )
```
